256 devices in a mesh: seq: 128 (over z, y, x), chan: 2 (over core).
Axes of the slice: x: 4, y: 4, z: 8, core: 2. Of those that a mesh axis runs over, the one named last changes fastest.
Arguments:
- q_proj: bfloat16 [16384, 8192], P('seq', 'chan'), may hold values from -6 to 6
- k_proj: bfloat16 [16384, 8192], P('seq', 'chan'), may hold values from -6 to 6
- v_proj: bfloat16 [16384, 8192], P('seq', 'chan'), may hold values from -6 to 6
- resid: bfloat16 [16384, 8192], P('seq', 'chan'), may hold values from -6 to 6
- short_filter: float32 [3, 7, 8192], P(None, None, 'chan'), may hold values from -2 to 2
- residue: float32 [8, 8192], P(None, 'chan'), may hold values from -1.5 to 1.5
- rate: float32 [8, 8192], P(None, 'chan'), may hold values from 3.0517578e-05 to 0.0333333333, as said below
- gain: float32 [8192], P('chan'), may hold values from 0.1 to 1.9
- seg_lengths: int32 [16], replicated, may hold values from 1 to 8192, 16384 in all
Outputs:
- stream: bfloat16 [16384, 8192], P('seq', 'chan')
- normed: bfloat16 [16384, 8192], P('seq', 'chan')
The draws below stay inside these ranges and needn't reach their ends.
Inputs may be any that keep to these rules, and one draw needn't show every extreme that they name: `rate`: rates of the long filter's modes per token, between 0.5 / 16384 and 1 / 30. `seg_lengths`: the lengths sum to 16384.
All inputs are finite; a program needn't handle non-finite values.
Results may differ from the reference program's by a relative error of at most 0.0049.
Values may be sent and summed in bfloat16 or wider, within the bound.
A program may use at most 128 MiB of HBM per device.

```python
import math
import jax
import jax.numpy as jnp
import numpy as np
from jax import lax

D = 8192
MODES = 8
KS = 7
L = 16384
NSEG = 16


def draw_rate(key, part):
    low = jnp.log(0.5 / L)
    high = jnp.log(1.0 / 30.0)
    unit = jax.random.uniform(key, (MODES, D), jnp.float32)
    return jnp.exp(low + unit * (high - low)).astype(jnp.float32)


def level_of(key, extent, split, low, high):
    def one(dim, shards_of):
        draws = jax.random.uniform(jax.random.fold_in(jax.random.fold_in(key, 6), dim), (shards_of,), jnp.float32, low / len(split), high / len(split))
        return jnp.repeat(jnp.exp(draws), extent[dim] // shards_of).reshape((-1,) + (1,) * (len(extent) - dim - 1))

    factor_of = one(*split[0])
    for cut in split[1:]:
        factor_of = factor_of * one(*cut)
    return factor_of


def split_up(number_of, total, reach, skew):
    loads = [(1 << 20) // math.isqrt(standing ** skew) + 1 for standing in range(2, number_of + 1)]
    rest, given = total - reach - (number_of - 1), [1] * (number_of - 1)
    while rest > 0:
        free = [i for i in range(number_of - 1) if given[i] < reach]
        mass, budget = sum([loads[i] for i in free]), rest
        for i in free:
            addition = min(reach - given[i], max(1, budget * loads[i] // mass), rest)
            given[i] = given[i] + addition
            rest = rest - addition
    return np.array([reach] + given)


def ragged(own_key, amount, total, reach, skew):
    if amount == 2:
        one = jax.random.randint(own_key, (), max(1, total - reach), min(reach, total - 1) + 1)
        return jnp.stack([one, total - one])
    lengths = jnp.asarray(split_up(amount, total, reach, skew), jnp.int32)
    pairs = (amount - 1) // 2
    donor, receiver = lengths[1:1 + 2 * pairs:2], lengths[2:2 + 2 * pairs:2]
    room = jnp.minimum(donor - 1, reach - receiver)
    shifted = jax.random.randint(jax.random.fold_in(own_key, 1), (pairs,), 0, 1 << 20) % (room + 1)
    lengths = lengths.at[1:1 + 2 * pairs:2].set(donor - shifted).at[2:2 + 2 * pairs:2].set(receiver + shifted)
    return lengths[jax.random.permutation(jax.random.fold_in(own_key, 2), amount)]


def noise(rng, extent, scale, limit, pieces=(), held_as=jnp.bfloat16):
    values = jax.random.normal(rng, extent, jnp.float32) * scale
    if len(pieces) > 0:
        values = level_of(rng, extent, pieces, -0.22, 0.18) * values
    return jnp.clip(values, min=-limit, max=limit).astype(held_as)


def setup_inputs(seed: int = 0) -> dict:
    key_list = jax.random.split(jax.random.key(seed), 10)
    q_proj = noise(key_list[0], (L, D), 1.0, 6.0, ((0, 128), (1, 2)))
    k_proj = noise(key_list[1], (L, D), 1.0, 6.0, ((0, 128), (1, 2)))
    v_proj = noise(key_list[2], (L, D), 1.0, 6.0, ((0, 128), (1, 2)))
    resid = noise(key_list[3], (L, D), 1.0, 6.0, ((0, 128), (1, 2)))
    short_filter = noise(key_list[4], (3, KS, D), KS ** -0.5, 2.0, ((2, 2),), jnp.float32)
    residue = noise(key_list[5], (MODES, D), 0.25, 1.5, ((1, 2),), jnp.float32)
    rate = draw_rate(jax.random.fold_in(key_list[9], 71), 0)
    gain = jnp.clip(1.0 + 0.18 * jax.random.normal(key_list[7], (D,), jnp.float32), 0.1, 1.9)
    seg_lengths = ragged(key_list[8], NSEG, L, L // 2, 2).astype(jnp.int32)
    return dict(q_proj=q_proj, k_proj=k_proj, v_proj=v_proj, resid=resid, short_filter=short_filter, residue=residue, rate=rate, gain=gain, seg_lengths=seg_lengths)


def short_conv(x, taps):
    width = taps.shape[0]
    count = x.shape[0]
    padded = jnp.pad(x.astype(jnp.float32), ((width - 1, 0), (0, 0)))
    out = jnp.zeros(x.shape, jnp.float32)
    for j in range(width):
        out = out + taps[j] * padded[width - 1 - j:width - 1 - j + count]
    return out

def reference(q_proj, k_proj, v_proj, resid, short_filter, residue, rate, gain, seg_lengths):
    total = q_proj.shape[0]
    ends = jnp.cumsum(seg_lengths).astype(jnp.int32)
    starts = (ends - seg_lengths).astype(jnp.int32)
    position = jnp.arange(total, dtype=jnp.int32)
    begins = jnp.any(position[:, None] == starts[None, :], axis=1)
    keeping = 1.0 - begins.astype(jnp.float32)
    q_conv = short_conv(q_proj, short_filter[0])
    k_conv = short_conv(k_proj, short_filter[1])
    v_conv = short_conv(v_proj, short_filter[2])
    z_prod = k_conv * v_conv
    decay = jnp.exp(-rate)
    coef = residue * jnp.sqrt(-jnp.expm1(-2.0 * rate))

    def advance(state, inputs):
        z_row, keep_row = inputs
        state = keep_row * decay * state + z_row[None, :]
        return (state, lax.optimization_barrier(jnp.sum(coef * state, axis=0)))
    init = jnp.zeros(rate.shape, jnp.float32)
    _, conv = lax.scan(advance, init, (z_prod, keeping))
    stream = (resid.astype(jnp.float32) + q_conv * conv).astype(jnp.bfloat16)
    widened = stream.astype(jnp.float32)
    square_mean = lax.optimization_barrier(jnp.mean(widened * widened, axis=1, keepdims=True))
    normed = (widened * lax.rsqrt(square_mean + 1e-06) * gain).astype(jnp.bfloat16)
    return (stream, normed)
```

```python
import functools
import jax
import jax.numpy as jnp
from jax import lax
from jax.experimental import pallas as pl
from jax.experimental.pallas import tpu as pltpu
from jax.sharding import PartitionSpec as P

MESH = pl.DeviceIdType.MESH
PLANE = 16
LANES = 128
SUB = 8
F32 = jnp.float32


def kernel(
    dims,
    q_hbm, k_hbm, v_hbm, r_hbm, sf_hbm, residue_hbm, rate_hbm, gain_hbm, seg_ref,
    stream_ref, normed_ref,
    q_in, k_in, v_in, r_in, sf_in, residue_in, rate_in, gain_in,
    rim_q, rim_k, rim_v,
    xq, xk, xv, zs, conv_std, qs_std,
    taps_t, rate_n, coef_n, dec_n, weights, dec8_n,
    keep_m, last_m, carry_m,
    e_loc, e_buf, pre_buf, total_buf, plane_buf, inc_buf, sq_loc, sq_far,
    in_sem, param_sem, rim_send, rim_recv, s1, r1, s2, r2, s3, r3, sq_send, sq_recv,
):
    shards, planes, tok, chans, modes, taps, segs = dims
    blocks = tok // SUB
    tiles = chans // LANES
    groups = tiles // SUB
    wide = SUB * LANES
    part = tiles * modes // PLANE
    me = lax.axis_index("seq")
    core = lax.axis_index("chan")
    zed = me // PLANE
    spot = lax.rem(me, PLANE)
    after = lax.rem(me + 1, shards)
    before = lax.rem(me + shards - 1, shards)

    def at(ref, start, size):
        return ref.at[pl.ds(pl.multiple_of(start, SUB), size)]

    params = [
        pltpu.make_async_copy(rate_hbm, rate_in, param_sem.at[0]),
        pltpu.make_async_copy(sf_hbm, sf_in, param_sem.at[1]),
        pltpu.make_async_copy(residue_hbm, residue_in, param_sem.at[2]),
        pltpu.make_async_copy(gain_hbm, gain_in, param_sem.at[3]),
    ]

    def load(index, src, dst, g):
        cols = pl.ds(g * wide, wide)
        return pltpu.make_async_copy(src.at[:, cols], dst.at[:, cols], in_sem.at[index, g])

    for copy in params[:2]:
        copy.start()
    for g in range(groups):
        load(1, k_hbm, k_in, g).start()
        load(2, v_hbm, v_in, g).start()
    for copy in params[2:]:
        copy.start()
    for g in range(groups):
        load(0, q_hbm, q_in, g).start()
    for g in range(groups):
        load(3, r_hbm, r_in, g).start()

    barrier = pltpu.get_barrier_semaphore()

    @pl.loop(1, PLANE)
    def _(step):
        other = zed * PLANE + lax.rem(spot + step, PLANE)
        pl.semaphore_signal(barrier, inc=1, device_id=(other, core), device_id_type=MESH)

    @pl.loop(1, planes)
    def _(step):
        other = lax.rem(zed + step, planes) * PLANE + spot
        pl.semaphore_signal(barrier, inc=1, device_id=(other, core), device_id_type=MESH)

    pl.semaphore_signal(barrier, inc=1, device_id=(before, core), device_id_type=MESH)
    pl.semaphore_signal(barrier, inc=1, device_id=(me, 1 - core), device_id_type=MESH)

    first = me * tok
    ends = []
    running = seg_ref[0]
    ends.append(running)
    for j in range(1, segs):
        running = running + seg_ref[j]
        ends.append(running)
    big = jnp.int32(1 << 30)
    low = big
    high = jnp.int32(-1)
    for end in ends:
        low = jnp.minimum(low, jnp.where(end >= first, end, big))
        high = jnp.maximum(high, jnp.where(end <= first + tok - 1, end, -1))
    rows = lax.broadcasted_iota(jnp.int32, (tok, LANES), 0) + first
    begins = rows == 0
    for end in ends:
        begins = begins | (rows == end)
    keep_m[...] = jnp.where(begins, 0.0, 1.0)
    last_m[...] = jnp.where(rows >= high, 1.0, 0.0)
    carry_m[...] = jnp.where(rows < low, 1.0, 0.0)

    params[0].wait()
    for t in range(tiles):
        rate = rate_in[:, t * LANES : (t + 1) * LANES]
        rate_n[t * modes : (t + 1) * modes, :] = rate
        dec_n[t * modes : (t + 1) * modes, :] = jnp.exp(-rate)
    params[1].wait()
    for a in range(3):
        for t in range(tiles):
            taps_t[a, t * SUB : t * SUB + taps, :] = sf_in[a, :, t * LANES : (t + 1) * LANES]

    pl.semaphore_wait(barrier, PLANE - 1 + planes - 1 + 2)

    def rim_copy(index, src, dst):
        return pltpu.make_async_remote_copy(
            src_ref=src.at[pl.ds(tok - SUB, SUB)], dst_ref=dst,
            send_sem=rim_send.at[index], recv_sem=rim_recv.at[index],
            device_id=(after, core), device_id_type=MESH,
        )

    rims = [rim_copy(0, k_hbm, rim_k), rim_copy(1, v_hbm, rim_v), rim_copy(2, q_hbm, rim_q)]
    for copy in rims:
        copy.start()

    def row_of(block, tile):
        return (block * tiles + tile) * SUB

    def relayout(src, dst, g):
        @pl.loop(0, blocks // 2)
        def _(pair):
            for j in range(SUB):
                x = src[pl.ds(pl.multiple_of(pair * 2 * SUB, 2 * SUB), 2 * SUB),
                        pl.ds(pl.multiple_of(g * wide + j * LANES, LANES), LANES)].astype(F32)
                lower = pl.multiple_of(row_of(2 * pair + 1, g * SUB + j), SUB)
                dst[pl.ds(lower, SUB), :] = x[:SUB]
                upper = pl.multiple_of(row_of(2 * pair + 2, g * SUB + j), SUB)
                dst[pl.ds(upper, SUB), :] = x[SUB:]

    def relayout_rim(src, dst):
        for t in range(tiles):
            x = src[:, t * LANES : (t + 1) * LANES].astype(F32)
            dst[t * SUB : (t + 1) * SUB, :] = jnp.where(me > 0, x, 0.0)

    def token(ref, block, g, s):
        return ref[pl.ds(row_of(block, g * SUB) + s, SUB, stride=SUB), :]

    def per_mode(ref, g, m):
        return ref[pl.ds(g * SUB * modes + m, SUB, stride=modes), :]

    def taps_of(a, g):
        return [taps_t[a, pl.ds(g * SUB * SUB + j, SUB, stride=SUB), :] for j in range(taps)]

    def fir(window, weight):
        out = weight[0] * window[-1]
        for j in range(1, taps):
            out = out + weight[j] * window[-1 - j]
        return out

    def z_rows(t, g):
        return pl.ds(pl.multiple_of((t * groups + g) * SUB, SUB), SUB)

    def block_of_z(block, g, k_win, v_win, state, k_taps, v_taps, decay):
        k_win, v_win, state = list(k_win), list(v_win), list(state)
        for s in range(SUB):
            k_win.append(token(xk, block, g, s))
            v_win.append(token(xv, block, g, s))
            z = fir(k_win[-taps:], k_taps) * fir(v_win[-taps:], v_taps)
            t = (block - 1) * SUB + s
            zs[z_rows(t, g), :] = z
            z = z * last_m[pl.ds(t, 1), :]
            state = [d * old + z for d, old in zip(decay, state)]
        return k_win[1 - taps :], v_win[1 - taps :], state

    zero = jnp.zeros((SUB, LANES), F32)

    @pl.loop(0, groups)
    def _(g):
        load(1, k_hbm, k_in, g).wait()
        load(2, v_hbm, v_in, g).wait()
        relayout(k_in, xk, g)
        relayout(v_in, xv, g)
        k_taps, v_taps = taps_of(1, g), taps_of(2, g)
        decay = [per_mode(dec_n, g, m) for m in range(modes)]
        behind = range(SUB - taps + 1, SUB)
        start = (
            [token(xk, 1, g, s) for s in behind],
            [token(xv, 1, g, s) for s in behind],
            [zero] * modes,
        )

        def step(block, carried):
            return block_of_z(block, g, *carried, k_taps, v_taps, decay)

        _, _, state = lax.fori_loop(2, blocks + 1, step, start)
        for m in range(modes):
            e_loc[pl.ds(g * SUB * modes + m, SUB, stride=modes), :] = state[m]

    rims[0].wait_recv()
    rims[1].wait_recv()
    relayout_rim(rim_k, xk)
    relayout_rim(rim_v, xv)

    @pl.loop(0, groups)
    def _(g):
        k_taps, v_taps = taps_of(1, g), taps_of(2, g)
        decay = [per_mode(dec_n, g, m) for m in range(modes)]
        behind = range(SUB - taps + 1, SUB)
        _, _, state = block_of_z(
            1, g, [token(xk, 0, g, s) for s in behind], [token(xv, 0, g, s) for s in behind],
            [zero] * modes, k_taps, v_taps, decay,
        )
        for m in range(modes):
            rest = jnp.exp(per_mode(rate_n, g, m) * float(SUB - tok))
            here = pl.ds(g * SUB * modes + m, SUB, stride=modes)
            e_loc[here, :] = e_loc[here, :] + rest * state[m]

    def round_1(other):
        return pltpu.make_async_remote_copy(
            src_ref=at(e_loc, other * part, part), dst_ref=e_buf.at[spot],
            send_sem=s1.at[other], recv_sem=r1.at[spot],
            device_id=(zed * PLANE + other, core), device_id_type=MESH,
        )

    def arrival_1(other):
        return pltpu.make_async_remote_copy(
            src_ref=at(e_loc, other * part, part), dst_ref=e_buf.at[other],
            send_sem=s1.at[other], recv_sem=r1.at[other],
            device_id=(zed * PLANE + other, core), device_id_type=MESH,
        )

    @pl.loop(1, PLANE)
    def _(step):
        round_1(lax.rem(spot + step, PLANE)).start()

    e_buf[spot] = at(e_loc, spot * part, part)[...]

    params[2].wait()
    params[3].wait()
    for t in range(tiles):
        x = -2.0 * rate_n[t * modes : (t + 1) * modes, :]
        series = 1.0 + x * (1.0 / 6.0)
        for n in (5.0, 4.0, 3.0, 2.0):
            series = 1.0 + x * (1.0 / n) * series
        coef_n[t * modes : (t + 1) * modes, :] = residue_in[:, t * LANES : (t + 1) * LANES] * jnp.sqrt(-x * series)

    @pl.loop(0, groups)
    def _(g):
        load(0, q_hbm, q_in, g).wait()
        relayout(q_in, xq, g)

    rims[2].wait_recv()
    relayout_rim(rim_q, xq)

    @pl.loop(1, PLANE)
    def _(step):
        arrival_1(lax.rem(spot + step, PLANE)).wait_recv()

    my_rate = at(rate_n, spot * part, part)[...]
    span = jnp.exp(my_rate * float(-tok))
    spot_rows = lax.broadcasted_iota(jnp.int32, (PLANE, LANES), 0) + zed * PLANE
    plane_rows = lax.broadcasted_iota(jnp.int32, (SUB, LANES), 0)
    open_here = jnp.ones((PLANE, LANES), F32)
    open_plane = jnp.ones((SUB, LANES), F32)
    for end in ends:
        open_here = jnp.where(spot_rows == end // tok, 0.0, open_here)
        open_plane = jnp.where(plane_rows == end // (tok * PLANE), 0.0, open_plane)

    state = jnp.zeros_like(span)
    reach = jnp.ones_like(span)
    reaches = []
    for other in range(PLANE):
        pre_buf[other] = state
        reaches.append(reach)
        factor = span * open_here[other : other + 1]
        state = factor * state + e_buf[other]
        reach = factor * reach
    total_buf[...] = state

    def round_2(there, slot):
        return pltpu.make_async_remote_copy(
            src_ref=total_buf, dst_ref=plane_buf.at[slot],
            send_sem=s2.at[there], recv_sem=r2.at[slot],
            device_id=(there * PLANE + spot, core), device_id_type=MESH,
        )

    @pl.loop(zed + 1, planes)
    def _(there):
        round_2(there, zed).start()

    def inner(g):
        q_taps = taps_of(0, g)
        decay = [per_mode(dec_n, g, m) for m in range(modes)]
        coef = [per_mode(coef_n, g, m) for m in range(modes)]
        behind = range(SUB - taps + 1, SUB)

        def step(block, carried):
            q_win, state = list(carried[0]), list(carried[1])
            for s in range(SUB):
                q_win.append(token(xq, block, g, s))
                qs = fir(q_win[-taps:], q_taps)
                t = (block - 1) * SUB + s
                z = zs[z_rows(t, g), :]
                keep = keep_m[pl.ds(t, 1), :]
                state = [(d * keep) * old + z for d, old in zip(decay, state)]
                out = coef[0] * state[0]
                for m in range(1, modes):
                    out = out + coef[m] * state[m]
                there = pl.ds(row_of(block - 1, g * SUB) + s, SUB, stride=SUB)
                conv_std[there, :] = out
                qs_std[there, :] = qs
            return q_win[1 - taps :], state

        start = ([token(xq, 0, g, s) for s in behind], [zero] * modes)
        lax.fori_loop(1, blocks + 1, step, start)

    @pl.loop(0, groups // 2)
    def _(g):
        inner(g)

    plane_span = jnp.exp(my_rate * float(-tok * PLANE))

    def plane_step(there, state):
        round_2(there, there).wait_recv()
        row = jnp.sum(jnp.where(plane_rows == there, open_plane, 0.0), axis=0, keepdims=True)
        return plane_span * row * state + plane_buf[there]

    state = lax.fori_loop(0, zed, plane_step, jnp.zeros_like(span))
    for other in range(PLANE):
        pre_buf[other] = pre_buf[other] + reaches[other] * state

    def round_3(other, slot):
        return pltpu.make_async_remote_copy(
            src_ref=pre_buf.at[other], dst_ref=inc_buf.at[slot],
            send_sem=s3.at[other], recv_sem=r3.at[slot],
            device_id=(zed * PLANE + other, core), device_id_type=MESH,
        )

    @pl.loop(1, PLANE)
    def _(step):
        round_3(lax.rem(spot + step, PLANE), spot).start()

    inc_buf[spot] = pre_buf[spot]

    @pl.loop(groups // 2, groups)
    def _(g):
        inner(g)

    rising = (lax.broadcasted_iota(jnp.int32, (SUB, LANES), 0) + 1).astype(F32)

    @pl.loop(0, tiles)
    def _(t):
        for m in range(modes):
            rate = rate_n[pl.ds(t * modes + m, 1), :]
            coef = coef_n[pl.ds(t * modes + m, 1), :]
            here = pl.ds(pl.multiple_of((t * modes + m) * SUB, SUB), SUB)
            weights[here, :] = coef * jnp.exp(-rate * rising)
        whole = pl.ds(pl.multiple_of(t * modes, SUB), modes)
        dec8_n[whole, :] = jnp.exp(rate_n[whole, :] * float(-SUB))

    for g in range(groups):
        load(3, r_hbm, r_in, g).wait()

    @pl.loop(1, PLANE)
    def _(step):
        other = lax.rem(spot + step, PLANE)
        round_3(other, other).wait_recv()

    per = tiles // PLANE

    def tile_of(t, squares):
        value, decay = [], []
        for m in range(modes):
            here = pl.ds(pl.multiple_of((t * modes + m) * SUB, SUB), SUB)
            slot = t // per
            row = (t - slot * per) * modes + m
            value.append(weights[here, :] * inc_buf[slot, pl.ds(row, 1), :])
            decay.append(jnp.broadcast_to(dec8_n[pl.ds(t * modes + m, 1), :], (SUB, LANES)))
        cols = pl.ds(pl.multiple_of(t * LANES, LANES), LANES)
        squares = list(squares)
        for pair in range(blocks // 2):
            halves = []
            for block in (2 * pair, 2 * pair + 1):
                carried = value[0]
                for m in range(1, modes):
                    carried = carried + value[m]
                value = [v * d for v, d in zip(value, decay)]
                here = pl.ds(pl.multiple_of(row_of(block, t), SUB), SUB)
                mask = carry_m[block * SUB : (block + 1) * SUB, :]
                halves.append(qs_std[here, :] * (conv_std[here, :] + carried * mask))
            both = pl.ds(pair * 2 * SUB, 2 * SUB)
            stream = (r_in[both, cols].astype(F32) + jnp.concatenate(halves, axis=0)).astype(jnp.bfloat16)
            stream_ref[both, cols] = stream
            back = stream.astype(F32)
            square = back * back
            squares[2 * pair] = squares[2 * pair] + square[:SUB]
            squares[2 * pair + 1] = squares[2 * pair + 1] + square[SUB:]
        return squares

    squares = lax.fori_loop(0, tiles, tile_of, [zero] * blocks)
    for block in range(blocks):
        sq_loc[block * SUB : (block + 1) * SUB, :] = squares[block]

    swap = pltpu.make_async_remote_copy(
        src_ref=sq_loc, dst_ref=sq_far, send_sem=sq_send, recv_sem=sq_recv,
        device_id=(me, 1 - core), device_id_type=MESH,
    )
    swap.start()

    for copy in rims:
        copy.wait_send()

    @pl.loop(1, PLANE)
    def _(step):
        other = lax.rem(spot + step, PLANE)
        round_1(other).wait_send()
        round_3(other, spot).wait_send()

    @pl.loop(zed + 1, planes)
    def _(there):
        round_2(there, zed).wait_send()

    swap.wait()
    total = jnp.sum(sq_loc[...] + sq_far[...], axis=1, keepdims=True)
    scale = lax.rsqrt(total * (1.0 / (2 * chans)) + 1e-6)
    sq_loc[...] = jnp.broadcast_to(scale, (tok, LANES))

    @pl.loop(0, tiles)
    def _(t):
        cols = pl.ds(pl.multiple_of(t * LANES, LANES), LANES)
        gain = gain_in[pl.ds(t, 1), :]
        for pair in range(blocks // 2):
            both = pl.ds(pair * 2 * SUB, 2 * SUB)
            x = stream_ref[both, cols].astype(F32)
            normed_ref[both, cols] = (x * sq_loc[both, :] * gain).astype(jnp.bfloat16)


def body(q_proj, k_proj, v_proj, resid, short_filter, residue, rate, gain, seg_lengths):
    tok, chans = q_proj.shape
    taps = short_filter.shape[1]
    modes = rate.shape[0]
    segs = seg_lengths.shape[0]
    shards = lax.axis_size("seq")
    planes = shards // PLANE
    tiles = chans // LANES
    groups = tiles // SUB
    blocks = tok // SUB
    part = tiles * modes // PLANE
    bf16 = jnp.bfloat16
    dims = (shards, planes, tok, chans, modes, taps, segs)
    vmem = pltpu.VMEM
    sem = pltpu.SemaphoreType.DMA
    any_spec = pl.BlockSpec(memory_space=pl.ANY)
    return pl.pallas_call(
        functools.partial(kernel, dims),
        out_shape=(jax.ShapeDtypeStruct((tok, chans), bf16),) * 2,
        in_specs=[any_spec] * 8 + [pl.BlockSpec(memory_space=pltpu.SMEM)],
        out_specs=(pl.BlockSpec(memory_space=vmem),) * 2,
        scratch_shapes=[
            vmem((tok, chans), bf16), vmem((tok, chans), bf16), vmem((tok, chans), bf16), vmem((tok, chans), bf16),
            vmem((3, taps, chans), F32), vmem((modes, chans), F32), vmem((modes, chans), F32), vmem((tiles, LANES), F32),
            vmem((SUB, chans), bf16), vmem((SUB, chans), bf16), vmem((SUB, chans), bf16),
            vmem(((blocks + 1) * tiles * SUB, LANES), F32),
            vmem(((blocks + 1) * tiles * SUB, LANES), F32),
            vmem(((blocks + 1) * tiles * SUB, LANES), F32),
            vmem((blocks * tiles * SUB, LANES), F32),
            vmem((blocks * tiles * SUB, LANES), F32),
            vmem((blocks * tiles * SUB, LANES), F32),
            vmem((3, tiles * SUB, LANES), F32),
            vmem((tiles * modes, LANES), F32), vmem((tiles * modes, LANES), F32), vmem((tiles * modes, LANES), F32),
            vmem((tiles * modes * SUB, LANES), F32), vmem((tiles * modes, LANES), F32),
            vmem((tok, LANES), F32), vmem((tok, LANES), F32), vmem((tok, LANES), F32),
            vmem((tiles * modes, LANES), F32),
            vmem((PLANE, part, LANES), F32), vmem((PLANE, part, LANES), F32),
            vmem((part, LANES), F32), vmem((planes, part, LANES), F32), vmem((PLANE, part, LANES), F32),
            vmem((tok, LANES), F32), vmem((tok, LANES), F32),
            sem((4, groups)), sem((4,)), sem((3,)), sem((3,)),
            sem((PLANE,)), sem((PLANE,)), sem((planes,)), sem((planes,)), sem((PLANE,)), sem((PLANE,)),
            sem, sem,
        ],
        compiler_params=pltpu.CompilerParams(
            collective_id=0, has_side_effects=True, vmem_limit_bytes=48 * 1024 * 1024
        ),
        name="hyena",
    )(q_proj, k_proj, v_proj, resid, short_filter, residue, rate, gain.reshape(tiles, LANES), seg_lengths)


def solution(mesh):
    placed = (
        P("seq", "chan"),
        P("seq", "chan"),
        P("seq", "chan"),
        P("seq", "chan"),
        P(None, None, "chan"),
        P(None, "chan"),
        P(None, "chan"),
        P("chan"),
        P(),
    )
    return jax.shard_map(
        body,
        mesh=mesh,
        in_specs=placed,
        out_specs=(P("seq", "chan"), P("seq", "chan")),
        check_vma=False,
    )
```

```python
import functools
import jax
import jax.numpy as jnp
from jax import lax
from jax.experimental import pallas as pl
from jax.experimental.pallas import tpu as pltpu
from jax.sharding import PartitionSpec as P

MESH = pl.DeviceIdType.MESH
PLANE = 16
LANES = 128
SUB = 8
F32 = jnp.float32


def kernel(
    dims,
    q_hbm, k_hbm, v_hbm, r_hbm, sf_hbm, residue_hbm, rate_hbm, gain_hbm, seg_hbm,
    stream_ref, scale_ref, gain_in,
    q_in, k_in, v_in, r_in, sf_in, residue_in, rate_in, seg_ref,
    rim_q, rim_k, rim_v,
    xq, xk, xv, zs, conv_std, qs_std,
    taps_t, rate_n, coef_n, dec_n, weights, dec8_n,
    keep_m, last_m, carry_m,
    e_loc, e_buf, pre_buf, reach_buf, total_buf, plane_buf, inc_buf, sq_loc, sq_far,
    in_sem, param_sem, rim_send, rim_recv, s1, r1, s2, r2, s3, r3, sq_send, sq_recv,
):
    shards, planes, tok, chans, modes, taps, segs = dims
    blocks = tok // SUB
    pairs = blocks // 2
    tiles = chans // LANES
    groups = tiles // SUB
    wide = SUB * LANES
    part = tiles * modes // PLANE
    me = lax.axis_index("seq")
    core = lax.axis_index("chan")
    zed = me // PLANE
    spot = lax.rem(me, PLANE)
    after = lax.rem(me + 1, shards)
    before = lax.rem(me + shards - 1, shards)

    def at(ref, start, size):
        return ref.at[pl.ds(pl.multiple_of(start, SUB), size)]

    params = [
        pltpu.make_async_copy(rate_hbm, rate_in, param_sem.at[0]),
        pltpu.make_async_copy(sf_hbm, sf_in, param_sem.at[1]),
        pltpu.make_async_copy(residue_hbm, residue_in, param_sem.at[2]),
        pltpu.make_async_copy(gain_hbm, gain_in, param_sem.at[3]),
        pltpu.make_async_copy(seg_hbm, seg_ref, param_sem.at[4]),
    ]

    def load(index, src, dst, g):
        cols = pl.ds(g * wide, wide)
        return pltpu.make_async_copy(src.at[:, cols], dst.at[:, cols], in_sem.at[index, g])

    for index in (4, 0, 1):
        params[index].start()
    for g in range(groups):
        load(1, k_hbm, k_in, g).start()
        load(2, v_hbm, v_in, g).start()
    for index in (2, 3):
        params[index].start()
    for g in range(groups):
        load(0, q_hbm, q_in, g).start()
    for g in range(groups):
        load(3, r_hbm, r_in, g).start()

    barrier = pltpu.get_barrier_semaphore()

    @pl.loop(1, PLANE)
    def _(step):
        other = zed * PLANE + lax.rem(spot + step, PLANE)
        pl.semaphore_signal(barrier, inc=1, device_id=(other, core), device_id_type=MESH)

    @pl.loop(1, planes)
    def _(step):
        other = lax.rem(zed + step, planes) * PLANE + spot
        pl.semaphore_signal(barrier, inc=1, device_id=(other, core), device_id_type=MESH)

    pl.semaphore_signal(barrier, inc=1, device_id=(before, core), device_id_type=MESH)
    pl.semaphore_signal(barrier, inc=1, device_id=(me, 1 - core), device_id_type=MESH)

    params[4].wait()
    first = me * tok
    ends = []
    running = seg_ref[0]
    ends.append(running)
    for j in range(1, segs):
        running = running + seg_ref[j]
        ends.append(running)
    big = jnp.int32(1 << 30)
    low = big
    high = jnp.int32(-1)
    for end in ends:
        low = jnp.minimum(low, jnp.where(end >= first, end, big))
        high = jnp.maximum(high, jnp.where(end <= first + tok - 1, end, -1))
    rows = lax.broadcasted_iota(jnp.int32, (tok, LANES), 0) + first
    last_m[...] = jnp.where(rows >= high, 1.0, 0.0)
    carry_m[...] = jnp.where(rows < low, 1.0, 0.0)

    params[0].wait()
    for t in range(tiles):
        rate = rate_in[:, t * LANES : (t + 1) * LANES]
        rate_n[t * modes : (t + 1) * modes, :] = rate
        dec_n[t * modes : (t + 1) * modes, :] = jnp.exp(-rate)
    params[1].wait()
    for a in (1, 2):
        for t in range(tiles):
            taps_t[a, t * SUB : t * SUB + taps, :] = sf_in[a, :, t * LANES : (t + 1) * LANES]

    pl.semaphore_wait(barrier, PLANE - 1 + planes - 1 + 2)

    def rim_copy(index, src, dst):
        return pltpu.make_async_remote_copy(
            src_ref=src.at[pl.ds(tok - SUB, SUB)], dst_ref=dst,
            send_sem=rim_send.at[index], recv_sem=rim_recv.at[index],
            device_id=(after, core), device_id_type=MESH,
        )

    rims = [rim_copy(0, k_hbm, rim_k), rim_copy(1, v_hbm, rim_v), rim_copy(2, q_hbm, rim_q)]
    for copy in rims:
        copy.start()

    def row_of(block, tile):
        return (block * tiles + tile) * SUB

    def relayout_tile(src, dst, g, pair, j):
        x = src[pl.ds(pl.multiple_of(pair * 2 * SUB, 2 * SUB), 2 * SUB),
                pl.ds(pl.multiple_of(g * wide + j * LANES, LANES), LANES)].astype(F32)
        lower = pl.multiple_of(row_of(2 * pair + 1, g * SUB + j), SUB)
        dst[pl.ds(lower, SUB), :] = x[:SUB]
        upper = pl.multiple_of(row_of(2 * pair + 2, g * SUB + j), SUB)
        dst[pl.ds(upper, SUB), :] = x[SUB:]

    def relayout(src, dst, g):
        @pl.loop(0, pairs)
        def _(pair):
            for j in range(SUB):
                relayout_tile(src, dst, g, pair, j)

    def relayout_rim(src, dst):
        for t in range(tiles):
            x = src[:, t * LANES : (t + 1) * LANES].astype(F32)
            dst[t * SUB : (t + 1) * SUB, :] = jnp.where(me > 0, x, 0.0)

    def token(ref, block, g, s):
        return ref[pl.ds(row_of(block, g * SUB) + s, SUB, stride=SUB), :]

    def per_mode(ref, g, m):
        return ref[pl.ds(g * SUB * modes + m, SUB, stride=modes), :]

    def taps_of(a, g):
        return [taps_t[a, pl.ds(g * SUB * SUB + j, SUB, stride=SUB), :] for j in range(taps)]

    def fir(window, weight):
        out = weight[0] * window[-1]
        for j in range(1, taps):
            out = out + weight[j] * window[-1 - j]
        return out

    def z_rows(t, g):
        return pl.ds(pl.multiple_of((t * groups + g) * SUB, SUB), SUB)

    def block_of_z(block, g, k_win, v_win, state, k_taps, v_taps, decay, beside=None):
        k_win, v_win, state = list(k_win), list(v_win), list(state)
        for s in range(SUB):
            if beside is not None:
                beside(s)
            k_win.append(token(xk, block, g, s))
            v_win.append(token(xv, block, g, s))
            z = fir(k_win[-taps:], k_taps) * fir(v_win[-taps:], v_taps)
            t = (block - 1) * SUB + s
            zs[z_rows(t, g), :] = z
            z = z * last_m[pl.ds(t, 1), :]
            state = [d * old + z for d, old in zip(decay, state)]
        return k_win[1 - taps :], v_win[1 - taps :], state

    zero = jnp.zeros((SUB, LANES), F32)

    load(1, k_hbm, k_in, 0).wait()
    load(2, v_hbm, v_in, 0).wait()
    for j in range(SUB):
        relayout_tile(k_in, xk, 0, 0, j)
        relayout_tile(v_in, xv, 0, 0, j)

    for g in range(groups - 1):
        load(1, k_hbm, k_in, g + 1).wait()
        load(2, v_hbm, v_in, g + 1).wait()

    @pl.loop(0, groups)
    def _(g):
        k_taps, v_taps = taps_of(1, g), taps_of(2, g)
        decay = [per_mode(dec_n, g, m) for m in range(modes)]
        behind = range(SUB - taps + 1, SUB)

        def ahead(pair, half):
            after_it = jnp.minimum(g * pairs + pair + 1, groups * pairs - 1)
            g_next, pair_next = after_it // pairs, lax.rem(after_it, pairs)

            def one(s):
                src, dst = ((k_in, xk), (v_in, xv))[s % 2]
                if half is None:
                    relayout_tile(k_in, xk, g_next, pair_next, s)
                    relayout_tile(v_in, xv, g_next, pair_next, s)
                else:
                    relayout_tile(src, dst, g_next, pair_next, half * SUB // 2 + s // 2)

            return one

        start = block_of_z(
            2, g, [token(xk, 1, g, s) for s in behind], [token(xv, 1, g, s) for s in behind],
            [zero] * modes, k_taps, v_taps, decay, ahead(0, None),
        )

        def step(pair, carried):
            for half in range(2):
                carried = block_of_z(
                    2 * pair + 1 + half, g, *carried, k_taps, v_taps, decay, ahead(pair, half)
                )
            return carried

        _, _, state = lax.fori_loop(1, pairs, step, start)
        for m in range(modes):
            e_loc[pl.ds(g * SUB * modes + m, SUB, stride=modes), :] = state[m]

    rims[0].wait_recv()
    rims[1].wait_recv()
    relayout_rim(rim_k, xk)
    relayout_rim(rim_v, xv)

    @pl.loop(0, groups)
    def _(g):
        k_taps, v_taps = taps_of(1, g), taps_of(2, g)
        decay = [per_mode(dec_n, g, m) for m in range(modes)]
        behind = range(SUB - taps + 1, SUB)
        _, _, state = block_of_z(
            1, g, [token(xk, 0, g, s) for s in behind], [token(xv, 0, g, s) for s in behind],
            [zero] * modes, k_taps, v_taps, decay,
        )
        for m in range(modes):
            rest = jnp.exp(per_mode(rate_n, g, m) * float(SUB - tok))
            here = pl.ds(g * SUB * modes + m, SUB, stride=modes)
            e_loc[here, :] = e_loc[here, :] + rest * state[m]

    def round_1(other):
        return pltpu.make_async_remote_copy(
            src_ref=at(e_loc, other * part, part), dst_ref=e_buf.at[spot],
            send_sem=s1.at[other], recv_sem=r1.at[spot],
            device_id=(zed * PLANE + other, core), device_id_type=MESH,
        )

    def arrival_1(other):
        return pltpu.make_async_remote_copy(
            src_ref=at(e_loc, other * part, part), dst_ref=e_buf.at[other],
            send_sem=s1.at[other], recv_sem=r1.at[other],
            device_id=(zed * PLANE + other, core), device_id_type=MESH,
        )

    side = 4

    def nth(i, j):
        near = lambda n: (n * (n + 1) // 2) % side
        y = lax.rem(spot // side + near(i), side)
        x = lax.rem(spot + near(j), side)
        return y * side + x

    def nth_of(n):
        return nth(n // side, lax.rem(n, side))

    @pl.loop(1, PLANE)
    def _(step):
        round_1(nth_of(PLANE - step)).start()

    e_buf[spot] = at(e_loc, spot * part, part)[...]

    begins = rows == 0
    for end in ends:
        begins = begins | (rows == end)
    keep_m[...] = jnp.where(begins, 0.0, 1.0)
    for t in range(tiles):
        taps_t[0, t * SUB : t * SUB + taps, :] = sf_in[0, :, t * LANES : (t + 1) * LANES]
    params[2].wait()
    params[3].wait()
    for t in range(tiles):
        x = -2.0 * rate_n[t * modes : (t + 1) * modes, :]
        series = 1.0 + x * (1.0 / 6.0)
        for n in (5.0, 4.0, 3.0, 2.0):
            series = 1.0 + x * (1.0 / n) * series
        coef_n[t * modes : (t + 1) * modes, :] = residue_in[:, t * LANES : (t + 1) * LANES] * jnp.sqrt(-x * series)

    @pl.loop(0, groups)
    def _(g):
        load(0, q_hbm, q_in, g).wait()
        relayout(q_in, xq, g)

    rims[2].wait_recv()
    relayout_rim(rim_q, xq)

    @pl.loop(1, PLANE)
    def _(step):
        arrival_1(lax.rem(spot + step, PLANE)).wait_recv()

    my_rate = at(rate_n, spot * part, part)[...]
    span = jnp.exp(my_rate * float(-tok))
    spot_rows = lax.broadcasted_iota(jnp.int32, (PLANE, LANES), 0) + zed * PLANE
    plane_rows = lax.broadcasted_iota(jnp.int32, (SUB, LANES), 0)
    open_here = jnp.ones((PLANE, LANES), F32)
    open_plane = jnp.ones((SUB, LANES), F32)
    for end in ends:
        open_here = jnp.where(spot_rows == end // tok, 0.0, open_here)
        open_plane = jnp.where(plane_rows == end // (tok * PLANE), 0.0, open_plane)

    state = jnp.zeros_like(span)
    reach = jnp.ones_like(span)
    for other in range(PLANE):
        pre_buf[other] = state
        reach_buf[other] = reach
        factor = span * open_here[other : other + 1]
        state = factor * state + e_buf[other]
        reach = factor * reach
    total_buf[...] = state

    def round_2(there, slot):
        return pltpu.make_async_remote_copy(
            src_ref=total_buf, dst_ref=plane_buf.at[slot],
            send_sem=s2.at[there], recv_sem=r2.at[slot],
            device_id=(there * PLANE + spot, core), device_id_type=MESH,
        )

    @pl.loop(zed + 1, planes)
    def _(there):
        round_2(there, zed).start()

    def inner(g):
        q_taps = taps_of(0, g)
        decay = [per_mode(dec_n, g, m) for m in range(modes)]
        coef = [per_mode(coef_n, g, m) for m in range(modes)]
        behind = range(SUB - taps + 1, SUB)

        def step(block, carried):
            q_win, state = list(carried[0]), list(carried[1])
            for s in range(SUB):
                q_win.append(token(xq, block, g, s))
                qs = fir(q_win[-taps:], q_taps)
                t = (block - 1) * SUB + s
                z = zs[z_rows(t, g), :]
                keep = keep_m[pl.ds(t, 1), :]
                state = [(d * keep) * old + z for d, old in zip(decay, state)]
                out = coef[0] * state[0]
                for m in range(1, modes):
                    out = out + coef[m] * state[m]
                there = pl.ds(row_of(block - 1, g * SUB) + s, SUB, stride=SUB)
                conv_std[there, :] = out * qs
                qs_std[there, :] = qs * carry_m[pl.ds(t, 1), :]
            return q_win[1 - taps :], state

        start = ([token(xq, 0, g, s) for s in behind], [zero] * modes)
        lax.fori_loop(1, blocks + 1, step, start)

    @pl.loop(0, groups // 2)
    def _(g):
        inner(g)

    plane_span = jnp.exp(my_rate * float(-tok * PLANE))

    def plane_step(there, state):
        round_2(there, there).wait_recv()
        row = jnp.sum(jnp.where(plane_rows == there, open_plane, 0.0), axis=0, keepdims=True)
        return plane_span * row * state + plane_buf[there]

    state = lax.fori_loop(0, zed, plane_step, jnp.zeros_like(span))
    def round_3(other, slot):
        return pltpu.make_async_remote_copy(
            src_ref=pre_buf.at[other], dst_ref=inc_buf.at[slot],
            send_sem=s3.at[other], recv_sem=r3.at[slot],
            device_id=(zed * PLANE + other, core), device_id_type=MESH,
        )

    @pl.loop(1, PLANE)
    def _(step):
        other = nth_of(PLANE - step)
        pre_buf[other] = pre_buf[other] + reach_buf[other] * state
        round_3(other, spot).start()

    inc_buf[spot] = pre_buf[spot] + reach_buf[spot] * state

    @pl.loop(groups // 2, groups)
    def _(g):
        inner(g)

    rising = (lax.broadcasted_iota(jnp.int32, (SUB, LANES), 0) + 1).astype(F32)

    @pl.loop(0, tiles)
    def _(t):
        for m in range(modes):
            rate = rate_n[pl.ds(t * modes + m, 1), :]
            coef = coef_n[pl.ds(t * modes + m, 1), :]
            here = pl.ds(pl.multiple_of((t * modes + m) * SUB, SUB), SUB)
            weights[here, :] = coef * jnp.exp(-rate * rising)
        whole = pl.ds(pl.multiple_of(t * modes, SUB), modes)
        dec8_n[whole, :] = jnp.exp(rate_n[whole, :] * float(-SUB))

    for g in range(groups):
        load(3, r_hbm, r_in, g).wait()

    @pl.loop(0, tiles)
    def _(t):
        cols = pl.ds(pl.multiple_of(t * LANES, LANES), LANES)
        for pair in range(pairs):
            x = r_in[pair * 2 * SUB : (pair + 1) * 2 * SUB, cols].astype(F32)
            for half in range(2):
                here = pl.ds(pl.multiple_of(row_of(2 * pair + half, t), SUB), SUB)
                conv_std[here, :] = conv_std[here, :] + x[half * SUB : (half + 1) * SUB]

    sq_loc[...] = jnp.zeros_like(sq_loc)

    per = tiles // PLANE

    def tree(terms):
        while len(terms) > 1:
            terms = [a + b for a, b in zip(terms[::2], terms[1::2])]
        return terms[0]

    def tile_of(slot, local):
        t = slot * per + local
        value, decay = [], []
        for m in range(modes):
            here = pl.ds(pl.multiple_of((t * modes + m) * SUB, SUB), SUB)
            value.append(weights[here, :] * inc_buf[slot, pl.ds(local * modes + m, 1), :])
            decay.append(jnp.broadcast_to(dec8_n[pl.ds(t * modes + m, 1), :], (SUB, LANES)))
        cols = pl.ds(pl.multiple_of(t * LANES, LANES), LANES)
        for pair in range(pairs):
            halves = []
            for block in (2 * pair, 2 * pair + 1):
                carried = tree(value)
                if block < blocks - 1:
                    value = [v * d for v, d in zip(value, decay)]
                here = pl.ds(pl.multiple_of(row_of(block, t), SUB), SUB)
                halves.append(conv_std[here, :] + qs_std[here, :] * carried)
            both = pl.ds(pair * 2 * SUB, 2 * SUB)
            stream = jnp.concatenate(halves, axis=0).astype(jnp.bfloat16)
            stream_ref[both, cols] = stream
            back = stream.astype(F32)
            sq_loc[both, :] = sq_loc[both, :] + back * back

    @pl.loop(0, PLANE)
    def _(n):
        slot = nth_of(n)

        @pl.when(n > 0)
        def _():
            round_3(slot, slot).wait_recv()

        for local in range(per):
            tile_of(slot, local)

    swap = pltpu.make_async_remote_copy(
        src_ref=sq_loc, dst_ref=sq_far, send_sem=sq_send, recv_sem=sq_recv,
        device_id=(me, 1 - core), device_id_type=MESH,
    )
    swap.start()

    for copy in rims:
        copy.wait_send()

    @pl.loop(1, PLANE)
    def _(step):
        other = lax.rem(spot + step, PLANE)
        round_1(other).wait_send()
        round_3(other, spot).wait_send()

    @pl.loop(zed + 1, planes)
    def _(there):
        round_2(there, zed).wait_send()

    swap.wait()
    total = jnp.sum(sq_loc[...] + sq_far[...], axis=1, keepdims=True)
    scale = lax.rsqrt(total * (1.0 / (2 * chans)) + 1e-6)
    scale_ref[...] = jnp.broadcast_to(scale, (tok, LANES))


def finish(tok, chans, stream_ref, scale_ref, gain_ref, stream_hbm, normed_hbm, normed, sem):
    wide = SUB * LANES
    groups = chans // wide
    copies = [pltpu.make_async_copy(stream_ref, stream_hbm, sem.at[groups])]
    copies[0].start()
    for g in range(groups):
        for t in range(g * SUB, (g + 1) * SUB):
            cols = slice(t * LANES, (t + 1) * LANES)
            gain = gain_ref[t : t + 1, :]

            @pl.loop(0, tok // (2 * SUB))
            def _(pair):
                both = pl.ds(pl.multiple_of(pair * 2 * SUB, 2 * SUB), 2 * SUB)
                x = stream_ref[both, cols].astype(F32)
                normed[both, cols] = (x * scale_ref[both, :] * gain).astype(jnp.bfloat16)

        part = slice(g * wide, (g + 1) * wide)
        copy = pltpu.make_async_copy(normed.at[:, part], normed_hbm.at[:, part], sem.at[g])
        copy.start()
        copies.append(copy)
    for copy in copies:
        copy.wait()


def body(q_proj, k_proj, v_proj, resid, short_filter, residue, rate, gain, seg_lengths):
    tok, chans = q_proj.shape
    taps = short_filter.shape[1]
    modes = rate.shape[0]
    segs = seg_lengths.shape[0]
    shards = lax.axis_size("seq")
    planes = shards // PLANE
    tiles = chans // LANES
    groups = tiles // SUB
    blocks = tok // SUB
    part = tiles * modes // PLANE
    bf16 = jnp.bfloat16
    dims = (shards, planes, tok, chans, modes, taps, segs)
    vmem = pltpu.VMEM
    sem = pltpu.SemaphoreType.DMA
    hbm_spec = pl.BlockSpec(memory_space=pltpu.HBM)
    stream, scale, gain = pl.pallas_call(
        functools.partial(kernel, dims),
        out_shape=(
            jax.ShapeDtypeStruct((tok, chans), bf16),
            jax.ShapeDtypeStruct((tok, LANES), F32),
            jax.ShapeDtypeStruct((tiles, LANES), F32),
        ),
        in_specs=[hbm_spec] * 9,
        out_specs=(pl.BlockSpec(memory_space=vmem),) * 3,
        scratch_shapes=[
            vmem((tok, chans), bf16), vmem((tok, chans), bf16), vmem((tok, chans), bf16), vmem((tok, chans), bf16),
            vmem((3, taps, chans), F32), vmem((modes, chans), F32), vmem((modes, chans), F32),
            pltpu.SMEM((segs,), jnp.int32),
            vmem((SUB, chans), bf16), vmem((SUB, chans), bf16), vmem((SUB, chans), bf16),
            vmem(((blocks + 1) * tiles * SUB, LANES), F32),
            vmem(((blocks + 1) * tiles * SUB, LANES), F32),
            vmem(((blocks + 1) * tiles * SUB, LANES), F32),
            vmem((blocks * tiles * SUB, LANES), F32),
            vmem((blocks * tiles * SUB, LANES), F32),
            vmem((blocks * tiles * SUB, LANES), F32),
            vmem((3, tiles * SUB, LANES), F32),
            vmem((tiles * modes, LANES), F32), vmem((tiles * modes, LANES), F32), vmem((tiles * modes, LANES), F32),
            vmem((tiles * modes * SUB, LANES), F32), vmem((tiles * modes, LANES), F32),
            vmem((tok, LANES), F32), vmem((tok, LANES), F32), vmem((tok, LANES), F32),
            vmem((tiles * modes, LANES), F32),
            vmem((PLANE, part, LANES), F32), vmem((PLANE, part, LANES), F32), vmem((PLANE, part, LANES), F32),
            vmem((part, LANES), F32), vmem((planes, part, LANES), F32), vmem((PLANE, part, LANES), F32),
            vmem((tok, LANES), F32), vmem((tok, LANES), F32),
            sem((4, groups)), sem((5,)), sem((3,)), sem((3,)),
            sem((PLANE,)), sem((PLANE,)), sem((planes,)), sem((planes,)), sem((PLANE,)), sem((PLANE,)),
            sem, sem,
        ],
        compiler_params=pltpu.CompilerParams(
            collective_id=0, has_side_effects=True, vmem_limit_bytes=40 * 1024 * 1024
        ),
        name="hyena",
    )(*(pltpu.with_memory_space_constraint(x, pltpu.HBM) for x in (
        q_proj, k_proj, v_proj, resid, short_filter, residue, rate, gain.reshape(tiles, LANES), seg_lengths
    )))
    return pl.pallas_call(
        functools.partial(finish, tok, chans),
        out_shape=(jax.ShapeDtypeStruct((tok, chans), bf16),) * 2,
        in_specs=[pl.BlockSpec(memory_space=vmem)] * 3,
        out_specs=(hbm_spec,) * 2,
        scratch_shapes=[vmem((tok, chans), bf16), sem((chans // (SUB * LANES) + 1,))],
        compiler_params=pltpu.CompilerParams(vmem_limit_bytes=16 * 1024 * 1024),
        name="finish",
    )(stream, scale, gain)


def solution(mesh):
    placed = (
        P("seq", "chan"),
        P("seq", "chan"),
        P("seq", "chan"),
        P("seq", "chan"),
        P(None, None, "chan"),
        P(None, "chan"),
        P(None, "chan"),
        P("chan"),
        P(),
    )
    return jax.shard_map(
        body,
        mesh=mesh,
        in_specs=placed,
        out_specs=(P("seq", "chan"), P("seq", "chan")),
        check_vma=False,
    )
```

```python
import functools
import jax
import jax.numpy as jnp
from jax import lax
from jax.experimental import pallas as pl
from jax.experimental.pallas import tpu as pltpu
from jax.sharding import PartitionSpec as P

MESH = pl.DeviceIdType.MESH
PLANE = 16
LANES = 128
SUB = 8
F32 = jnp.float32


def kernel(
    dims,
    q_hbm, k_hbm, v_hbm, r_hbm, sf_hbm, residue_hbm, rate_hbm, gain_hbm, seg_hbm,
    stream_ref, scale_ref, gain_in,
    q_in, k_in, v_in, r_in, sf_in, residue_in, rate_in, seg_ref,
    rim_q, rim_k, rim_v, edge, edges, ek, ev, e_first, dec_own, taps_own,
    xq, xk, xv, zs, conv_std, qs_std,
    taps_t, rate_n, coef_n, dec_n, weights, dec8_n,
    keep_m, last_m, carry_m,
    e_loc, e_buf, pre_buf, reach_buf, total_buf, plane_buf, inc_buf, sq_loc, sq_far,
    in_sem, param_sem, rim_send, rim_recv, edge_send, edge_recv, s1, r1, s2, r2, s3, r3, sq_send, sq_recv,
):
    shards, planes, tok, chans, modes, taps, segs = dims
    blocks = tok // SUB
    pairs = blocks // 2
    tiles = chans // LANES
    groups = tiles // SUB
    wide = SUB * LANES
    part = tiles * modes // PLANE
    me = lax.axis_index("seq")
    core = lax.axis_index("chan")
    zed = me // PLANE
    spot = lax.rem(me, PLANE)
    after = lax.rem(me + 1, shards)
    before = lax.rem(me + shards - 1, shards)

    def at(ref, start, size):
        return ref.at[pl.ds(pl.multiple_of(start, SUB), size)]

    params = [
        pltpu.make_async_copy(rate_hbm, rate_in, param_sem.at[0]),
        pltpu.make_async_copy(sf_hbm, sf_in, param_sem.at[1]),
        pltpu.make_async_copy(residue_hbm, residue_in, param_sem.at[2]),
        pltpu.make_async_copy(gain_hbm, gain_in, param_sem.at[3]),
        pltpu.make_async_copy(seg_hbm, seg_ref, param_sem.at[4]),
    ]

    def load(index, src, dst, g):
        cols = pl.ds(g * wide, wide)
        return pltpu.make_async_copy(src.at[:, cols], dst.at[:, cols], in_sem.at[index, g])

    for index in (4, 0, 1):
        params[index].start()
    for g in range(groups):
        load(1, k_hbm, k_in, g).start()
        load(2, v_hbm, v_in, g).start()
    for index in (2, 3):
        params[index].start()
    for g in range(groups):
        load(0, q_hbm, q_in, g).start()
    for g in range(groups):
        load(3, r_hbm, r_in, g).start()

    barrier = pltpu.get_barrier_semaphore()

    @pl.loop(1, PLANE)
    def _(step):
        other = zed * PLANE + lax.rem(spot + step, PLANE)
        pl.semaphore_signal(barrier, inc=1, device_id=(other, core), device_id_type=MESH)

    @pl.loop(1, planes)
    def _(step):
        other = lax.rem(zed + step, planes) * PLANE + spot
        pl.semaphore_signal(barrier, inc=1, device_id=(other, core), device_id_type=MESH)

    @pl.when(zed > 0)
    def _():
        last = (zed - 1) * PLANE + PLANE - 1
        pl.semaphore_signal(barrier, inc=1, device_id=(last, core), device_id_type=MESH)

    pl.semaphore_signal(barrier, inc=1, device_id=(before, core), device_id_type=MESH)
    pl.semaphore_signal(barrier, inc=1, device_id=(me, 1 - core), device_id_type=MESH)

    params[4].wait()
    first = me * tok
    ends = []
    running = seg_ref[0]
    ends.append(running)
    for j in range(1, segs):
        running = running + seg_ref[j]
        ends.append(running)
    big = jnp.int32(1 << 30)
    low = big
    high = jnp.int32(-1)
    for end in ends:
        low = jnp.minimum(low, jnp.where(end >= first, end, big))
        high = jnp.maximum(high, jnp.where(end <= first + tok - 1, end, -1))
    rows = lax.broadcasted_iota(jnp.int32, (tok, LANES), 0) + first
    last_m[...] = jnp.where(rows >= high, 1.0, 0.0)
    carry_m[...] = jnp.where(rows < low, 1.0, 0.0)

    params[0].wait()
    for t in range(tiles):
        rate = rate_in[:, t * LANES : (t + 1) * LANES]
        rate_n[t * modes : (t + 1) * modes, :] = rate
        dec_n[t * modes : (t + 1) * modes, :] = jnp.exp(-rate)
    params[1].wait()
    for a in (1, 2):
        for t in range(tiles):
            taps_t[a, t * SUB : t * SUB + taps, :] = sf_in[a, :, t * LANES : (t + 1) * LANES]

    def row_of(block, tile):
        return (block * tiles + tile) * SUB

    def relayout_tile(src, dst, g, pair, j):
        x = src[pl.ds(pl.multiple_of(pair * 2 * SUB, 2 * SUB), 2 * SUB),
                pl.ds(pl.multiple_of(g * wide + j * LANES, LANES), LANES)].astype(F32)
        lower = pl.multiple_of(row_of(2 * pair + 1, g * SUB + j), SUB)
        dst[pl.ds(lower, SUB), :] = x[:SUB]
        upper = pl.multiple_of(row_of(2 * pair + 2, g * SUB + j), SUB)
        dst[pl.ds(upper, SUB), :] = x[SUB:]

    def relayout(src, dst, g):
        @pl.loop(0, pairs)
        def _(pair):
            for j in range(SUB):
                relayout_tile(src, dst, g, pair, j)

    def relayout_rim(src, dst):
        for t in range(tiles):
            x = src[:, t * LANES : (t + 1) * LANES].astype(F32)
            dst[t * SUB : (t + 1) * SUB, :] = jnp.where(me > 0, x, 0.0)

    def token(ref, block, g, s):
        return ref[pl.ds(row_of(block, g * SUB) + s, SUB, stride=SUB), :]

    def per_mode(ref, g, m):
        return ref[pl.ds(g * SUB * modes + m, SUB, stride=modes), :]

    def taps_of(a, g):
        return [taps_t[a, pl.ds(g * SUB * SUB + j, SUB, stride=SUB), :] for j in range(taps)]

    def fir(window, weight):
        out = weight[0] * window[-1]
        for j in range(1, taps):
            out = out + weight[j] * window[-1 - j]
        return out

    def z_rows(t, g):
        return pl.ds(pl.multiple_of((t * groups + g) * SUB, SUB), SUB)

    def block_of_z(block, g, k_win, v_win, state, k_taps, v_taps, decay, beside=None):
        k_win, v_win, state = list(k_win), list(v_win), list(state)
        for s in range(SUB):
            if beside is not None:
                beside(s)
            k_win.append(token(xk, block, g, s))
            v_win.append(token(xv, block, g, s))
            z = fir(k_win[-taps:], k_taps) * fir(v_win[-taps:], v_taps)
            t = (block - 1) * SUB + s
            zs[z_rows(t, g), :] = z
            z = z * last_m[pl.ds(t, 1), :]
            state = [d * old + z for d, old in zip(decay, state)]
        return k_win[1 - taps :], v_win[1 - taps :], state

    zero = jnp.zeros((SUB, LANES), F32)

    load(1, k_hbm, k_in, 0).wait()
    load(2, v_hbm, v_in, 0).wait()
    for j in range(SUB):
        relayout_tile(k_in, xk, 0, 0, j)
        relayout_tile(v_in, xv, 0, 0, j)

    for g in range(groups - 1):
        load(1, k_hbm, k_in, g + 1).wait()
        load(2, v_hbm, v_in, g + 1).wait()

    def end_states(g):
        k_taps, v_taps = taps_of(1, g), taps_of(2, g)
        decay = [per_mode(dec_n, g, m) for m in range(modes)]
        behind = range(SUB - taps + 1, SUB)

        def ahead(pair, half):
            after_it = jnp.minimum(g * pairs + pair + 1, groups * pairs - 1)
            g_next, pair_next = after_it // pairs, lax.rem(after_it, pairs)

            def one(s):
                src, dst = ((k_in, xk), (v_in, xv))[s % 2]
                if half is None:
                    relayout_tile(k_in, xk, g_next, pair_next, s)
                    relayout_tile(v_in, xv, g_next, pair_next, s)
                else:
                    relayout_tile(src, dst, g_next, pair_next, half * SUB // 2 + s // 2)

            return one

        start = block_of_z(
            2, g, [token(xk, 1, g, s) for s in behind], [token(xv, 1, g, s) for s in behind],
            [zero] * modes, k_taps, v_taps, decay, ahead(0, None),
        )

        def step(pair, carried):
            for half in range(2):
                carried = block_of_z(
                    2 * pair + 1 + half, g, *carried, k_taps, v_taps, decay, ahead(pair, half)
                )
            return carried

        _, _, state = lax.fori_loop(1, pairs, step, start)
        for m in range(modes):
            e_loc[pl.ds(g * SUB * modes + m, SUB, stride=modes), :] = state[m]

    side = 4

    def nth(i, j):
        near = lambda n: (n * (n + 1) // 2) % side
        y = lax.rem(spot // side + near(i), side)
        x = lax.rem(spot + near(j), side)
        return y * side + x

    def nth_of(n):
        return nth(n // side, lax.rem(n, side))

    @pl.loop(0, groups // 2)
    def _(g):
        end_states(g)

    owned = chans // PLANE
    for owner in range(PLANE):
        cols = slice(owner * owned, (owner + 1) * owned)
        edge[owner, 0] = k_in[tok - SUB : tok, cols]
        edge[owner, 1] = v_in[tok - SUB : tok, cols]
        edge[owner, 2] = k_in[0:SUB, cols]
        edge[owner, 3] = v_in[0:SUB, cols]

    crossing = ((spot + 1) // PLANE) * ((2 * planes - 3 - zed) // (planes - 1))
    crosses = crossing > 0
    pl.semaphore_wait(barrier, PLANE - 1 + planes - 1 + 2 + PLANE * crossing)

    def edge_copy(owner, slot, plane, kind):
        return pltpu.make_async_remote_copy(
            src_ref=edge.at[owner], dst_ref=edges.at[slot],
            send_sem=edge_send.at[kind, owner], recv_sem=edge_recv.at[slot],
            device_id=(plane * PLANE + owner, core), device_id_type=MESH,
        )

    @pl.loop(1, PLANE)
    def _(step):
        edge_copy(nth_of(PLANE - step), spot, zed, 0).start()

    @pl.when(crosses)
    def _():
        @pl.loop(0, PLANE)
        def _(owner):
            edge_copy(owner, PLANE, zed + 1, 1).start()

    edges[spot] = edge[spot]

    @pl.when(zed == 0)
    def _():
        edges[PLANE] = jnp.zeros_like(edges[PLANE])

    @pl.loop(groups // 2, groups)
    def _(g):
        end_states(g)

    def round_1(other):
        return pltpu.make_async_remote_copy(
            src_ref=at(e_loc, other * part, part), dst_ref=e_buf.at[spot],
            send_sem=s1.at[other], recv_sem=r1.at[spot],
            device_id=(zed * PLANE + other, core), device_id_type=MESH,
        )

    def arrival_1(other):
        return pltpu.make_async_remote_copy(
            src_ref=at(e_loc, other * part, part), dst_ref=e_buf.at[other],
            send_sem=s1.at[other], recv_sem=r1.at[other],
            device_id=(zed * PLANE + other, core), device_id_type=MESH,
        )

    @pl.loop(1, PLANE)
    def _(step):
        round_1(nth_of(PLANE - step)).start()

    def rim_copy(index, src, dst):
        return pltpu.make_async_remote_copy(
            src_ref=src.at[pl.ds(tok - SUB, SUB)], dst_ref=dst,
            send_sem=rim_send.at[index], recv_sem=rim_recv.at[index],
            device_id=(after, core), device_id_type=MESH,
        )

    rims = [rim_copy(0, k_hbm, rim_k), rim_copy(1, v_hbm, rim_v), rim_copy(2, q_hbm, rim_q)]
    for copy in rims:
        copy.start()

    e_buf[spot] = at(e_loc, spot * part, part)[...]

    begins = rows == 0
    for end in ends:
        begins = begins | (rows == end)
    keep_m[...] = jnp.where(begins, 0.0, 1.0)
    for t in range(tiles):
        taps_t[0, t * SUB : t * SUB + taps, :] = sf_in[0, :, t * LANES : (t + 1) * LANES]
    params[2].wait()
    params[3].wait()
    for t in range(tiles):
        x = -2.0 * rate_n[t * modes : (t + 1) * modes, :]
        series = 1.0 + x * (1.0 / 6.0)
        for n in (5.0, 4.0, 3.0, 2.0):
            series = 1.0 + x * (1.0 / n) * series
        coef_n[t * modes : (t + 1) * modes, :] = residue_in[:, t * LANES : (t + 1) * LANES] * jnp.sqrt(-x * series)

    @pl.loop(0, groups)
    def _(g):
        load(0, q_hbm, q_in, g).wait()
        relayout(q_in, xq, g)

    rising = (lax.broadcasted_iota(jnp.int32, (SUB, LANES), 0) + 1).astype(F32)

    @pl.loop(0, tiles)
    def _(t):
        for m in range(modes):
            rate = rate_n[pl.ds(t * modes + m, 1), :]
            coef = coef_n[pl.ds(t * modes + m, 1), :]
            here = pl.ds(pl.multiple_of((t * modes + m) * SUB, SUB), SUB)
            weights[here, :] = coef * jnp.exp(-rate * rising)
        whole = pl.ds(pl.multiple_of(t * modes, SUB), modes)
        dec8_n[whole, :] = jnp.exp(rate_n[whole, :] * float(-SUB))

    per = tiles // PLANE
    my_rate = at(rate_n, spot * part, part)[...]
    for i in range(SUB):
        source = pl.multiple_of((spot * per + i % per) * SUB, SUB)
        dec_own[i * SUB : (i + 1) * SUB, :] = dec_n[pl.ds(source, SUB), :]
        for a in (1, 2):
            taps_own[a - 1, i * SUB : (i + 1) * SUB, :] = taps_t[a, pl.ds(source, SUB), :]
    own_decay = [dec_own[pl.ds(m, SUB, stride=modes), :] for m in range(modes)]
    own_taps = [[taps_own[a, pl.ds(j, SUB, stride=SUB), :] for j in range(taps)] for a in range(2)]

    @pl.loop(1, PLANE)
    def _(step):
        source = lax.rem(spot + step, PLANE)
        edge_copy(source, source, zed, 0).wait_recv()

    @pl.when(zed > 0)
    def _():
        edge_copy(spot, PLANE, zed, 1).wait_recv()

    for j in range(PLANE):
        for a, dst in ((0, ek), (1, ev)):
            past = edges[(j + PLANE) % (PLANE + 1), a].astype(F32)
            here = edges[j, a + 2].astype(F32)
            for i in range(per):
                tile = j * per + i
                dst[row_of(0, tile) : row_of(0, tile) + SUB, :] = past[:, i * LANES : (i + 1) * LANES]
                dst[row_of(1, tile) : row_of(1, tile) + SUB, :] = here[:, i * LANES : (i + 1) * LANES]

    for g in range(groups):
        shard = zed * PLANE + (lax.broadcasted_iota(jnp.int32, (SUB, LANES), 0) + g * SUB) // per
        begin = shard * tok
        latest = jnp.full((SUB, LANES), -1, jnp.int32)
        for end in ends:
            latest = jnp.maximum(latest, jnp.where(end <= begin + (tok - 1), end, -1))
        window = [[token(x, 0, g, s) for s in range(SUB - taps + 1, SUB)] for x in (ek, ev)]
        state = [zero] * modes
        for s in range(SUB):
            window[0].append(token(ek, 1, g, s))
            window[1].append(token(ev, 1, g, s))
            z = fir(window[0][-taps:], own_taps[0]) * fir(window[1][-taps:], own_taps[1])
            z = jnp.where(begin + s >= latest, z, 0.0)
            state = [d * old + z for d, old in zip(own_decay, state)]
        for m in range(modes):
            e_first[pl.ds(g * SUB * modes + m, SUB, stride=modes), :] = state[m]

    @pl.loop(1, PLANE)
    def _(step):
        arrival_1(lax.rem(spot + step, PLANE)).wait_recv()

    span = jnp.exp(my_rate * float(-tok))
    spot_rows = lax.broadcasted_iota(jnp.int32, (PLANE, LANES), 0) + zed * PLANE
    plane_rows = lax.broadcasted_iota(jnp.int32, (SUB, LANES), 0)
    open_here = jnp.ones((PLANE, LANES), F32)
    open_plane = jnp.ones((SUB, LANES), F32)
    for end in ends:
        open_here = jnp.where(spot_rows == end // tok, 0.0, open_here)
        open_plane = jnp.where(plane_rows == end // (tok * PLANE), 0.0, open_plane)

    rest = jnp.exp(my_rate * float(SUB - tok))
    state = jnp.zeros_like(span)
    reach = jnp.ones_like(span)
    for other in range(PLANE):
        pre_buf[other] = state
        reach_buf[other] = reach
        factor = span * open_here[other : other + 1]
        state = factor * state + e_buf[other] + rest * e_first[other * part : (other + 1) * part, :]
        reach = factor * reach
    total_buf[...] = state

    def round_2(there, slot):
        return pltpu.make_async_remote_copy(
            src_ref=total_buf, dst_ref=plane_buf.at[slot],
            send_sem=s2.at[there], recv_sem=r2.at[slot],
            device_id=(there * PLANE + spot, core), device_id_type=MESH,
        )

    @pl.loop(zed + 1, planes)
    def _(there):
        round_2(there, zed).start()

    for copy in rims:
        copy.wait_recv()
    relayout_rim(rim_k, xk)
    relayout_rim(rim_v, xv)
    relayout_rim(rim_q, xq)

    @pl.loop(0, groups)
    def _(g):
        behind = range(SUB - taps + 1, SUB)
        block_of_z(
            1, g, [token(xk, 0, g, s) for s in behind], [token(xv, 0, g, s) for s in behind],
            [], taps_of(1, g), taps_of(2, g), [],
        )

    def inner(g):
        q_taps = taps_of(0, g)
        decay = [per_mode(dec_n, g, m) for m in range(modes)]
        coef = [per_mode(coef_n, g, m) for m in range(modes)]
        behind = range(SUB - taps + 1, SUB)

        def step(block, carried):
            q_win, state = list(carried[0]), list(carried[1])
            for s in range(SUB):
                q_win.append(token(xq, block, g, s))
                qs = fir(q_win[-taps:], q_taps)
                t = (block - 1) * SUB + s
                z = zs[z_rows(t, g), :]
                keep = keep_m[pl.ds(t, 1), :]
                state = [(d * keep) * old + z for d, old in zip(decay, state)]
                out = coef[0] * state[0]
                for m in range(1, modes):
                    out = out + coef[m] * state[m]
                there = pl.ds(row_of(block - 1, g * SUB) + s, SUB, stride=SUB)
                conv_std[there, :] = out * qs
                qs_std[there, :] = qs * carry_m[pl.ds(t, 1), :]
            return q_win[1 - taps :], state

        start = ([token(xq, 0, g, s) for s in behind], [zero] * modes)
        lax.fori_loop(1, blocks + 1, step, start)

    @pl.loop(0, groups // 2)
    def _(g):
        inner(g)

    plane_span = jnp.exp(my_rate * float(-tok * PLANE))

    def plane_step(there, state):
        round_2(there, there).wait_recv()
        row = jnp.sum(jnp.where(plane_rows == there, open_plane, 0.0), axis=0, keepdims=True)
        return plane_span * row * state + plane_buf[there]

    state = lax.fori_loop(0, zed, plane_step, jnp.zeros_like(span))
    def round_3(other, slot):
        return pltpu.make_async_remote_copy(
            src_ref=pre_buf.at[other], dst_ref=inc_buf.at[slot],
            send_sem=s3.at[other], recv_sem=r3.at[slot],
            device_id=(zed * PLANE + other, core), device_id_type=MESH,
        )

    @pl.loop(1, PLANE)
    def _(step):
        other = nth_of(PLANE - step)
        pre_buf[other] = pre_buf[other] + reach_buf[other] * state
        round_3(other, spot).start()

    inc_buf[spot] = pre_buf[spot] + reach_buf[spot] * state

    @pl.loop(groups // 2, groups)
    def _(g):
        inner(g)

    for g in range(groups):
        load(3, r_hbm, r_in, g).wait()

    @pl.loop(0, tiles)
    def _(t):
        cols = pl.ds(pl.multiple_of(t * LANES, LANES), LANES)
        for pair in range(pairs):
            x = r_in[pair * 2 * SUB : (pair + 1) * 2 * SUB, cols].astype(F32)
            for half in range(2):
                here = pl.ds(pl.multiple_of(row_of(2 * pair + half, t), SUB), SUB)
                conv_std[here, :] = conv_std[here, :] + x[half * SUB : (half + 1) * SUB]

    sq_loc[...] = jnp.zeros_like(sq_loc)


    def tree(terms):
        while len(terms) > 1:
            terms = [a + b for a, b in zip(terms[::2], terms[1::2])]
        return terms[0]

    def tile_of(slot, local):
        t = slot * per + local
        value, decay = [], []
        for m in range(modes):
            here = pl.ds(pl.multiple_of((t * modes + m) * SUB, SUB), SUB)
            value.append(weights[here, :] * inc_buf[slot, pl.ds(local * modes + m, 1), :])
            decay.append(jnp.broadcast_to(dec8_n[pl.ds(t * modes + m, 1), :], (SUB, LANES)))
        cols = pl.ds(pl.multiple_of(t * LANES, LANES), LANES)
        for pair in range(pairs):
            halves = []
            for block in (2 * pair, 2 * pair + 1):
                carried = tree(value)
                if block < blocks - 1:
                    value = [v * d for v, d in zip(value, decay)]
                here = pl.ds(pl.multiple_of(row_of(block, t), SUB), SUB)
                halves.append(conv_std[here, :] + qs_std[here, :] * carried)
            both = pl.ds(pair * 2 * SUB, 2 * SUB)
            stream = jnp.concatenate(halves, axis=0).astype(jnp.bfloat16)
            stream_ref[both, cols] = stream
            back = stream.astype(F32)
            sq_loc[both, :] = sq_loc[both, :] + back * back

    @pl.loop(0, PLANE)
    def _(n):
        slot = nth_of(n)

        @pl.when(n > 0)
        def _():
            round_3(slot, slot).wait_recv()

        for local in range(per):
            tile_of(slot, local)

    swap = pltpu.make_async_remote_copy(
        src_ref=sq_loc, dst_ref=sq_far, send_sem=sq_send, recv_sem=sq_recv,
        device_id=(me, 1 - core), device_id_type=MESH,
    )
    swap.start()

    for copy in rims:
        copy.wait_send()

    @pl.loop(1, PLANE)
    def _(step):
        other = lax.rem(spot + step, PLANE)
        round_1(other).wait_send()
        round_3(other, spot).wait_send()
        edge_copy(other, spot, zed, 0).wait_send()

    @pl.when(crosses)
    def _():
        @pl.loop(0, PLANE)
        def _(owner):
            edge_copy(owner, PLANE, zed + 1, 1).wait_send()

    @pl.loop(zed + 1, planes)
    def _(there):
        round_2(there, zed).wait_send()

    swap.wait()
    total = jnp.sum(sq_loc[...] + sq_far[...], axis=1, keepdims=True)
    scale = lax.rsqrt(total * (1.0 / (2 * chans)) + 1e-6)
    scale_ref[...] = jnp.broadcast_to(scale, (tok, LANES))


def finish(tok, chans, stream_ref, scale_ref, gain_ref, stream_hbm, normed_hbm, normed, sem):
    wide = SUB * LANES
    groups = chans // wide
    copies = [pltpu.make_async_copy(stream_ref, stream_hbm, sem.at[groups])]
    copies[0].start()
    scales = [scale_ref[pair * 2 * SUB : (pair + 1) * 2 * SUB, :] for pair in range(tok // (2 * SUB))]
    for g in range(groups):
        @pl.loop(g * SUB, (g + 1) * SUB)
        def _(t):
            cols = pl.ds(pl.multiple_of(t * LANES, LANES), LANES)
            gain = gain_ref[pl.ds(t, 1), :]
            for pair, scale in enumerate(scales):
                both = slice(pair * 2 * SUB, (pair + 1) * 2 * SUB)
                x = stream_ref[both, cols].astype(F32)
                normed[both, cols] = (x * scale * gain).astype(jnp.bfloat16)

        part = slice(g * wide, (g + 1) * wide)
        copy = pltpu.make_async_copy(normed.at[:, part], normed_hbm.at[:, part], sem.at[g])
        copy.start()
        copies.append(copy)
    for copy in copies:
        copy.wait()


def body(q_proj, k_proj, v_proj, resid, short_filter, residue, rate, gain, seg_lengths):
    tok, chans = q_proj.shape
    taps = short_filter.shape[1]
    modes = rate.shape[0]
    segs = seg_lengths.shape[0]
    shards = lax.axis_size("seq")
    planes = shards // PLANE
    tiles = chans // LANES
    groups = tiles // SUB
    blocks = tok // SUB
    part = tiles * modes // PLANE
    bf16 = jnp.bfloat16
    dims = (shards, planes, tok, chans, modes, taps, segs)
    vmem = pltpu.VMEM
    sem = pltpu.SemaphoreType.DMA
    hbm_spec = pl.BlockSpec(memory_space=pltpu.HBM)
    stream, scale, gain = pl.pallas_call(
        functools.partial(kernel, dims),
        out_shape=(
            jax.ShapeDtypeStruct((tok, chans), bf16),
            jax.ShapeDtypeStruct((tok, LANES), F32),
            jax.ShapeDtypeStruct((tiles, LANES), F32),
        ),
        in_specs=[hbm_spec] * 9,
        out_specs=(pl.BlockSpec(memory_space=vmem),) * 3,
        scratch_shapes=[
            vmem((tok, chans), bf16), vmem((tok, chans), bf16), vmem((tok, chans), bf16), vmem((tok, chans), bf16),
            vmem((3, taps, chans), F32), vmem((modes, chans), F32), vmem((modes, chans), F32),
            pltpu.SMEM((segs,), jnp.int32),
            vmem((SUB, chans), bf16), vmem((SUB, chans), bf16), vmem((SUB, chans), bf16),
            vmem((PLANE, 4, SUB, chans // PLANE), bf16), vmem((PLANE + 1, 4, SUB, chans // PLANE), bf16),
            vmem((2 * tiles * SUB, LANES), F32), vmem((2 * tiles * SUB, LANES), F32),
            vmem((tiles * modes, LANES), F32), vmem((SUB * modes, LANES), F32), vmem((2, SUB * SUB, LANES), F32),
            vmem(((blocks + 1) * tiles * SUB, LANES), F32),
            vmem(((blocks + 1) * tiles * SUB, LANES), F32),
            vmem(((blocks + 1) * tiles * SUB, LANES), F32),
            vmem((blocks * tiles * SUB, LANES), F32),
            vmem((blocks * tiles * SUB, LANES), F32),
            vmem((blocks * tiles * SUB, LANES), F32),
            vmem((3, tiles * SUB, LANES), F32),
            vmem((tiles * modes, LANES), F32), vmem((tiles * modes, LANES), F32), vmem((tiles * modes, LANES), F32),
            vmem((tiles * modes * SUB, LANES), F32), vmem((tiles * modes, LANES), F32),
            vmem((tok, LANES), F32), vmem((tok, LANES), F32), vmem((tok, LANES), F32),
            vmem((tiles * modes, LANES), F32),
            vmem((PLANE, part, LANES), F32), vmem((PLANE, part, LANES), F32), vmem((PLANE, part, LANES), F32),
            vmem((part, LANES), F32), vmem((planes, part, LANES), F32), vmem((PLANE, part, LANES), F32),
            vmem((tok, LANES), F32), vmem((tok, LANES), F32),
            sem((4, groups)), sem((5,)), sem((3,)), sem((3,)), sem((2, PLANE)), sem((PLANE + 1,)),
            sem((PLANE,)), sem((PLANE,)), sem((planes,)), sem((planes,)), sem((PLANE,)), sem((PLANE,)),
            sem, sem,
        ],
        compiler_params=pltpu.CompilerParams(
            collective_id=0, has_side_effects=True, vmem_limit_bytes=40 * 1024 * 1024
        ),
        name="hyena",
    )(*(pltpu.with_memory_space_constraint(x, pltpu.HBM) for x in (
        q_proj, k_proj, v_proj, resid, short_filter, residue, rate, gain.reshape(tiles, LANES), seg_lengths
    )))
    return pl.pallas_call(
        functools.partial(finish, tok, chans),
        out_shape=(jax.ShapeDtypeStruct((tok, chans), bf16),) * 2,
        in_specs=[pl.BlockSpec(memory_space=vmem)] * 3,
        out_specs=(hbm_spec,) * 2,
        scratch_shapes=[vmem((tok, chans), bf16), sem((chans // (SUB * LANES) + 1,))],
        compiler_params=pltpu.CompilerParams(vmem_limit_bytes=16 * 1024 * 1024),
        name="finish",
    )(stream, scale, gain)


def solution(mesh):
    placed = (
        P("seq", "chan"),
        P("seq", "chan"),
        P("seq", "chan"),
        P("seq", "chan"),
        P(None, None, "chan"),
        P(None, "chan"),
        P(None, "chan"),
        P("chan"),
        P(),
    )
    return jax.shard_map(
        body,
        mesh=mesh,
        in_specs=placed,
        out_specs=(P("seq", "chan"), P("seq", "chan")),
        check_vma=False,
    )
```

```python
import functools
import jax
import jax.numpy as jnp
from jax import lax
from jax.experimental import pallas as pl
from jax.experimental.pallas import tpu as pltpu
from jax.sharding import PartitionSpec as P

MESH = pl.DeviceIdType.MESH
PLANE = 16
LANES = 128
SUB = 8
F32 = jnp.float32


def kernel(
    dims,
    q_hbm, k_hbm, v_hbm, r_hbm, sf_hbm, residue_hbm, rate_hbm, gain_hbm, seg_hbm,
    stream_ref, scale_ref, gain_in,
    q_in, k_in, v_in, r_in, sf_in, residue_in, rate_in, seg_ref,
    rim_q, rim_k, rim_v, edge, edges, ek, ev, e_first, head_n, dec_own, taps_own,
    xq, xk, xv, zs, conv_std, qs_std,
    taps_t, rate_n, coef_n, dec_n, weights, dec8_n,
    keep_m, last_m, carry_m,
    e_loc, e_buf, pre_buf, reach_buf, total_buf, plane_buf, inc_buf, sq_loc, sq_far,
    in_sem, param_sem, rim_send, rim_recv, edge_send, edge_recv, s1, r1, s2, r2, s3, r3, sq_send, sq_recv,
):
    shards, planes, tok, chans, modes, taps, segs = dims
    blocks = tok // SUB
    pairs = blocks // 2
    tiles = chans // LANES
    groups = tiles // SUB
    wide = SUB * LANES
    part = tiles * modes // PLANE
    me = lax.axis_index("seq")
    core = lax.axis_index("chan")
    zed = me // PLANE
    spot = lax.rem(me, PLANE)
    after = lax.rem(me + 1, shards)
    before = lax.rem(me + shards - 1, shards)

    def at(ref, start, size):
        return ref.at[pl.ds(pl.multiple_of(start, SUB), size)]

    params = [
        pltpu.make_async_copy(rate_hbm, rate_in, param_sem.at[0]),
        pltpu.make_async_copy(sf_hbm, sf_in, param_sem.at[1]),
        pltpu.make_async_copy(residue_hbm, residue_in, param_sem.at[2]),
        pltpu.make_async_copy(gain_hbm, gain_in, param_sem.at[3]),
        pltpu.make_async_copy(seg_hbm, seg_ref, param_sem.at[4]),
    ]

    def load(index, src, dst, g):
        cols = pl.ds(g * wide, wide)
        return pltpu.make_async_copy(src.at[:, cols], dst.at[:, cols], in_sem.at[index, g])

    for index in (4, 0, 1):
        params[index].start()
    for g in range(groups):
        load(1, k_hbm, k_in, g).start()
        load(2, v_hbm, v_in, g).start()
    for index in (2, 3):
        params[index].start()
    for g in range(groups):
        load(0, q_hbm, q_in, g).start()
    for g in range(groups):
        load(3, r_hbm, r_in, g).start()

    barrier = pltpu.get_barrier_semaphore()

    @pl.loop(1, PLANE)
    def _(step):
        other = zed * PLANE + lax.rem(spot + step, PLANE)
        pl.semaphore_signal(barrier, inc=1, device_id=(other, core), device_id_type=MESH)

    @pl.loop(1, planes)
    def _(step):
        other = lax.rem(zed + step, planes) * PLANE + spot
        pl.semaphore_signal(barrier, inc=1, device_id=(other, core), device_id_type=MESH)

    @pl.when(zed > 0)
    def _():
        last = (zed - 1) * PLANE + PLANE - 1
        pl.semaphore_signal(barrier, inc=1, device_id=(last, core), device_id_type=MESH)

    pl.semaphore_signal(barrier, inc=1, device_id=(before, core), device_id_type=MESH)
    pl.semaphore_signal(barrier, inc=1, device_id=(me, 1 - core), device_id_type=MESH)

    params[4].wait()
    first = me * tok
    ends = []
    running = seg_ref[0]
    ends.append(running)
    for j in range(1, segs):
        running = running + seg_ref[j]
        ends.append(running)
    big = jnp.int32(1 << 30)
    low = big
    low8 = big
    high = jnp.int32(-1)
    for end in ends:
        low = jnp.minimum(low, jnp.where(end >= first, end, big))
        low8 = jnp.minimum(low8, jnp.where(end >= first + SUB, end, big))
        high = jnp.maximum(high, jnp.where(end <= first + tok - 1, end, -1))
    rows = lax.broadcasted_iota(jnp.int32, (tok, LANES), 0) + first
    last_m[...] = jnp.where(rows >= high, 1.0, 0.0)
    carry_m[...] = jnp.where(rows < low8, 1.0, 0.0)
    carry_m[:SUB, :] = jnp.where(rows[:SUB] < low, 1.0, 0.0)

    params[0].wait()
    for t in range(tiles):
        rate = rate_in[:, t * LANES : (t + 1) * LANES]
        rate_n[t * modes : (t + 1) * modes, :] = rate
        dec_n[t * modes : (t + 1) * modes, :] = jnp.exp(-rate)
    params[1].wait()
    for a in (1, 2):
        for t in range(tiles):
            taps_t[a, t * SUB : t * SUB + taps, :] = sf_in[a, :, t * LANES : (t + 1) * LANES]

    def row_of(block, tile):
        return (block * tiles + tile) * SUB

    def relayout_tile(src, dst, g, pair, j):
        x = src[pl.ds(pl.multiple_of(pair * 2 * SUB, 2 * SUB), 2 * SUB),
                pl.ds(pl.multiple_of(g * wide + j * LANES, LANES), LANES)].astype(F32)
        lower = pl.multiple_of(row_of(2 * pair + 1, g * SUB + j), SUB)
        dst[pl.ds(lower, SUB), :] = x[:SUB]
        upper = pl.multiple_of(row_of(2 * pair + 2, g * SUB + j), SUB)
        dst[pl.ds(upper, SUB), :] = x[SUB:]

    def relayout(src, dst, g):
        @pl.loop(0, pairs)
        def _(pair):
            for j in range(SUB):
                relayout_tile(src, dst, g, pair, j)

    def relayout_rim(src, dst):
        for t in range(tiles):
            x = src[:, t * LANES : (t + 1) * LANES].astype(F32)
            dst[t * SUB : (t + 1) * SUB, :] = jnp.where(me > 0, x, 0.0)

    def token(ref, block, g, s):
        return ref[pl.ds(row_of(block, g * SUB) + s, SUB, stride=SUB), :]

    def per_mode(ref, g, m):
        return ref[pl.ds(g * SUB * modes + m, SUB, stride=modes), :]

    def taps_of(a, g):
        return [taps_t[a, pl.ds(g * SUB * SUB + j, SUB, stride=SUB), :] for j in range(taps)]

    def fir(window, weight):
        out = weight[0] * window[-1]
        for j in range(1, taps):
            out = out + weight[j] * window[-1 - j]
        return out

    def z_rows(t, g):
        return pl.ds(pl.multiple_of((t * groups + g) * SUB, SUB), SUB)

    def block_of_z(block, g, k_win, v_win, state, k_taps, v_taps, decay, beside=None):
        k_win, v_win, state = list(k_win), list(v_win), list(state)
        for s in range(SUB):
            if beside is not None:
                beside(s)
            k_win.append(token(xk, block, g, s))
            v_win.append(token(xv, block, g, s))
            z = fir(k_win[-taps:], k_taps) * fir(v_win[-taps:], v_taps)
            t = (block - 1) * SUB + s
            zs[z_rows(t, g), :] = z
            z = z * last_m[pl.ds(t, 1), :]
            state = [d * old + z for d, old in zip(decay, state)]
        return k_win[1 - taps :], v_win[1 - taps :], state

    zero = jnp.zeros((SUB, LANES), F32)

    load(1, k_hbm, k_in, 0).wait()
    load(2, v_hbm, v_in, 0).wait()
    for j in range(SUB):
        relayout_tile(k_in, xk, 0, 0, j)
        relayout_tile(v_in, xv, 0, 0, j)

    for g in range(groups - 1):
        load(1, k_hbm, k_in, g + 1).wait()
        load(2, v_hbm, v_in, g + 1).wait()

    def end_states(g):
        k_taps, v_taps = taps_of(1, g), taps_of(2, g)
        decay = [per_mode(dec_n, g, m) for m in range(modes)]
        behind = range(SUB - taps + 1, SUB)

        def ahead(pair, half):
            after_it = jnp.minimum(g * pairs + pair + 1, groups * pairs - 1)
            g_next, pair_next = after_it // pairs, lax.rem(after_it, pairs)

            def one(s):
                src, dst = ((k_in, xk), (v_in, xv))[s % 2]
                if half is None:
                    relayout_tile(k_in, xk, g_next, pair_next, s)
                    relayout_tile(v_in, xv, g_next, pair_next, s)
                else:
                    relayout_tile(src, dst, g_next, pair_next, half * SUB // 2 + s // 2)

            return one

        start = block_of_z(
            2, g, [token(xk, 1, g, s) for s in behind], [token(xv, 1, g, s) for s in behind],
            [zero] * modes, k_taps, v_taps, decay, ahead(0, None),
        )

        def step(pair, carried):
            for half in range(2):
                carried = block_of_z(
                    2 * pair + 1 + half, g, *carried, k_taps, v_taps, decay, ahead(pair, half)
                )
            return carried

        _, _, state = lax.fori_loop(1, pairs, step, start)
        for m in range(modes):
            e_loc[pl.ds(g * SUB * modes + m, SUB, stride=modes), :] = state[m]

    side = 4

    def nth(i, j):
        near = lambda n: (n * (n + 1) // 2) % side
        y = lax.rem(spot // side + near(i), side)
        x = lax.rem(spot + near(j), side)
        return y * side + x

    def nth_of(n):
        return nth(n // side, lax.rem(n, side))

    @pl.loop(0, groups // 2)
    def _(g):
        end_states(g)

    owned = chans // PLANE
    for owner in range(PLANE):
        cols = slice(owner * owned, (owner + 1) * owned)
        edge[owner, 0] = k_in[tok - SUB : tok, cols]
        edge[owner, 1] = v_in[tok - SUB : tok, cols]
        edge[owner, 2] = k_in[0:SUB, cols]
        edge[owner, 3] = v_in[0:SUB, cols]

    crossing = ((spot + 1) // PLANE) * ((2 * planes - 3 - zed) // (planes - 1))
    crosses = crossing > 0
    pl.semaphore_wait(barrier, PLANE - 1 + planes - 1 + 2 + PLANE * crossing)

    def edge_copy(owner, slot, plane, kind):
        return pltpu.make_async_remote_copy(
            src_ref=edge.at[owner], dst_ref=edges.at[slot],
            send_sem=edge_send.at[kind, owner], recv_sem=edge_recv.at[slot],
            device_id=(plane * PLANE + owner, core), device_id_type=MESH,
        )

    @pl.loop(1, PLANE)
    def _(step):
        edge_copy(nth_of(PLANE - step), spot, zed, 0).start()

    @pl.when(crosses)
    def _():
        @pl.loop(0, PLANE)
        def _(owner):
            edge_copy(owner, PLANE, zed + 1, 1).start()

    edges[spot] = edge[spot]

    @pl.when(zed == 0)
    def _():
        edges[PLANE] = jnp.zeros_like(edges[PLANE])

    @pl.loop(groups // 2, groups)
    def _(g):
        end_states(g)

    def round_1(other):
        return pltpu.make_async_remote_copy(
            src_ref=at(e_loc, other * part, part), dst_ref=e_buf.at[spot],
            send_sem=s1.at[other], recv_sem=r1.at[spot],
            device_id=(zed * PLANE + other, core), device_id_type=MESH,
        )

    def arrival_1(other):
        return pltpu.make_async_remote_copy(
            src_ref=at(e_loc, other * part, part), dst_ref=e_buf.at[other],
            send_sem=s1.at[other], recv_sem=r1.at[other],
            device_id=(zed * PLANE + other, core), device_id_type=MESH,
        )

    @pl.loop(1, PLANE)
    def _(step):
        round_1(nth_of(PLANE - step)).start()

    def rim_copy(index, src, dst):
        return pltpu.make_async_remote_copy(
            src_ref=src.at[pl.ds(tok - SUB, SUB)], dst_ref=dst,
            send_sem=rim_send.at[index], recv_sem=rim_recv.at[index],
            device_id=(after, core), device_id_type=MESH,
        )

    rims = [rim_copy(0, k_hbm, rim_k), rim_copy(1, v_hbm, rim_v), rim_copy(2, q_hbm, rim_q)]
    for copy in rims:
        copy.start()

    e_buf[spot] = at(e_loc, spot * part, part)[...]

    begins = rows == 0
    for end in ends:
        begins = begins | (rows == end)
    keep_m[...] = jnp.where(begins, 0.0, 1.0)
    for t in range(tiles):
        taps_t[0, t * SUB : t * SUB + taps, :] = sf_in[0, :, t * LANES : (t + 1) * LANES]
    params[2].wait()
    params[3].wait()
    for t in range(tiles):
        x = -2.0 * rate_n[t * modes : (t + 1) * modes, :]
        series = 1.0 + x * (1.0 / 6.0)
        for n in (5.0, 4.0, 3.0, 2.0):
            series = 1.0 + x * (1.0 / n) * series
        coef_n[t * modes : (t + 1) * modes, :] = residue_in[:, t * LANES : (t + 1) * LANES] * jnp.sqrt(-x * series)

    @pl.loop(0, groups)
    def _(g):
        load(0, q_hbm, q_in, g).wait()
        relayout(q_in, xq, g)

    rising = (lax.broadcasted_iota(jnp.int32, (SUB, LANES), 0) + 1).astype(F32)

    @pl.loop(0, tiles)
    def _(t):
        for m in range(modes):
            rate = rate_n[pl.ds(t * modes + m, 1), :]
            coef = coef_n[pl.ds(t * modes + m, 1), :]
            here = pl.ds(pl.multiple_of((t * modes + m) * SUB, SUB), SUB)
            weights[here, :] = coef * jnp.exp(-rate * rising)
        whole = pl.ds(pl.multiple_of(t * modes, SUB), modes)
        dec8_n[whole, :] = jnp.exp(rate_n[whole, :] * float(-SUB))

    def tree(terms):
        while len(terms) > 1:
            terms = [a + b for a, b in zip(terms[::2], terms[1::2])]
        return terms[0]

    def conv_block(block, g, q_win, state, q_taps, decay, coef, z_of):
        q_win, state = list(q_win), list(state)
        for s in range(SUB):
            q_win.append(token(xq, block, g, s))
            qs = fir(q_win[-taps:], q_taps)
            t = (block - 1) * SUB + s
            z = z_of(t, s)
            keep = keep_m[pl.ds(t, 1), :]
            state = [(d * keep) * old + z for d, old in zip(decay, state)]
            out = tree([c * part for c, part in zip(coef, state)])
            there = pl.ds(row_of(block - 1, g * SUB) + s, SUB, stride=SUB)
            conv_std[there, :] = out * qs
            qs_std[there, :] = qs * carry_m[pl.ds(t, 1), :]
        return q_win[1 - taps :], state

    behind = range(SUB - taps + 1, SUB)

    def inner(g):
        q_taps = taps_of(0, g)
        decay = [per_mode(dec_n, g, m) for m in range(modes)]
        coef = [per_mode(coef_n, g, m) for m in range(modes)]

        def step(block, carried):
            return conv_block(block, g, *carried, q_taps, decay, coef, lambda t, s: zs[z_rows(t, g), :])

        lax.fori_loop(2, blocks + 1, step, ([token(xq, 1, g, s) for s in behind], [zero] * modes))

    def head(g):
        windows = [[token(x, 0, g, s) for s in behind] for x in (xk, xv)]
        weight = [taps_of(1, g), taps_of(2, g)]

        def z_of(t, s):
            for window, x in zip(windows, (xk, xv)):
                window.append(token(x, 1, g, s))
            return fir(windows[0][-taps:], weight[0]) * fir(windows[1][-taps:], weight[1])

        decay = [per_mode(dec_n, g, m) for m in range(modes)]
        coef = [per_mode(coef_n, g, m) for m in range(modes)]
        _, state = conv_block(
            1, g, [token(xq, 0, g, s) for s in behind], [zero] * modes, taps_of(0, g), decay, coef, z_of
        )
        for m in range(modes):
            head_n[pl.ds(g * SUB * modes + m, SUB, stride=modes), :] = state[m]

    inner(0)

    per = tiles // PLANE
    my_rate = at(rate_n, spot * part, part)[...]
    for i in range(SUB):
        source = pl.multiple_of((spot * per + i % per) * SUB, SUB)
        dec_own[i * SUB : (i + 1) * SUB, :] = dec_n[pl.ds(source, SUB), :]
        for a in (1, 2):
            taps_own[a - 1, i * SUB : (i + 1) * SUB, :] = taps_t[a, pl.ds(source, SUB), :]
    own_decay = [dec_own[pl.ds(m, SUB, stride=modes), :] for m in range(modes)]
    own_taps = [[taps_own[a, pl.ds(j, SUB, stride=SUB), :] for j in range(taps)] for a in range(2)]

    @pl.loop(1, PLANE)
    def _(step):
        source = lax.rem(spot + step, PLANE)
        edge_copy(source, source, zed, 0).wait_recv()

    @pl.when(zed > 0)
    def _():
        edge_copy(spot, PLANE, zed, 1).wait_recv()

    for j in range(PLANE):
        for a, dst in ((0, ek), (1, ev)):
            past = edges[(j + PLANE) % (PLANE + 1), a].astype(F32)
            here = edges[j, a + 2].astype(F32)
            for i in range(per):
                tile = j * per + i
                dst[row_of(0, tile) : row_of(0, tile) + SUB, :] = past[:, i * LANES : (i + 1) * LANES]
                dst[row_of(1, tile) : row_of(1, tile) + SUB, :] = here[:, i * LANES : (i + 1) * LANES]

    for g in range(groups):
        shard = zed * PLANE + (lax.broadcasted_iota(jnp.int32, (SUB, LANES), 0) + g * SUB) // per
        begin = shard * tok
        latest = jnp.full((SUB, LANES), -1, jnp.int32)
        for end in ends:
            latest = jnp.maximum(latest, jnp.where(end <= begin + (tok - 1), end, -1))
        window = [[token(x, 0, g, s) for s in range(SUB - taps + 1, SUB)] for x in (ek, ev)]
        state = [zero] * modes
        for s in range(SUB):
            window[0].append(token(ek, 1, g, s))
            window[1].append(token(ev, 1, g, s))
            z = fir(window[0][-taps:], own_taps[0]) * fir(window[1][-taps:], own_taps[1])
            z = jnp.where(begin + s >= latest, z, 0.0)
            state = [d * old + z for d, old in zip(own_decay, state)]
        for m in range(modes):
            e_first[pl.ds(g * SUB * modes + m, SUB, stride=modes), :] = state[m]

    @pl.loop(1, PLANE)
    def _(step):
        arrival_1(lax.rem(spot + step, PLANE)).wait_recv()

    span = jnp.exp(my_rate * float(-tok))
    spot_rows = lax.broadcasted_iota(jnp.int32, (PLANE, LANES), 0) + zed * PLANE
    plane_rows = lax.broadcasted_iota(jnp.int32, (SUB, LANES), 0)
    open_here = jnp.ones((PLANE, LANES), F32)
    open_plane = jnp.ones((SUB, LANES), F32)
    for end in ends:
        open_here = jnp.where(spot_rows == end // tok, 0.0, open_here)
        open_plane = jnp.where(plane_rows == end // (tok * PLANE), 0.0, open_plane)

    rest = jnp.exp(my_rate * float(SUB - tok))
    state = jnp.zeros_like(span)
    reach = jnp.ones_like(span)
    for other in range(PLANE):
        pre_buf[other] = state
        reach_buf[other] = reach
        factor = span * open_here[other : other + 1]
        state = factor * state + e_buf[other] + rest * e_first[other * part : (other + 1) * part, :]
        reach = factor * reach
    total_buf[...] = state

    def round_2(there, slot):
        return pltpu.make_async_remote_copy(
            src_ref=total_buf, dst_ref=plane_buf.at[slot],
            send_sem=s2.at[there], recv_sem=r2.at[slot],
            device_id=(there * PLANE + spot, core), device_id_type=MESH,
        )

    @pl.loop(zed + 1, planes)
    def _(there):
        round_2(there, zed).start()

    @pl.loop(1, groups - 1)
    def _(g):
        inner(g)

    plane_span = jnp.exp(my_rate * float(-tok * PLANE))

    def plane_step(there, state):
        round_2(there, there).wait_recv()
        row = jnp.sum(jnp.where(plane_rows == there, open_plane, 0.0), axis=0, keepdims=True)
        return plane_span * row * state + plane_buf[there]

    state = lax.fori_loop(0, zed, plane_step, jnp.zeros_like(span))
    def round_3(other, slot):
        return pltpu.make_async_remote_copy(
            src_ref=pre_buf.at[other], dst_ref=inc_buf.at[slot],
            send_sem=s3.at[other], recv_sem=r3.at[slot],
            device_id=(zed * PLANE + other, core), device_id_type=MESH,
        )

    @pl.loop(1, PLANE)
    def _(step):
        other = nth_of(PLANE - step)
        pre_buf[other] = pre_buf[other] + reach_buf[other] * state
        round_3(other, spot).start()

    inc_buf[spot] = pre_buf[spot] + reach_buf[spot] * state

    inner(groups - 1)

    for copy in rims:
        copy.wait_recv()
    relayout_rim(rim_k, xk)
    relayout_rim(rim_v, xv)
    relayout_rim(rim_q, xq)

    @pl.loop(0, groups)
    def _(g):
        head(g)

    for g in range(groups):
        load(3, r_hbm, r_in, g).wait()

    @pl.loop(0, tiles)
    def _(t):
        cols = pl.ds(pl.multiple_of(t * LANES, LANES), LANES)
        for pair in range(pairs):
            x = r_in[pair * 2 * SUB : (pair + 1) * 2 * SUB, cols].astype(F32)
            for half in range(2):
                here = pl.ds(pl.multiple_of(row_of(2 * pair + half, t), SUB), SUB)
                conv_std[here, :] = conv_std[here, :] + x[half * SUB : (half + 1) * SUB]

    sq_loc[...] = jnp.zeros_like(sq_loc)


    def tile_of(slot, local):
        t = slot * per + local
        whole = pl.ds(pl.multiple_of(t * modes, SUB), modes)
        incoming = inc_buf[slot, local * modes : (local + 1) * modes, :]
        at_8 = dec8_n[whole, :] * carry_m[SUB - 1 : SUB, :] * incoming + head_n[whole, :]
        value, later, decay = [], [], []
        for m in range(modes):
            here = pl.ds(pl.multiple_of((t * modes + m) * SUB, SUB), SUB)
            weight = weights[here, :]
            value.append(weight * incoming[m : m + 1])
            later.append(weight * at_8[m : m + 1])
            decay.append(jnp.broadcast_to(dec8_n[pl.ds(t * modes + m, 1), :], (SUB, LANES)))
        cols = pl.ds(pl.multiple_of(t * LANES, LANES), LANES)
        for pair in range(pairs):
            halves = []
            for block in (2 * pair, 2 * pair + 1):
                carried = tree(value)
                if block == 0:
                    value = later
                elif block < blocks - 1:
                    value = [v * d for v, d in zip(value, decay)]
                here = pl.ds(pl.multiple_of(row_of(block, t), SUB), SUB)
                halves.append(conv_std[here, :] + qs_std[here, :] * carried)
            both = pl.ds(pair * 2 * SUB, 2 * SUB)
            stream = jnp.concatenate(halves, axis=0).astype(jnp.bfloat16)
            stream_ref[both, cols] = stream
            back = stream.astype(F32)
            sq_loc[both, :] = sq_loc[both, :] + back * back

    @pl.loop(0, PLANE)
    def _(n):
        slot = nth_of(n)

        @pl.when(n > 0)
        def _():
            round_3(slot, slot).wait_recv()

        for local in range(per):
            tile_of(slot, local)

    swap = pltpu.make_async_remote_copy(
        src_ref=sq_loc, dst_ref=sq_far, send_sem=sq_send, recv_sem=sq_recv,
        device_id=(me, 1 - core), device_id_type=MESH,
    )
    swap.start()

    for copy in rims:
        copy.wait_send()

    @pl.loop(1, PLANE)
    def _(step):
        other = lax.rem(spot + step, PLANE)
        round_1(other).wait_send()
        round_3(other, spot).wait_send()
        edge_copy(other, spot, zed, 0).wait_send()

    @pl.when(crosses)
    def _():
        @pl.loop(0, PLANE)
        def _(owner):
            edge_copy(owner, PLANE, zed + 1, 1).wait_send()

    @pl.loop(zed + 1, planes)
    def _(there):
        round_2(there, zed).wait_send()

    swap.wait()
    total = jnp.sum(sq_loc[...] + sq_far[...], axis=1, keepdims=True)
    scale = lax.rsqrt(total * (1.0 / (2 * chans)) + 1e-6)
    scale_ref[...] = jnp.broadcast_to(scale, (tok, LANES))


def finish(tok, chans, stream_ref, scale_ref, gain_ref, stream_hbm, normed_hbm, normed, sem):
    wide = SUB * LANES
    groups = chans // wide
    copies = [pltpu.make_async_copy(stream_ref, stream_hbm, sem.at[groups])]
    copies[0].start()
    scales = [scale_ref[pair * 2 * SUB : (pair + 1) * 2 * SUB, :] for pair in range(tok // (2 * SUB))]
    for g in range(groups):
        @pl.loop(g * SUB, (g + 1) * SUB)
        def _(t):
            cols = pl.ds(pl.multiple_of(t * LANES, LANES), LANES)
            gain = gain_ref[pl.ds(t, 1), :]
            for pair, scale in enumerate(scales):
                both = slice(pair * 2 * SUB, (pair + 1) * 2 * SUB)
                x = stream_ref[both, cols].astype(F32)
                normed[both, cols] = (x * scale * gain).astype(jnp.bfloat16)

        part = slice(g * wide, (g + 1) * wide)
        copy = pltpu.make_async_copy(normed.at[:, part], normed_hbm.at[:, part], sem.at[g])
        copy.start()
        copies.append(copy)
    for copy in copies:
        copy.wait()


def body(q_proj, k_proj, v_proj, resid, short_filter, residue, rate, gain, seg_lengths):
    tok, chans = q_proj.shape
    taps = short_filter.shape[1]
    modes = rate.shape[0]
    segs = seg_lengths.shape[0]
    shards = lax.axis_size("seq")
    planes = shards // PLANE
    tiles = chans // LANES
    groups = tiles // SUB
    blocks = tok // SUB
    part = tiles * modes // PLANE
    bf16 = jnp.bfloat16
    dims = (shards, planes, tok, chans, modes, taps, segs)
    vmem = pltpu.VMEM
    sem = pltpu.SemaphoreType.DMA
    hbm_spec = pl.BlockSpec(memory_space=pltpu.HBM)
    stream, scale, gain = pl.pallas_call(
        functools.partial(kernel, dims),
        out_shape=(
            jax.ShapeDtypeStruct((tok, chans), bf16),
            jax.ShapeDtypeStruct((tok, LANES), F32),
            jax.ShapeDtypeStruct((tiles, LANES), F32),
        ),
        in_specs=[hbm_spec] * 9,
        out_specs=(pl.BlockSpec(memory_space=vmem),) * 3,
        scratch_shapes=[
            vmem((tok, chans), bf16), vmem((tok, chans), bf16), vmem((tok, chans), bf16), vmem((tok, chans), bf16),
            vmem((3, taps, chans), F32), vmem((modes, chans), F32), vmem((modes, chans), F32),
            pltpu.SMEM((segs,), jnp.int32),
            vmem((SUB, chans), bf16), vmem((SUB, chans), bf16), vmem((SUB, chans), bf16),
            vmem((PLANE, 4, SUB, chans // PLANE), bf16), vmem((PLANE + 1, 4, SUB, chans // PLANE), bf16),
            vmem((2 * tiles * SUB, LANES), F32), vmem((2 * tiles * SUB, LANES), F32),
            vmem((tiles * modes, LANES), F32), vmem((tiles * modes, LANES), F32),
            vmem((SUB * modes, LANES), F32), vmem((2, SUB * SUB, LANES), F32),
            vmem(((blocks + 1) * tiles * SUB, LANES), F32),
            vmem(((blocks + 1) * tiles * SUB, LANES), F32),
            vmem(((blocks + 1) * tiles * SUB, LANES), F32),
            vmem((blocks * tiles * SUB, LANES), F32),
            vmem((blocks * tiles * SUB, LANES), F32),
            vmem((blocks * tiles * SUB, LANES), F32),
            vmem((3, tiles * SUB, LANES), F32),
            vmem((tiles * modes, LANES), F32), vmem((tiles * modes, LANES), F32), vmem((tiles * modes, LANES), F32),
            vmem((tiles * modes * SUB, LANES), F32), vmem((tiles * modes, LANES), F32),
            vmem((tok, LANES), F32), vmem((tok, LANES), F32), vmem((tok, LANES), F32),
            vmem((tiles * modes, LANES), F32),
            vmem((PLANE, part, LANES), F32), vmem((PLANE, part, LANES), F32), vmem((PLANE, part, LANES), F32),
            vmem((part, LANES), F32), vmem((planes, part, LANES), F32), vmem((PLANE, part, LANES), F32),
            vmem((tok, LANES), F32), vmem((tok, LANES), F32),
            sem((4, groups)), sem((5,)), sem((3,)), sem((3,)), sem((2, PLANE)), sem((PLANE + 1,)),
            sem((PLANE,)), sem((PLANE,)), sem((planes,)), sem((planes,)), sem((PLANE,)), sem((PLANE,)),
            sem, sem,
        ],
        compiler_params=pltpu.CompilerParams(
            collective_id=0, has_side_effects=True, vmem_limit_bytes=40 * 1024 * 1024
        ),
        name="hyena",
    )(*(pltpu.with_memory_space_constraint(x, pltpu.HBM) for x in (
        q_proj, k_proj, v_proj, resid, short_filter, residue, rate, gain.reshape(tiles, LANES), seg_lengths
    )))
    return pl.pallas_call(
        functools.partial(finish, tok, chans),
        out_shape=(jax.ShapeDtypeStruct((tok, chans), bf16),) * 2,
        in_specs=[pl.BlockSpec(memory_space=vmem)] * 3,
        out_specs=(hbm_spec,) * 2,
        scratch_shapes=[vmem((tok, chans), bf16), sem((chans // (SUB * LANES) + 1,))],
        compiler_params=pltpu.CompilerParams(vmem_limit_bytes=16 * 1024 * 1024),
        name="finish",
    )(stream, scale, gain)


def solution(mesh):
    placed = (
        P("seq", "chan"),
        P("seq", "chan"),
        P("seq", "chan"),
        P("seq", "chan"),
        P(None, None, "chan"),
        P(None, "chan"),
        P(None, "chan"),
        P("chan"),
        P(),
    )
    return jax.shard_map(
        body,
        mesh=mesh,
        in_specs=placed,
        out_specs=(P("seq", "chan"), P("seq", "chan")),
        check_vma=False,
    )
```

```python
import functools
import jax
import jax.numpy as jnp
from jax import lax
from jax.experimental import pallas as pl
from jax.experimental.pallas import tpu as pltpu
from jax.sharding import PartitionSpec as P

MESH = pl.DeviceIdType.MESH
PLANE = 16
LANES = 128
SUB = 8
F32 = jnp.float32


def kernel(
    dims,
    q_hbm, k_hbm, v_hbm, r_hbm, sf_hbm, residue_hbm, rate_hbm, gain_hbm, seg_hbm,
    stream_ref, scale_ref, gain_in,
    q_in, k_in, v_in, r_in, sf_in, residue_in, rate_in, seg_ref,
    rim_q, rim_k, rim_v, edge, edges, ek, ev, e_first, head_n, dec_own, taps_own,
    xq, xk, xv, zs, conv_std, qs_std,
    taps_t, rate_n, coef_n, dec_n, weights, dec8_n,
    keep_m, last_m, carry_m,
    e_loc, e_buf, pre_buf, reach_buf, total_buf, plane_buf, inc_buf, sq_loc, sq_far,
    in_sem, param_sem, rim_send, rim_recv, edge_send, edge_recv, s1, r1, s2, r2, s3, r3, sq_send, sq_recv,
):
    shards, planes, tok, chans, modes, taps, segs = dims
    blocks = tok // SUB
    pairs = blocks // 2
    tiles = chans // LANES
    groups = tiles // SUB
    wide = SUB * LANES
    part = tiles * modes // PLANE
    me = lax.axis_index("seq")
    core = lax.axis_index("chan")
    zed = me // PLANE
    spot = lax.rem(me, PLANE)
    after = lax.rem(me + 1, shards)
    before = lax.rem(me + shards - 1, shards)

    def at(ref, start, size):
        return ref.at[pl.ds(pl.multiple_of(start, SUB), size)]

    params = [
        pltpu.make_async_copy(rate_hbm, rate_in, param_sem.at[0]),
        pltpu.make_async_copy(sf_hbm, sf_in, param_sem.at[1]),
        pltpu.make_async_copy(residue_hbm, residue_in, param_sem.at[2]),
        pltpu.make_async_copy(gain_hbm, gain_in, param_sem.at[3]),
        pltpu.make_async_copy(seg_hbm, seg_ref, param_sem.at[4]),
    ]

    def load(index, src, dst, g):
        cols = pl.ds(g * wide, wide)
        return pltpu.make_async_copy(src.at[:, cols], dst.at[:, cols], in_sem.at[index, g])

    for index in (4, 0, 1):
        params[index].start()
    for g in range(groups):
        load(1, k_hbm, k_in, g).start()
        load(2, v_hbm, v_in, g).start()
    barrier = pltpu.get_barrier_semaphore()

    @pl.loop(1, PLANE)
    def _(step):
        other = zed * PLANE + lax.rem(spot + step, PLANE)
        pl.semaphore_signal(barrier, inc=1, device_id=(other, core), device_id_type=MESH)

    @pl.loop(1, planes)
    def _(step):
        other = lax.rem(zed + step, planes) * PLANE + spot
        pl.semaphore_signal(barrier, inc=1, device_id=(other, core), device_id_type=MESH)

    @pl.when(zed > 0)
    def _():
        last = (zed - 1) * PLANE + PLANE - 1
        pl.semaphore_signal(barrier, inc=1, device_id=(last, core), device_id_type=MESH)

    pl.semaphore_signal(barrier, inc=1, device_id=(before, core), device_id_type=MESH)
    pl.semaphore_signal(barrier, inc=1, device_id=(me, 1 - core), device_id_type=MESH)

    params[4].wait()
    first = me * tok
    ends = []
    running = seg_ref[0]
    ends.append(running)
    for j in range(1, segs):
        running = running + seg_ref[j]
        ends.append(running)
    big = jnp.int32(1 << 30)
    low = big
    low8 = big
    high = jnp.int32(-1)
    for end in ends:
        low = jnp.minimum(low, jnp.where(end >= first, end, big))
        low8 = jnp.minimum(low8, jnp.where(end >= first + SUB, end, big))
        high = jnp.maximum(high, jnp.where(end <= first + tok - 1, end, -1))
    rows = lax.broadcasted_iota(jnp.int32, (tok, LANES), 0) + first
    last_m[...] = jnp.where(rows >= high, 1.0, 0.0)
    carry_m[...] = jnp.where(rows < low8, 1.0, 0.0)
    carry_m[:SUB, :] = jnp.where(rows[:SUB] < low, 1.0, 0.0)

    params[0].wait()
    for t in range(tiles):
        rate = rate_in[:, t * LANES : (t + 1) * LANES]
        rate_n[t * modes : (t + 1) * modes, :] = rate
        dec_n[t * modes : (t + 1) * modes, :] = jnp.exp(-rate)
    params[1].wait()
    for a in (1, 2):
        for t in range(tiles):
            taps_t[a, t * SUB : t * SUB + taps, :] = sf_in[a, :, t * LANES : (t + 1) * LANES]

    def row_of(block, tile):
        return (block * tiles + tile) * SUB

    def relayout_tile(src, dst, g, pair, j):
        x = src[pl.ds(pl.multiple_of(pair * 2 * SUB, 2 * SUB), 2 * SUB),
                pl.ds(pl.multiple_of(g * wide + j * LANES, LANES), LANES)].astype(F32)
        lower = pl.multiple_of(row_of(2 * pair + 1, g * SUB + j), SUB)
        dst[pl.ds(lower, SUB), :] = x[:SUB]
        upper = pl.multiple_of(row_of(2 * pair + 2, g * SUB + j), SUB)
        dst[pl.ds(upper, SUB), :] = x[SUB:]

    def relayout(src, dst, g):
        @pl.loop(0, pairs)
        def _(pair):
            for j in range(SUB):
                relayout_tile(src, dst, g, pair, j)

    def relayout_rim(src, dst):
        for t in range(tiles):
            x = src[:, t * LANES : (t + 1) * LANES].astype(F32)
            dst[t * SUB : (t + 1) * SUB, :] = jnp.where(me > 0, x, 0.0)

    def token(ref, block, g, s):
        return ref[pl.ds(row_of(block, g * SUB) + s, SUB, stride=SUB), :]

    def per_mode(ref, g, m):
        return ref[pl.ds(g * SUB * modes + m, SUB, stride=modes), :]

    def taps_of(a, g):
        return [taps_t[a, pl.ds(g * SUB * SUB + j, SUB, stride=SUB), :] for j in range(taps)]

    def fir(window, weight):
        out = weight[0] * window[-1]
        for j in range(1, taps):
            out = out + weight[j] * window[-1 - j]
        return out

    def z_rows(t, g):
        return pl.ds(pl.multiple_of((t * groups + g) * SUB, SUB), SUB)

    def block_of_z(block, g, k_win, v_win, state, k_taps, v_taps, decay, beside=None):
        k_win, v_win, state = list(k_win), list(v_win), list(state)
        for s in range(SUB):
            if beside is not None:
                beside(s)
            k_win.append(token(xk, block, g, s))
            v_win.append(token(xv, block, g, s))
            z = fir(k_win[-taps:], k_taps) * fir(v_win[-taps:], v_taps)
            t = (block - 1) * SUB + s
            zs[z_rows(t, g), :] = z
            z = z * last_m[pl.ds(t, 1), :]
            state = [d * old + z for d, old in zip(decay, state)]
        return k_win[1 - taps :], v_win[1 - taps :], state

    zero = jnp.zeros((SUB, LANES), F32)

    load(1, k_hbm, k_in, 0).wait()
    load(2, v_hbm, v_in, 0).wait()
    for j in range(SUB):
        relayout_tile(k_in, xk, 0, 0, j)
        relayout_tile(v_in, xv, 0, 0, j)

    def end_states(g):
        k_taps, v_taps = taps_of(1, g), taps_of(2, g)
        decay = [per_mode(dec_n, g, m) for m in range(modes)]
        behind = range(SUB - taps + 1, SUB)

        def ahead(pair, half):
            after_it = jnp.minimum(g * pairs + pair + 1, groups * pairs - 1)
            g_next, pair_next = after_it // pairs, lax.rem(after_it, pairs)

            def one(s):
                src, dst = ((k_in, xk), (v_in, xv))[s % 2]
                if half is None:
                    relayout_tile(k_in, xk, g_next, pair_next, s)
                    relayout_tile(v_in, xv, g_next, pair_next, s)
                else:
                    relayout_tile(src, dst, g_next, pair_next, half * SUB // 2 + s // 2)

            return one

        start = block_of_z(
            2, g, [token(xk, 1, g, s) for s in behind], [token(xv, 1, g, s) for s in behind],
            [zero] * modes, k_taps, v_taps, decay, ahead(0, None),
        )

        def step(pair, carried):
            for half in range(2):
                carried = block_of_z(
                    2 * pair + 1 + half, g, *carried, k_taps, v_taps, decay, ahead(pair, half)
                )
            return carried

        _, _, state = lax.fori_loop(1, pairs, step, start)
        for m in range(modes):
            e_loc[pl.ds(g * SUB * modes + m, SUB, stride=modes), :] = state[m]

    side = 4

    def nth(i, j):
        near = lambda n: (n * (n + 1) // 2) % side
        y = lax.rem(spot // side + near(i), side)
        x = lax.rem(spot + near(j), side)
        return y * side + x

    def nth_of(n):
        return nth(n // side, lax.rem(n, side))

    @pl.loop(0, groups // 2)
    def _(g):
        load(1, k_hbm, k_in, g + 1).wait()
        load(2, v_hbm, v_in, g + 1).wait()
        end_states(g)

    for g in range(groups // 2 + 1, groups):
        load(1, k_hbm, k_in, g).wait()
        load(2, v_hbm, v_in, g).wait()
    for index in (2, 3):
        params[index].start()
    for g in range(groups):
        load(0, q_hbm, q_in, g).start()
    for g in range(groups):
        load(3, r_hbm, r_in, g).start()

    owned = chans // PLANE
    for owner in range(PLANE):
        cols = slice(owner * owned, (owner + 1) * owned)
        edge[owner, 0] = k_in[tok - SUB : tok, cols]
        edge[owner, 1] = v_in[tok - SUB : tok, cols]
        edge[owner, 2] = k_in[0:SUB, cols]
        edge[owner, 3] = v_in[0:SUB, cols]

    crossing = ((spot + 1) // PLANE) * ((2 * planes - 3 - zed) // (planes - 1))
    crosses = crossing > 0
    pl.semaphore_wait(barrier, PLANE - 1 + planes - 1 + 2 + PLANE * crossing)

    def edge_copy(owner, slot, plane, kind):
        return pltpu.make_async_remote_copy(
            src_ref=edge.at[owner], dst_ref=edges.at[slot],
            send_sem=edge_send.at[kind, owner], recv_sem=edge_recv.at[slot],
            device_id=(plane * PLANE + owner, core), device_id_type=MESH,
        )

    @pl.loop(1, PLANE)
    def _(step):
        edge_copy(nth_of(PLANE - step), spot, zed, 0).start()

    @pl.when(crosses)
    def _():
        @pl.loop(0, PLANE)
        def _(owner):
            edge_copy(owner, PLANE, zed + 1, 1).start()

    edges[spot] = edge[spot]

    @pl.when(zed == 0)
    def _():
        edges[PLANE] = jnp.zeros_like(edges[PLANE])

    @pl.loop(groups // 2, groups)
    def _(g):
        end_states(g)

    def round_1(other):
        return pltpu.make_async_remote_copy(
            src_ref=at(e_loc, other * part, part), dst_ref=e_buf.at[spot],
            send_sem=s1.at[other], recv_sem=r1.at[spot],
            device_id=(zed * PLANE + other, core), device_id_type=MESH,
        )

    def arrival_1(other):
        return pltpu.make_async_remote_copy(
            src_ref=at(e_loc, other * part, part), dst_ref=e_buf.at[other],
            send_sem=s1.at[other], recv_sem=r1.at[other],
            device_id=(zed * PLANE + other, core), device_id_type=MESH,
        )

    @pl.loop(1, PLANE)
    def _(step):
        round_1(nth_of(PLANE - step)).start()

    def rim_copy(index, src, dst):
        return pltpu.make_async_remote_copy(
            src_ref=src.at[pl.ds(tok - SUB, SUB)], dst_ref=dst,
            send_sem=rim_send.at[index], recv_sem=rim_recv.at[index],
            device_id=(after, core), device_id_type=MESH,
        )

    rims = [rim_copy(0, k_hbm, rim_k), rim_copy(1, v_hbm, rim_v), rim_copy(2, q_hbm, rim_q)]
    e_buf[spot] = at(e_loc, spot * part, part)[...]

    begins = rows == 0
    for end in ends:
        begins = begins | (rows == end)
    keep_m[...] = jnp.where(begins, 0.0, 1.0)
    for t in range(tiles):
        taps_t[0, t * SUB : t * SUB + taps, :] = sf_in[0, :, t * LANES : (t + 1) * LANES]
    params[2].wait()
    params[3].wait()
    for t in range(tiles):
        x = -2.0 * rate_n[t * modes : (t + 1) * modes, :]
        series = 1.0 + x * (1.0 / 6.0)
        for n in (5.0, 4.0, 3.0, 2.0):
            series = 1.0 + x * (1.0 / n) * series
        coef_n[t * modes : (t + 1) * modes, :] = residue_in[:, t * LANES : (t + 1) * LANES] * jnp.sqrt(-x * series)

    @pl.loop(0, groups)
    def _(g):
        load(0, q_hbm, q_in, g).wait()
        relayout(q_in, xq, g)

    rising = (lax.broadcasted_iota(jnp.int32, (SUB, LANES), 0) + 1).astype(F32)

    @pl.loop(0, tiles)
    def _(t):
        for m in range(modes):
            rate = rate_n[pl.ds(t * modes + m, 1), :]
            coef = coef_n[pl.ds(t * modes + m, 1), :]
            here = pl.ds(pl.multiple_of((t * modes + m) * SUB, SUB), SUB)
            weights[here, :] = coef * jnp.exp(-rate * rising)
        whole = pl.ds(pl.multiple_of(t * modes, SUB), modes)
        dec8_n[whole, :] = jnp.exp(rate_n[whole, :] * float(-SUB))

    def tree(terms):
        while len(terms) > 1:
            terms = [a + b for a, b in zip(terms[::2], terms[1::2])]
        return terms[0]

    def conv_block(block, g, q_win, state, q_taps, decay, coef, z_of):
        q_win, state = list(q_win), list(state)
        for s in range(SUB):
            q_win.append(token(xq, block, g, s))
            qs = fir(q_win[-taps:], q_taps)
            t = (block - 1) * SUB + s
            z = z_of(t, s)
            keep = keep_m[pl.ds(t, 1), :]
            state = [(d * keep) * old + z for d, old in zip(decay, state)]
            out = tree([c * part for c, part in zip(coef, state)])
            there = pl.ds(row_of(block - 1, g * SUB) + s, SUB, stride=SUB)
            conv_std[there, :] = out * qs
            qs_std[there, :] = qs * carry_m[pl.ds(t, 1), :]
        return q_win[1 - taps :], state

    behind = range(SUB - taps + 1, SUB)

    def inner(g):
        q_taps = taps_of(0, g)
        decay = [per_mode(dec_n, g, m) for m in range(modes)]
        coef = [per_mode(coef_n, g, m) for m in range(modes)]

        def step(block, carried):
            return conv_block(block, g, *carried, q_taps, decay, coef, lambda t, s: zs[z_rows(t, g), :])

        lax.fori_loop(2, blocks + 1, step, ([token(xq, 1, g, s) for s in behind], [zero] * modes))

    def head(g):
        windows = [[token(x, 0, g, s) for s in behind] for x in (xk, xv)]
        weight = [taps_of(1, g), taps_of(2, g)]

        def z_of(t, s):
            for window, x in zip(windows, (xk, xv)):
                window.append(token(x, 1, g, s))
            return fir(windows[0][-taps:], weight[0]) * fir(windows[1][-taps:], weight[1])

        decay = [per_mode(dec_n, g, m) for m in range(modes)]
        coef = [per_mode(coef_n, g, m) for m in range(modes)]
        _, state = conv_block(
            1, g, [token(xq, 0, g, s) for s in behind], [zero] * modes, taps_of(0, g), decay, coef, z_of
        )
        for m in range(modes):
            head_n[pl.ds(g * SUB * modes + m, SUB, stride=modes), :] = state[m]

    inner(0)

    per = tiles // PLANE
    my_rate = at(rate_n, spot * part, part)[...]
    for i in range(SUB):
        source = pl.multiple_of((spot * per + i % per) * SUB, SUB)
        dec_own[i * SUB : (i + 1) * SUB, :] = dec_n[pl.ds(source, SUB), :]
        for a in (1, 2):
            taps_own[a - 1, i * SUB : (i + 1) * SUB, :] = taps_t[a, pl.ds(source, SUB), :]
    own_decay = [dec_own[pl.ds(m, SUB, stride=modes), :] for m in range(modes)]
    own_taps = [[taps_own[a, pl.ds(j, SUB, stride=SUB), :] for j in range(taps)] for a in range(2)]

    @pl.loop(1, PLANE)
    def _(step):
        source = lax.rem(spot + step, PLANE)
        edge_copy(source, source, zed, 0).wait_recv()

    @pl.when(zed > 0)
    def _():
        edge_copy(spot, PLANE, zed, 1).wait_recv()

    for j in range(PLANE):
        for a, dst in ((0, ek), (1, ev)):
            past = edges[(j + PLANE) % (PLANE + 1), a].astype(F32)
            here = edges[j, a + 2].astype(F32)
            for i in range(per):
                tile = j * per + i
                dst[row_of(0, tile) : row_of(0, tile) + SUB, :] = past[:, i * LANES : (i + 1) * LANES]
                dst[row_of(1, tile) : row_of(1, tile) + SUB, :] = here[:, i * LANES : (i + 1) * LANES]

    for g in range(groups):
        shard = zed * PLANE + (lax.broadcasted_iota(jnp.int32, (SUB, LANES), 0) + g * SUB) // per
        begin = shard * tok
        latest = jnp.full((SUB, LANES), -1, jnp.int32)
        for end in ends:
            latest = jnp.maximum(latest, jnp.where(end <= begin + (tok - 1), end, -1))
        window = [[token(x, 0, g, s) for s in range(SUB - taps + 1, SUB)] for x in (ek, ev)]
        state = [zero] * modes
        for s in range(SUB):
            window[0].append(token(ek, 1, g, s))
            window[1].append(token(ev, 1, g, s))
            z = fir(window[0][-taps:], own_taps[0]) * fir(window[1][-taps:], own_taps[1])
            z = jnp.where(begin + s >= latest, z, 0.0)
            state = [d * old + z for d, old in zip(own_decay, state)]
        for m in range(modes):
            e_first[pl.ds(g * SUB * modes + m, SUB, stride=modes), :] = state[m]

    @pl.loop(1, PLANE)
    def _(step):
        arrival_1(lax.rem(spot + step, PLANE)).wait_recv()

    span = jnp.exp(my_rate * float(-tok))
    spot_rows = lax.broadcasted_iota(jnp.int32, (PLANE, LANES), 0) + zed * PLANE
    plane_rows = lax.broadcasted_iota(jnp.int32, (SUB, LANES), 0)
    open_here = jnp.ones((PLANE, LANES), F32)
    open_plane = jnp.ones((SUB, LANES), F32)
    for end in ends:
        open_here = jnp.where(spot_rows == end // tok, 0.0, open_here)
        open_plane = jnp.where(plane_rows == end // (tok * PLANE), 0.0, open_plane)

    rest = jnp.exp(my_rate * float(SUB - tok))
    state = jnp.zeros_like(span)
    reach = jnp.ones_like(span)
    for other in range(PLANE):
        pre_buf[other] = state
        reach_buf[other] = reach
        factor = span * open_here[other : other + 1]
        state = factor * state + e_buf[other] + rest * e_first[other * part : (other + 1) * part, :]
        reach = factor * reach
    total_buf[...] = state

    def round_2(there, slot):
        return pltpu.make_async_remote_copy(
            src_ref=total_buf, dst_ref=plane_buf.at[slot],
            send_sem=s2.at[there], recv_sem=r2.at[slot],
            device_id=(there * PLANE + spot, core), device_id_type=MESH,
        )

    @pl.loop(zed + 1, planes)
    def _(there):
        round_2(there, zed).start()

    for copy in rims:
        copy.start()

    @pl.loop(1, groups - 1)
    def _(g):
        inner(g)

    plane_span = jnp.exp(my_rate * float(-tok * PLANE))

    def plane_step(there, state):
        round_2(there, there).wait_recv()
        row = jnp.sum(jnp.where(plane_rows == there, open_plane, 0.0), axis=0, keepdims=True)
        return plane_span * row * state + plane_buf[there]

    state = lax.fori_loop(0, zed, plane_step, jnp.zeros_like(span))
    def round_3(other, slot):
        return pltpu.make_async_remote_copy(
            src_ref=pre_buf.at[other], dst_ref=inc_buf.at[slot],
            send_sem=s3.at[other], recv_sem=r3.at[slot],
            device_id=(zed * PLANE + other, core), device_id_type=MESH,
        )

    @pl.loop(1, PLANE)
    def _(step):
        other = nth_of(PLANE - step)
        pre_buf[other] = pre_buf[other] + reach_buf[other] * state
        round_3(other, spot).start()

    inc_buf[spot] = pre_buf[spot] + reach_buf[spot] * state

    inner(groups - 1)

    for copy in rims:
        copy.wait_recv()
    relayout_rim(rim_k, xk)
    relayout_rim(rim_v, xv)
    relayout_rim(rim_q, xq)

    @pl.loop(0, groups)
    def _(g):
        head(g)

    for g in range(groups):
        load(3, r_hbm, r_in, g).wait()

    @pl.loop(0, tiles)
    def _(t):
        cols = pl.ds(pl.multiple_of(t * LANES, LANES), LANES)
        for pair in range(pairs):
            x = r_in[pair * 2 * SUB : (pair + 1) * 2 * SUB, cols].astype(F32)
            for half in range(2):
                here = pl.ds(pl.multiple_of(row_of(2 * pair + half, t), SUB), SUB)
                conv_std[here, :] = conv_std[here, :] + x[half * SUB : (half + 1) * SUB]

    sq_loc[...] = jnp.zeros_like(sq_loc)


    def tile_of(slot, local):
        t = slot * per + local
        whole = pl.ds(pl.multiple_of(t * modes, SUB), modes)
        incoming = inc_buf[slot, local * modes : (local + 1) * modes, :]
        at_8 = dec8_n[whole, :] * carry_m[SUB - 1 : SUB, :] * incoming + head_n[whole, :]
        value, later, decay = [], [], []
        for m in range(modes):
            here = pl.ds(pl.multiple_of((t * modes + m) * SUB, SUB), SUB)
            weight = weights[here, :]
            value.append(weight * incoming[m : m + 1])
            later.append(weight * at_8[m : m + 1])
            decay.append(jnp.broadcast_to(dec8_n[pl.ds(t * modes + m, 1), :], (SUB, LANES)))
        cols = pl.ds(pl.multiple_of(t * LANES, LANES), LANES)
        for pair in range(pairs):
            halves = []
            for block in (2 * pair, 2 * pair + 1):
                carried = tree(value)
                if block == 0:
                    value = later
                elif block < blocks - 1:
                    value = [v * d for v, d in zip(value, decay)]
                here = pl.ds(pl.multiple_of(row_of(block, t), SUB), SUB)
                halves.append(conv_std[here, :] + qs_std[here, :] * carried)
            both = pl.ds(pair * 2 * SUB, 2 * SUB)
            stream = jnp.concatenate(halves, axis=0).astype(jnp.bfloat16)
            stream_ref[both, cols] = stream
            back = stream.astype(F32)
            sq_loc[both, :] = sq_loc[both, :] + back * back

    @pl.loop(0, PLANE)
    def _(n):
        slot = nth_of(n)

        @pl.when(n > 0)
        def _():
            round_3(slot, slot).wait_recv()

        for local in range(per):
            tile_of(slot, local)

    swap = pltpu.make_async_remote_copy(
        src_ref=sq_loc, dst_ref=sq_far, send_sem=sq_send, recv_sem=sq_recv,
        device_id=(me, 1 - core), device_id_type=MESH,
    )
    swap.start()

    for copy in rims:
        copy.wait_send()

    @pl.loop(1, PLANE)
    def _(step):
        other = lax.rem(spot + step, PLANE)
        round_1(other).wait_send()
        round_3(other, spot).wait_send()
        edge_copy(other, spot, zed, 0).wait_send()

    @pl.when(crosses)
    def _():
        @pl.loop(0, PLANE)
        def _(owner):
            edge_copy(owner, PLANE, zed + 1, 1).wait_send()

    @pl.loop(zed + 1, planes)
    def _(there):
        round_2(there, zed).wait_send()

    swap.wait()
    total = jnp.sum(sq_loc[...] + sq_far[...], axis=1, keepdims=True)
    scale = lax.rsqrt(total * (1.0 / (2 * chans)) + 1e-6)
    scale_ref[...] = jnp.broadcast_to(scale, (tok, LANES))


def finish(tok, chans, stream_ref, scale_ref, gain_ref, stream_hbm, normed_hbm, normed, sem):
    wide = SUB * LANES
    groups = chans // wide
    copies = [pltpu.make_async_copy(stream_ref, stream_hbm, sem.at[groups])]
    copies[0].start()
    scales = [scale_ref[pair * 2 * SUB : (pair + 1) * 2 * SUB, :] for pair in range(tok // (2 * SUB))]
    for g in range(groups):
        @pl.loop(g * SUB, (g + 1) * SUB)
        def _(t):
            cols = pl.ds(pl.multiple_of(t * LANES, LANES), LANES)
            gain = gain_ref[pl.ds(t, 1), :]
            for pair, scale in enumerate(scales):
                both = slice(pair * 2 * SUB, (pair + 1) * 2 * SUB)
                x = stream_ref[both, cols].astype(F32)
                normed[both, cols] = (x * scale * gain).astype(jnp.bfloat16)

        part = slice(g * wide, (g + 1) * wide)
        copy = pltpu.make_async_copy(normed.at[:, part], normed_hbm.at[:, part], sem.at[g])
        copy.start()
        copies.append(copy)
    for copy in copies:
        copy.wait()


def body(q_proj, k_proj, v_proj, resid, short_filter, residue, rate, gain, seg_lengths):
    tok, chans = q_proj.shape
    taps = short_filter.shape[1]
    modes = rate.shape[0]
    segs = seg_lengths.shape[0]
    shards = lax.axis_size("seq")
    planes = shards // PLANE
    tiles = chans // LANES
    groups = tiles // SUB
    blocks = tok // SUB
    part = tiles * modes // PLANE
    bf16 = jnp.bfloat16
    dims = (shards, planes, tok, chans, modes, taps, segs)
    vmem = pltpu.VMEM
    sem = pltpu.SemaphoreType.DMA
    hbm_spec = pl.BlockSpec(memory_space=pltpu.HBM)
    stream, scale, gain = pl.pallas_call(
        functools.partial(kernel, dims),
        out_shape=(
            jax.ShapeDtypeStruct((tok, chans), bf16),
            jax.ShapeDtypeStruct((tok, LANES), F32),
            jax.ShapeDtypeStruct((tiles, LANES), F32),
        ),
        in_specs=[hbm_spec] * 9,
        out_specs=(pl.BlockSpec(memory_space=vmem),) * 3,
        scratch_shapes=[
            vmem((tok, chans), bf16), vmem((tok, chans), bf16), vmem((tok, chans), bf16), vmem((tok, chans), bf16),
            vmem((3, taps, chans), F32), vmem((modes, chans), F32), vmem((modes, chans), F32),
            pltpu.SMEM((segs,), jnp.int32),
            vmem((SUB, chans), bf16), vmem((SUB, chans), bf16), vmem((SUB, chans), bf16),
            vmem((PLANE, 4, SUB, chans // PLANE), bf16), vmem((PLANE + 1, 4, SUB, chans // PLANE), bf16),
            vmem((2 * tiles * SUB, LANES), F32), vmem((2 * tiles * SUB, LANES), F32),
            vmem((tiles * modes, LANES), F32), vmem((tiles * modes, LANES), F32),
            vmem((SUB * modes, LANES), F32), vmem((2, SUB * SUB, LANES), F32),
            vmem(((blocks + 1) * tiles * SUB, LANES), F32),
            vmem(((blocks + 1) * tiles * SUB, LANES), F32),
            vmem(((blocks + 1) * tiles * SUB, LANES), F32),
            vmem((blocks * tiles * SUB, LANES), F32),
            vmem((blocks * tiles * SUB, LANES), F32),
            vmem((blocks * tiles * SUB, LANES), F32),
            vmem((3, tiles * SUB, LANES), F32),
            vmem((tiles * modes, LANES), F32), vmem((tiles * modes, LANES), F32), vmem((tiles * modes, LANES), F32),
            vmem((tiles * modes * SUB, LANES), F32), vmem((tiles * modes, LANES), F32),
            vmem((tok, LANES), F32), vmem((tok, LANES), F32), vmem((tok, LANES), F32),
            vmem((tiles * modes, LANES), F32),
            vmem((PLANE, part, LANES), F32), vmem((PLANE, part, LANES), F32), vmem((PLANE, part, LANES), F32),
            vmem((part, LANES), F32), vmem((planes, part, LANES), F32), vmem((PLANE, part, LANES), F32),
            vmem((tok, LANES), F32), vmem((tok, LANES), F32),
            sem((4, groups)), sem((5,)), sem((3,)), sem((3,)), sem((2, PLANE)), sem((PLANE + 1,)),
            sem((PLANE,)), sem((PLANE,)), sem((planes,)), sem((planes,)), sem((PLANE,)), sem((PLANE,)),
            sem, sem,
        ],
        compiler_params=pltpu.CompilerParams(
            collective_id=0, has_side_effects=True, vmem_limit_bytes=40 * 1024 * 1024
        ),
        name="hyena",
    )(*(pltpu.with_memory_space_constraint(x, pltpu.HBM) for x in (
        q_proj, k_proj, v_proj, resid, short_filter, residue, rate, gain.reshape(tiles, LANES), seg_lengths
    )))
    return pl.pallas_call(
        functools.partial(finish, tok, chans),
        out_shape=(jax.ShapeDtypeStruct((tok, chans), bf16),) * 2,
        in_specs=[pl.BlockSpec(memory_space=vmem)] * 3,
        out_specs=(hbm_spec,) * 2,
        scratch_shapes=[vmem((tok, chans), bf16), sem((chans // (SUB * LANES) + 1,))],
        compiler_params=pltpu.CompilerParams(vmem_limit_bytes=16 * 1024 * 1024),
        name="finish",
    )(stream, scale, gain)


def solution(mesh):
    placed = (
        P("seq", "chan"),
        P("seq", "chan"),
        P("seq", "chan"),
        P("seq", "chan"),
        P(None, None, "chan"),
        P(None, "chan"),
        P(None, "chan"),
        P("chan"),
        P(),
    )
    return jax.shard_map(
        body,
        mesh=mesh,
        in_specs=placed,
        out_specs=(P("seq", "chan"), P("seq", "chan")),
        check_vma=False,
    )
```

```python
import functools
import jax
import jax.numpy as jnp
from jax import lax
from jax.experimental import pallas as pl
from jax.experimental.pallas import tpu as pltpu
from jax.sharding import PartitionSpec as P

MESH = pl.DeviceIdType.MESH
PLANE = 16
LANES = 128
SUB = 8
F32 = jnp.float32


def kernel(
    dims,
    q_hbm, k_hbm, v_hbm, r_hbm, sf_hbm, residue_hbm, rate_hbm, gain_hbm, seg_hbm,
    stream_ref, scale_ref, gain_in,
    q_in, k_in, v_in, r_in, sf_in, residue_in, rate_in, seg_ref,
    rim_q, rim_k, rim_v, edge, edges, ek, ev, e_first, head_n, dec_own, taps_own,
    xq, xk, xv, zs, conv_std, qs_std,
    taps_t, rate_n, coef_n, dec_n, weights, dec8_n,
    keep_m, last_m, carry_m,
    e_loc, e_buf, pre_buf, reach_buf, total_buf, plane_buf, inc_buf, sq_loc, sq_far,
    in_sem, param_sem, rim_send, rim_recv, edge_send, edge_recv, s1, r1, s2, r2, s3, r3, sq_send, sq_recv,
):
    shards, planes, tok, chans, modes, taps, segs = dims
    blocks = tok // SUB
    pairs = blocks // 2
    tiles = chans // LANES
    groups = tiles // SUB
    wide = SUB * LANES
    part = tiles * modes // PLANE
    me = lax.axis_index("seq")
    core = lax.axis_index("chan")
    zed = me // PLANE
    spot = lax.rem(me, PLANE)
    after = lax.rem(me + 1, shards)
    before = lax.rem(me + shards - 1, shards)

    def at(ref, start, size):
        return ref.at[pl.ds(pl.multiple_of(start, SUB), size)]

    side = 4

    def nth(i, j):
        near = lambda n: (n * (n + 1) // 2) % side
        y = lax.rem(spot // side + near(i), side)
        x = lax.rem(spot + near(j), side)
        return y * side + x

    def nth_of(n):
        return nth(n // side, lax.rem(n, side))

    barrier = pltpu.get_barrier_semaphore()

    @pl.loop(1, PLANE)
    def _(step):
        other = zed * PLANE + nth_of(PLANE - step)
        pl.semaphore_signal(barrier, inc=1, device_id=(other, core), device_id_type=MESH)

    @pl.loop(1, planes)
    def _(step):
        other = lax.rem(zed + step, planes) * PLANE + spot
        pl.semaphore_signal(barrier, inc=1, device_id=(other, core), device_id_type=MESH)

    @pl.when(zed > 0)
    def _():
        last = (zed - 1) * PLANE + PLANE - 1
        pl.semaphore_signal(barrier, inc=1, device_id=(last, core), device_id_type=MESH)

    pl.semaphore_signal(barrier, inc=1, device_id=(before, core), device_id_type=MESH)
    pl.semaphore_signal(barrier, inc=1, device_id=(me, 1 - core), device_id_type=MESH)

    params = [
        pltpu.make_async_copy(rate_hbm, rate_in, param_sem.at[0]),
        pltpu.make_async_copy(sf_hbm, sf_in, param_sem.at[1]),
        pltpu.make_async_copy(residue_hbm, residue_in, param_sem.at[2]),
        pltpu.make_async_copy(gain_hbm, gain_in, param_sem.at[3]),
        pltpu.make_async_copy(seg_hbm, seg_ref, param_sem.at[4]),
    ]

    def load(index, src, dst, g):
        cols = pl.ds(g * wide, wide)
        return pltpu.make_async_copy(src.at[:, cols], dst.at[:, cols], in_sem.at[index, g])

    for index in (4, 0, 1):
        params[index].start()
    for g in range(groups):
        load(1, k_hbm, k_in, g).start()
        load(2, v_hbm, v_in, g).start()
    params[4].wait()
    first = me * tok
    ends = []
    running = seg_ref[0]
    ends.append(running)
    for j in range(1, segs):
        running = running + seg_ref[j]
        ends.append(running)
    big = jnp.int32(1 << 30)
    low = big
    low8 = big
    high = jnp.int32(-1)
    for end in ends:
        low = jnp.minimum(low, jnp.where(end >= first, end, big))
        low8 = jnp.minimum(low8, jnp.where(end >= first + SUB, end, big))
        high = jnp.maximum(high, jnp.where(end <= first + tok - 1, end, -1))
    rows = lax.broadcasted_iota(jnp.int32, (tok, LANES), 0) + first
    last_m[...] = jnp.where(rows >= high, 1.0, 0.0)
    carry_m[...] = jnp.where(rows < low8, 1.0, 0.0)
    carry_m[:SUB, :] = jnp.where(rows[:SUB] < low, 1.0, 0.0)

    params[0].wait()
    for t in range(tiles):
        rate = rate_in[:, t * LANES : (t + 1) * LANES]
        rate_n[t * modes : (t + 1) * modes, :] = rate
        dec_n[t * modes : (t + 1) * modes, :] = jnp.exp(-rate)
    params[1].wait()
    for a in (1, 2):
        for t in range(tiles):
            taps_t[a, t * SUB : t * SUB + taps, :] = sf_in[a, :, t * LANES : (t + 1) * LANES]

    def row_of(block, tile):
        return (block * tiles + tile) * SUB

    def relayout_tile(src, dst, g, pair, j):
        x = src[pl.ds(pl.multiple_of(pair * 2 * SUB, 2 * SUB), 2 * SUB),
                pl.ds(pl.multiple_of(g * wide + j * LANES, LANES), LANES)].astype(F32)
        lower = pl.multiple_of(row_of(2 * pair + 1, g * SUB + j), SUB)
        dst[pl.ds(lower, SUB), :] = x[:SUB]
        upper = pl.multiple_of(row_of(2 * pair + 2, g * SUB + j), SUB)
        dst[pl.ds(upper, SUB), :] = x[SUB:]

    def relayout(src, dst, g):
        @pl.loop(0, pairs)
        def _(pair):
            for j in range(SUB):
                relayout_tile(src, dst, g, pair, j)

    def relayout_rim(src, dst):
        for t in range(tiles):
            x = src[:, t * LANES : (t + 1) * LANES].astype(F32)
            dst[t * SUB : (t + 1) * SUB, :] = jnp.where(me > 0, x, 0.0)

    def token(ref, block, g, s):
        return ref[pl.ds(row_of(block, g * SUB) + s, SUB, stride=SUB), :]

    def per_mode(ref, g, m):
        return ref[pl.ds(g * SUB * modes + m, SUB, stride=modes), :]

    def taps_of(a, g):
        return [taps_t[a, pl.ds(g * SUB * SUB + j, SUB, stride=SUB), :] for j in range(taps)]

    def fir(window, weight):
        out = weight[0] * window[-1]
        for j in range(1, taps):
            out = out + weight[j] * window[-1 - j]
        return out

    def z_rows(t, g):
        return pl.ds(pl.multiple_of((t * groups + g) * SUB, SUB), SUB)

    def block_of_z(block, g, k_win, v_win, state, k_taps, v_taps, decay, beside=None):
        k_win, v_win, state = list(k_win), list(v_win), list(state)
        for s in range(SUB):
            if beside is not None:
                beside(s)
            k_win.append(token(xk, block, g, s))
            v_win.append(token(xv, block, g, s))
            z = fir(k_win[-taps:], k_taps) * fir(v_win[-taps:], v_taps)
            t = (block - 1) * SUB + s
            zs[z_rows(t, g), :] = z
            z = z * last_m[pl.ds(t, 1), :]
            state = [d * old + z for d, old in zip(decay, state)]
        return k_win[1 - taps :], v_win[1 - taps :], state

    zero = jnp.zeros((SUB, LANES), F32)

    load(1, k_hbm, k_in, 0).wait()
    load(2, v_hbm, v_in, 0).wait()
    for j in range(SUB):
        relayout_tile(k_in, xk, 0, 0, j)
        relayout_tile(v_in, xv, 0, 0, j)

    def end_states(g):
        k_taps, v_taps = taps_of(1, g), taps_of(2, g)
        decay = [per_mode(dec_n, g, m) for m in range(modes)]
        behind = range(SUB - taps + 1, SUB)

        def ahead(pair, half):
            after_it = jnp.minimum(g * pairs + pair + 1, groups * pairs - 1)
            g_next, pair_next = after_it // pairs, lax.rem(after_it, pairs)

            def one(s):
                src, dst = ((k_in, xk), (v_in, xv))[s % 2]
                if half is None:
                    relayout_tile(k_in, xk, g_next, pair_next, s)
                    relayout_tile(v_in, xv, g_next, pair_next, s)
                else:
                    relayout_tile(src, dst, g_next, pair_next, half * SUB // 2 + s // 2)

            return one

        start = block_of_z(
            2, g, [token(xk, 1, g, s) for s in behind], [token(xv, 1, g, s) for s in behind],
            [zero] * modes, k_taps, v_taps, decay, ahead(0, None),
        )

        def step(pair, carried):
            for half in range(2):
                carried = block_of_z(
                    2 * pair + 1 + half, g, *carried, k_taps, v_taps, decay, ahead(pair, half)
                )
            return carried

        _, _, state = lax.fori_loop(1, pairs, step, start)
        for m in range(modes):
            e_loc[pl.ds(g * SUB * modes + m, SUB, stride=modes), :] = state[m]

    @pl.loop(0, groups // 2)
    def _(g):
        load(1, k_hbm, k_in, g + 1).wait()
        load(2, v_hbm, v_in, g + 1).wait()
        end_states(g)

    for g in range(groups // 2 + 1, groups):
        load(1, k_hbm, k_in, g).wait()
        load(2, v_hbm, v_in, g).wait()
    for index in (2, 3):
        params[index].start()
    for g in range(groups):
        load(0, q_hbm, q_in, g).start()
    for g in range(groups):
        load(3, r_hbm, r_in, g).start()

    owned = chans // PLANE
    for owner in range(PLANE):
        cols = slice(owner * owned, (owner + 1) * owned)
        edge[owner, 0] = k_in[tok - SUB : tok, cols]
        edge[owner, 1] = v_in[tok - SUB : tok, cols]
        edge[owner, 2] = k_in[0:SUB, cols]
        edge[owner, 3] = v_in[0:SUB, cols]

    crossing = ((spot + 1) // PLANE) * ((2 * planes - 3 - zed) // (planes - 1))
    crosses = crossing > 0
    pl.semaphore_wait(barrier, PLANE - 1 + planes - 1 + 2 + PLANE * crossing)

    def edge_copy(owner, slot, plane, kind):
        return pltpu.make_async_remote_copy(
            src_ref=edge.at[owner], dst_ref=edges.at[slot],
            send_sem=edge_send.at[kind, owner], recv_sem=edge_recv.at[slot],
            device_id=(plane * PLANE + owner, core), device_id_type=MESH,
        )

    @pl.loop(1, PLANE)
    def _(step):
        edge_copy(nth_of(PLANE - step), spot, zed, 0).start()

    @pl.when(crosses)
    def _():
        @pl.loop(0, PLANE)
        def _(owner):
            edge_copy(owner, PLANE, zed + 1, 1).start()

    edges[spot] = edge[spot]

    @pl.when(zed == 0)
    def _():
        edges[PLANE] = jnp.zeros_like(edges[PLANE])

    @pl.loop(groups // 2, groups)
    def _(g):
        end_states(g)

    def round_1(other):
        return pltpu.make_async_remote_copy(
            src_ref=at(e_loc, other * part, part), dst_ref=e_buf.at[spot],
            send_sem=s1.at[other], recv_sem=r1.at[spot],
            device_id=(zed * PLANE + other, core), device_id_type=MESH,
        )

    def arrival_1(other):
        return pltpu.make_async_remote_copy(
            src_ref=at(e_loc, other * part, part), dst_ref=e_buf.at[other],
            send_sem=s1.at[other], recv_sem=r1.at[other],
            device_id=(zed * PLANE + other, core), device_id_type=MESH,
        )

    @pl.loop(1, PLANE)
    def _(step):
        round_1(nth_of(PLANE - step)).start()

    def rim_copy(index, src, dst):
        return pltpu.make_async_remote_copy(
            src_ref=src.at[pl.ds(tok - SUB, SUB)], dst_ref=dst,
            send_sem=rim_send.at[index], recv_sem=rim_recv.at[index],
            device_id=(after, core), device_id_type=MESH,
        )

    rims = [rim_copy(0, k_hbm, rim_k), rim_copy(1, v_hbm, rim_v), rim_copy(2, q_hbm, rim_q)]
    for copy in rims:
        copy.start()

    e_buf[spot] = at(e_loc, spot * part, part)[...]

    begins = rows == 0
    for end in ends:
        begins = begins | (rows == end)
    keep_m[...] = jnp.where(begins, 0.0, 1.0)
    for t in range(tiles):
        taps_t[0, t * SUB : t * SUB + taps, :] = sf_in[0, :, t * LANES : (t + 1) * LANES]
    params[2].wait()
    params[3].wait()
    for t in range(tiles):
        x = -2.0 * rate_n[t * modes : (t + 1) * modes, :]
        series = 1.0 + x * (1.0 / 6.0)
        for n in (5.0, 4.0, 3.0, 2.0):
            series = 1.0 + x * (1.0 / n) * series
        coef_n[t * modes : (t + 1) * modes, :] = residue_in[:, t * LANES : (t + 1) * LANES] * jnp.sqrt(-x * series)

    @pl.loop(0, groups)
    def _(g):
        load(0, q_hbm, q_in, g).wait()
        relayout(q_in, xq, g)

    rising = (lax.broadcasted_iota(jnp.int32, (SUB, LANES), 0) + 1).astype(F32)

    @pl.loop(0, tiles)
    def _(t):
        for m in range(modes):
            rate = rate_n[pl.ds(t * modes + m, 1), :]
            coef = coef_n[pl.ds(t * modes + m, 1), :]
            here = pl.ds(pl.multiple_of((t * modes + m) * SUB, SUB), SUB)
            weights[here, :] = coef * jnp.exp(-rate * rising)
        whole = pl.ds(pl.multiple_of(t * modes, SUB), modes)
        dec8_n[whole, :] = jnp.exp(rate_n[whole, :] * float(-SUB))

    def tree(terms):
        while len(terms) > 1:
            terms = [a + b for a, b in zip(terms[::2], terms[1::2])]
        return terms[0]

    def conv_block(block, g, q_win, state, q_taps, decay, coef, z_of):
        q_win, state = list(q_win), list(state)
        for s in range(SUB):
            q_win.append(token(xq, block, g, s))
            qs = fir(q_win[-taps:], q_taps)
            t = (block - 1) * SUB + s
            z = z_of(t, s)
            keep = keep_m[pl.ds(t, 1), :]
            state = [(d * keep) * old + z for d, old in zip(decay, state)]
            out = tree([c * part for c, part in zip(coef, state)])
            there = pl.ds(row_of(block - 1, g * SUB) + s, SUB, stride=SUB)
            conv_std[there, :] = out * qs
            qs_std[there, :] = qs * carry_m[pl.ds(t, 1), :]
        return q_win[1 - taps :], state

    behind = range(SUB - taps + 1, SUB)

    def inner(g):
        q_taps = taps_of(0, g)
        decay = [per_mode(dec_n, g, m) for m in range(modes)]
        coef = [per_mode(coef_n, g, m) for m in range(modes)]

        def step(block, carried):
            return conv_block(block, g, *carried, q_taps, decay, coef, lambda t, s: zs[z_rows(t, g), :])

        lax.fori_loop(2, blocks + 1, step, ([token(xq, 1, g, s) for s in behind], [zero] * modes))

    def head(g):
        windows = [[token(x, 0, g, s) for s in behind] for x in (xk, xv)]
        weight = [taps_of(1, g), taps_of(2, g)]

        def z_of(t, s):
            for window, x in zip(windows, (xk, xv)):
                window.append(token(x, 1, g, s))
            return fir(windows[0][-taps:], weight[0]) * fir(windows[1][-taps:], weight[1])

        decay = [per_mode(dec_n, g, m) for m in range(modes)]
        coef = [per_mode(coef_n, g, m) for m in range(modes)]
        _, state = conv_block(
            1, g, [token(xq, 0, g, s) for s in behind], [zero] * modes, taps_of(0, g), decay, coef, z_of
        )
        for m in range(modes):
            head_n[pl.ds(g * SUB * modes + m, SUB, stride=modes), :] = state[m]

    inner(0)

    per = tiles // PLANE
    my_rate = at(rate_n, spot * part, part)[...]
    for i in range(SUB):
        source = pl.multiple_of((spot * per + i % per) * SUB, SUB)
        dec_own[i * SUB : (i + 1) * SUB, :] = dec_n[pl.ds(source, SUB), :]
        for a in (1, 2):
            taps_own[a - 1, i * SUB : (i + 1) * SUB, :] = taps_t[a, pl.ds(source, SUB), :]
    own_decay = [dec_own[pl.ds(m, SUB, stride=modes), :] for m in range(modes)]
    own_taps = [[taps_own[a, pl.ds(j, SUB, stride=SUB), :] for j in range(taps)] for a in range(2)]

    @pl.loop(1, PLANE)
    def _(step):
        source = lax.rem(spot + step, PLANE)
        edge_copy(source, source, zed, 0).wait_recv()

    @pl.when(zed > 0)
    def _():
        edge_copy(spot, PLANE, zed, 1).wait_recv()

    for j in range(PLANE):
        for a, dst in ((0, ek), (1, ev)):
            past = edges[(j + PLANE) % (PLANE + 1), a].astype(F32)
            here = edges[j, a + 2].astype(F32)
            for i in range(per):
                tile = j * per + i
                dst[row_of(0, tile) : row_of(0, tile) + SUB, :] = past[:, i * LANES : (i + 1) * LANES]
                dst[row_of(1, tile) : row_of(1, tile) + SUB, :] = here[:, i * LANES : (i + 1) * LANES]

    for g in range(groups):
        shard = zed * PLANE + (lax.broadcasted_iota(jnp.int32, (SUB, LANES), 0) + g * SUB) // per
        begin = shard * tok
        latest = jnp.full((SUB, LANES), -1, jnp.int32)
        for end in ends:
            latest = jnp.maximum(latest, jnp.where(end <= begin + (tok - 1), end, -1))
        window = [[token(x, 0, g, s) for s in range(SUB - taps + 1, SUB)] for x in (ek, ev)]
        state = [zero] * modes
        for s in range(SUB):
            window[0].append(token(ek, 1, g, s))
            window[1].append(token(ev, 1, g, s))
            z = fir(window[0][-taps:], own_taps[0]) * fir(window[1][-taps:], own_taps[1])
            z = jnp.where(begin + s >= latest, z, 0.0)
            state = [d * old + z for d, old in zip(own_decay, state)]
        for m in range(modes):
            e_first[pl.ds(g * SUB * modes + m, SUB, stride=modes), :] = state[m]

    @pl.loop(1, PLANE)
    def _(step):
        arrival_1(lax.rem(spot + step, PLANE)).wait_recv()

    span = jnp.exp(my_rate * float(-tok))
    spot_rows = lax.broadcasted_iota(jnp.int32, (PLANE, LANES), 0) + zed * PLANE
    plane_rows = lax.broadcasted_iota(jnp.int32, (SUB, LANES), 0)
    open_here = jnp.ones((PLANE, LANES), F32)
    open_plane = jnp.ones((SUB, LANES), F32)
    for end in ends:
        open_here = jnp.where(spot_rows == end // tok, 0.0, open_here)
        open_plane = jnp.where(plane_rows == end // (tok * PLANE), 0.0, open_plane)

    rest = jnp.exp(my_rate * float(SUB - tok))
    state = jnp.zeros_like(span)
    reach = jnp.ones_like(span)
    for other in range(PLANE):
        pre_buf[other] = state
        reach_buf[other] = reach
        factor = span * open_here[other : other + 1]
        state = factor * state + e_buf[other] + rest * e_first[other * part : (other + 1) * part, :]
        reach = factor * reach
    total_buf[...] = state

    def round_2(there, slot):
        return pltpu.make_async_remote_copy(
            src_ref=total_buf, dst_ref=plane_buf.at[slot],
            send_sem=s2.at[there], recv_sem=r2.at[slot],
            device_id=(there * PLANE + spot, core), device_id_type=MESH,
        )

    @pl.loop(zed + 1, planes)
    def _(there):
        round_2(there, zed).start()

    @pl.loop(1, groups - 1)
    def _(g):
        inner(g)

    plane_span = jnp.exp(my_rate * float(-tok * PLANE))

    def plane_step(there, state):
        round_2(there, there).wait_recv()
        row = jnp.sum(jnp.where(plane_rows == there, open_plane, 0.0), axis=0, keepdims=True)
        return plane_span * row * state + plane_buf[there]

    state = lax.fori_loop(0, zed, plane_step, jnp.zeros_like(span))
    def round_3(other, slot):
        return pltpu.make_async_remote_copy(
            src_ref=pre_buf.at[other], dst_ref=inc_buf.at[slot],
            send_sem=s3.at[other], recv_sem=r3.at[slot],
            device_id=(zed * PLANE + other, core), device_id_type=MESH,
        )

    @pl.loop(1, PLANE)
    def _(step):
        other = nth_of(PLANE - step)
        pre_buf[other] = pre_buf[other] + reach_buf[other] * state
        round_3(other, spot).start()

    inc_buf[spot] = pre_buf[spot] + reach_buf[spot] * state

    inner(groups - 1)

    @pl.loop(1, PLANE)
    def _(step):
        other = lax.rem(spot + step, PLANE)
        round_1(other).wait_send()
        edge_copy(other, spot, zed, 0).wait_send()

    @pl.when(crosses)
    def _():
        @pl.loop(0, PLANE)
        def _(owner):
            edge_copy(owner, PLANE, zed + 1, 1).wait_send()

    @pl.loop(zed + 1, planes)
    def _(there):
        round_2(there, zed).wait_send()

    for copy in rims:
        copy.wait_recv()
    relayout_rim(rim_k, xk)
    relayout_rim(rim_v, xv)
    relayout_rim(rim_q, xq)

    @pl.loop(0, groups)
    def _(g):
        head(g)

    for g in range(groups):
        load(3, r_hbm, r_in, g).wait()

    @pl.loop(0, tiles)
    def _(t):
        cols = pl.ds(pl.multiple_of(t * LANES, LANES), LANES)
        for pair in range(pairs):
            x = r_in[pair * 2 * SUB : (pair + 1) * 2 * SUB, cols].astype(F32)
            for half in range(2):
                here = pl.ds(pl.multiple_of(row_of(2 * pair + half, t), SUB), SUB)
                conv_std[here, :] = conv_std[here, :] + x[half * SUB : (half + 1) * SUB]

    sq_loc[...] = jnp.zeros_like(sq_loc)


    def tile_of(slot, local):
        t = slot * per + local
        whole = pl.ds(pl.multiple_of(t * modes, SUB), modes)
        incoming = inc_buf[slot, local * modes : (local + 1) * modes, :]
        at_8 = dec8_n[whole, :] * carry_m[SUB - 1 : SUB, :] * incoming + head_n[whole, :]
        value, later, decay = [], [], []
        for m in range(modes):
            here = pl.ds(pl.multiple_of((t * modes + m) * SUB, SUB), SUB)
            weight = weights[here, :]
            value.append(weight * incoming[m : m + 1])
            later.append(weight * at_8[m : m + 1])
            decay.append(jnp.broadcast_to(dec8_n[pl.ds(t * modes + m, 1), :], (SUB, LANES)))
        cols = pl.ds(pl.multiple_of(t * LANES, LANES), LANES)
        for pair in range(pairs):
            halves = []
            for block in (2 * pair, 2 * pair + 1):
                carried = tree(value)
                if block == 0:
                    value = later
                elif block < blocks - 1:
                    value = [v * d for v, d in zip(value, decay)]
                here = pl.ds(pl.multiple_of(row_of(block, t), SUB), SUB)
                halves.append(conv_std[here, :] + qs_std[here, :] * carried)
            both = pl.ds(pair * 2 * SUB, 2 * SUB)
            stream = jnp.concatenate(halves, axis=0).astype(jnp.bfloat16)
            stream_ref[both, cols] = stream
            back = stream.astype(F32)
            sq_loc[both, :] = sq_loc[both, :] + back * back

    @pl.loop(0, PLANE)
    def _(n):
        slot = nth_of(n)

        @pl.when(n > 0)
        def _():
            round_3(slot, slot).wait_recv()

        for local in range(per):
            tile_of(slot, local)

    swap = pltpu.make_async_remote_copy(
        src_ref=sq_loc, dst_ref=sq_far, send_sem=sq_send, recv_sem=sq_recv,
        device_id=(me, 1 - core), device_id_type=MESH,
    )
    swap.start()

    for copy in rims:
        copy.wait_send()

    @pl.loop(1, PLANE)
    def _(step):
        other = lax.rem(spot + step, PLANE)
        round_3(other, spot).wait_send()

    swap.wait()
    total = jnp.sum(sq_loc[...] + sq_far[...], axis=1, keepdims=True)
    scale = lax.rsqrt(total * (1.0 / (2 * chans)) + 1e-6)
    scale_ref[...] = jnp.broadcast_to(scale, (tok, LANES))


def finish(tok, chans, stream_ref, scale_ref, gain_ref, stream_hbm, normed_hbm, normed, sem):
    wide = SUB * LANES
    groups = chans // wide
    copies = [pltpu.make_async_copy(stream_ref, stream_hbm, sem.at[groups])]
    copies[0].start()
    scales = [scale_ref[pair * 2 * SUB : (pair + 1) * 2 * SUB, :] for pair in range(tok // (2 * SUB))]
    for g in range(groups):
        @pl.loop(g * SUB, (g + 1) * SUB)
        def _(t):
            cols = pl.ds(pl.multiple_of(t * LANES, LANES), LANES)
            gain = gain_ref[pl.ds(t, 1), :]
            for pair, scale in enumerate(scales):
                both = slice(pair * 2 * SUB, (pair + 1) * 2 * SUB)
                x = stream_ref[both, cols].astype(F32)
                normed[both, cols] = (x * scale * gain).astype(jnp.bfloat16)

        part = slice(g * wide, (g + 1) * wide)
        copy = pltpu.make_async_copy(normed.at[:, part], normed_hbm.at[:, part], sem.at[g])
        copy.start()
        copies.append(copy)
    for copy in copies:
        copy.wait()


def body(q_proj, k_proj, v_proj, resid, short_filter, residue, rate, gain, seg_lengths):
    tok, chans = q_proj.shape
    taps = short_filter.shape[1]
    modes = rate.shape[0]
    segs = seg_lengths.shape[0]
    shards = lax.axis_size("seq")
    planes = shards // PLANE
    tiles = chans // LANES
    groups = tiles // SUB
    blocks = tok // SUB
    part = tiles * modes // PLANE
    bf16 = jnp.bfloat16
    dims = (shards, planes, tok, chans, modes, taps, segs)
    vmem = pltpu.VMEM
    sem = pltpu.SemaphoreType.DMA
    hbm_spec = pl.BlockSpec(memory_space=pltpu.HBM)
    stream, scale, gain = pl.pallas_call(
        functools.partial(kernel, dims),
        out_shape=(
            jax.ShapeDtypeStruct((tok, chans), bf16),
            jax.ShapeDtypeStruct((tok, LANES), F32),
            jax.ShapeDtypeStruct((tiles, LANES), F32),
        ),
        in_specs=[hbm_spec] * 9,
        out_specs=(pl.BlockSpec(memory_space=vmem),) * 3,
        scratch_shapes=[
            vmem((tok, chans), bf16), vmem((tok, chans), bf16), vmem((tok, chans), bf16), vmem((tok, chans), bf16),
            vmem((3, taps, chans), F32), vmem((modes, chans), F32), vmem((modes, chans), F32),
            pltpu.SMEM((segs,), jnp.int32),
            vmem((SUB, chans), bf16), vmem((SUB, chans), bf16), vmem((SUB, chans), bf16),
            vmem((PLANE, 4, SUB, chans // PLANE), bf16), vmem((PLANE + 1, 4, SUB, chans // PLANE), bf16),
            vmem((2 * tiles * SUB, LANES), F32), vmem((2 * tiles * SUB, LANES), F32),
            vmem((tiles * modes, LANES), F32), vmem((tiles * modes, LANES), F32),
            vmem((SUB * modes, LANES), F32), vmem((2, SUB * SUB, LANES), F32),
            vmem(((blocks + 1) * tiles * SUB, LANES), F32),
            vmem(((blocks + 1) * tiles * SUB, LANES), F32),
            vmem(((blocks + 1) * tiles * SUB, LANES), F32),
            vmem((blocks * tiles * SUB, LANES), F32),
            vmem((blocks * tiles * SUB, LANES), F32),
            vmem((blocks * tiles * SUB, LANES), F32),
            vmem((3, tiles * SUB, LANES), F32),
            vmem((tiles * modes, LANES), F32), vmem((tiles * modes, LANES), F32), vmem((tiles * modes, LANES), F32),
            vmem((tiles * modes * SUB, LANES), F32), vmem((tiles * modes, LANES), F32),
            vmem((tok, LANES), F32), vmem((tok, LANES), F32), vmem((tok, LANES), F32),
            vmem((tiles * modes, LANES), F32),
            vmem((PLANE, part, LANES), F32), vmem((PLANE, part, LANES), F32), vmem((PLANE, part, LANES), F32),
            vmem((part, LANES), F32), vmem((planes, part, LANES), F32), vmem((PLANE, part, LANES), F32),
            vmem((tok, LANES), F32), vmem((tok, LANES), F32),
            sem((4, groups)), sem((5,)), sem((3,)), sem((3,)), sem((2, PLANE)), sem((PLANE + 1,)),
            sem((PLANE,)), sem((PLANE,)), sem((planes,)), sem((planes,)), sem((PLANE,)), sem((PLANE,)),
            sem, sem,
        ],
        compiler_params=pltpu.CompilerParams(
            collective_id=0, has_side_effects=True, vmem_limit_bytes=40 * 1024 * 1024
        ),
        name="hyena",
    )(*(pltpu.with_memory_space_constraint(x, pltpu.HBM) for x in (
        q_proj, k_proj, v_proj, resid, short_filter, residue, rate, gain.reshape(tiles, LANES), seg_lengths
    )))
    return pl.pallas_call(
        functools.partial(finish, tok, chans),
        out_shape=(jax.ShapeDtypeStruct((tok, chans), bf16),) * 2,
        in_specs=[pl.BlockSpec(memory_space=vmem)] * 3,
        out_specs=(hbm_spec,) * 2,
        scratch_shapes=[vmem((tok, chans), bf16), sem((chans // (SUB * LANES) + 1,))],
        compiler_params=pltpu.CompilerParams(vmem_limit_bytes=16 * 1024 * 1024),
        name="finish",
    )(stream, scale, gain)


def solution(mesh):
    placed = (
        P("seq", "chan"),
        P("seq", "chan"),
        P("seq", "chan"),
        P("seq", "chan"),
        P(None, None, "chan"),
        P(None, "chan"),
        P(None, "chan"),
        P("chan"),
        P(),
    )
    return jax.shard_map(
        body,
        mesh=mesh,
        in_specs=placed,
        out_specs=(P("seq", "chan"), P("seq", "chan")),
        check_vma=False,
    )
```

```python
import functools
import jax
import jax.numpy as jnp
from jax import lax
from jax.experimental import pallas as pl
from jax.experimental.pallas import tpu as pltpu
from jax.sharding import PartitionSpec as P

MESH = pl.DeviceIdType.MESH
PLANE = 16
LANES = 128
SUB = 8
F32 = jnp.float32


def kernel(
    dims,
    q_hbm, k_hbm, v_hbm, r_hbm, sf_hbm, residue_hbm, rate_hbm, gain_hbm, seg_hbm,
    stream_ref, scale_ref, gain_in,
    q_in, k_in, v_in, r_in, sf_in, residue_in, rate_in, seg_ref,
    rim_q, rim_k, rim_v, edge, edges, ek, ev, e_first, head_n, dec_own, taps_own,
    xq, xk, xv, zs, conv_std, qs_std,
    taps_t, rate_n, coef_n, dec_n, weights, dec8_n,
    keep_m, last_m, carry_m,
    e_loc, e_out, e_buf, pre_buf, reach_buf, total_buf, plane_buf, inc_out, inc_buf, sq_loc, sq_far,
    in_sem, param_sem, rim_send, rim_recv, edge_send, edge_recv, s1, r1, s2, r2, s3, r3, sq_send, sq_recv,
):
    shards, planes, tok, chans, modes, taps, segs = dims
    blocks = tok // SUB
    pairs = blocks // 2
    tiles = chans // LANES
    groups = tiles // SUB
    wide = SUB * LANES
    part = tiles * modes // PLANE
    me = lax.axis_index("seq")
    core = lax.axis_index("chan")
    zed = me // PLANE
    spot = lax.rem(me, PLANE)
    after = lax.rem(me + 1, shards)
    before = lax.rem(me + shards - 1, shards)

    def at(ref, start, size):
        return ref.at[pl.ds(pl.multiple_of(start, SUB), size)]

    params = [
        pltpu.make_async_copy(rate_hbm, rate_in, param_sem.at[0]),
        pltpu.make_async_copy(sf_hbm, sf_in, param_sem.at[1]),
        pltpu.make_async_copy(residue_hbm, residue_in, param_sem.at[2]),
        pltpu.make_async_copy(gain_hbm, gain_in, param_sem.at[3]),
        pltpu.make_async_copy(seg_hbm, seg_ref, param_sem.at[4]),
    ]

    def load(index, src, dst, g):
        cols = pl.ds(g * wide, wide)
        return pltpu.make_async_copy(src.at[:, cols], dst.at[:, cols], in_sem.at[index, g])

    for index in (4, 0, 1):
        params[index].start()
    for g in range(groups):
        load(1, k_hbm, k_in, g).start()
        load(2, v_hbm, v_in, g).start()
    for index in (2, 3):
        params[index].start()
    for g in range(groups):
        load(0, q_hbm, q_in, g).start()
    for g in range(groups):
        load(3, r_hbm, r_in, g).start()

    barrier = pltpu.get_barrier_semaphore()

    @pl.loop(1, PLANE)
    def _(step):
        other = zed * PLANE + lax.rem(spot + step, PLANE)
        pl.semaphore_signal(barrier, inc=1, device_id=(other, core), device_id_type=MESH)

    @pl.loop(1, planes)
    def _(step):
        other = lax.rem(zed + step, planes) * PLANE + spot
        pl.semaphore_signal(barrier, inc=1, device_id=(other, core), device_id_type=MESH)

    @pl.when(zed > 0)
    def _():
        last = (zed - 1) * PLANE + PLANE - 1
        pl.semaphore_signal(barrier, inc=1, device_id=(last, core), device_id_type=MESH)

    @pl.when(me > 0)
    def _():
        pl.semaphore_signal(barrier, inc=1, device_id=(before, core), device_id_type=MESH)

    pl.semaphore_signal(barrier, inc=1, device_id=(me, 1 - core), device_id_type=MESH)

    params[4].wait()
    first = me * tok
    ends = []
    running = seg_ref[0]
    ends.append(running)
    for j in range(1, segs):
        running = running + seg_ref[j]
        ends.append(running)
    big = jnp.int32(1 << 30)
    low = big
    low8 = big
    high = jnp.int32(-1)
    for end in ends:
        low = jnp.minimum(low, jnp.where(end >= first, end, big))
        low8 = jnp.minimum(low8, jnp.where(end >= first + SUB, end, big))
        high = jnp.maximum(high, jnp.where(end <= first + tok - 1, end, -1))
    rows = lax.broadcasted_iota(jnp.int32, (tok, LANES), 0) + first
    last_m[...] = jnp.where(rows >= high, 1.0, 0.0)
    carry_m[...] = jnp.where(rows < low8, 1.0, 0.0)
    carry_m[:SUB, :] = jnp.where(rows[:SUB] < low, 1.0, 0.0)

    params[0].wait()
    for t in range(tiles):
        rate = rate_in[:, t * LANES : (t + 1) * LANES]
        rate_n[t * modes : (t + 1) * modes, :] = rate
        dec_n[t * modes : (t + 1) * modes, :] = jnp.exp(-rate)
    params[1].wait()
    for a in (1, 2):
        for t in range(tiles):
            taps_t[a, t * SUB : t * SUB + taps, :] = sf_in[a, :, t * LANES : (t + 1) * LANES]

    def row_of(block, tile):
        return (block * tiles + tile) * SUB

    def relayout_tile(src, dst, g, pair, j):
        x = src[pl.ds(pl.multiple_of(pair * 2 * SUB, 2 * SUB), 2 * SUB),
                pl.ds(pl.multiple_of(g * wide + j * LANES, LANES), LANES)].astype(F32)
        lower = pl.multiple_of(row_of(2 * pair + 1, g * SUB + j), SUB)
        dst[pl.ds(lower, SUB), :] = x[:SUB]
        upper = pl.multiple_of(row_of(2 * pair + 2, g * SUB + j), SUB)
        dst[pl.ds(upper, SUB), :] = x[SUB:]

    def relayout(src, dst, g):
        @pl.loop(0, pairs)
        def _(pair):
            for j in range(SUB):
                relayout_tile(src, dst, g, pair, j)

    def relayout_rim(src, dst):
        for t in range(tiles):
            x = src[:, t * LANES : (t + 1) * LANES].astype(F32)
            dst[t * SUB : (t + 1) * SUB, :] = jnp.where(me > 0, x, 0.0)

    def token(ref, block, g, s):
        return ref[pl.ds(row_of(block, g * SUB) + s, SUB, stride=SUB), :]

    def per_mode(ref, g, m):
        return ref[pl.ds(g * SUB * modes + m, SUB, stride=modes), :]

    def taps_of(a, g):
        return [taps_t[a, pl.ds(g * SUB * SUB + j, SUB, stride=SUB), :] for j in range(taps)]

    def fir(window, weight):
        out = weight[0] * window[-1]
        for j in range(1, taps):
            out = out + weight[j] * window[-1 - j]
        return out

    def z_rows(t, g):
        return pl.ds(pl.multiple_of((t * groups + g) * SUB, SUB), SUB)

    def block_of_z(block, g, k_win, v_win, state, k_taps, v_taps, decay, beside=None):
        k_win, v_win, state = list(k_win), list(v_win), list(state)
        for s in range(SUB):
            if beside is not None:
                beside(s)
            k_win.append(token(xk, block, g, s))
            v_win.append(token(xv, block, g, s))
            z = fir(k_win[-taps:], k_taps) * fir(v_win[-taps:], v_taps)
            t = (block - 1) * SUB + s
            zs[z_rows(t, g), :] = z
            z = z * last_m[pl.ds(t, 1), :]
            state = [d * old + z for d, old in zip(decay, state)]
        return k_win[1 - taps :], v_win[1 - taps :], state

    zero = jnp.zeros((SUB, LANES), F32)

    load(1, k_hbm, k_in, 0).wait()
    load(2, v_hbm, v_in, 0).wait()
    for j in range(SUB):
        relayout_tile(k_in, xk, 0, 0, j)
        relayout_tile(v_in, xv, 0, 0, j)

    for g in range(groups - 1):
        load(1, k_hbm, k_in, g + 1).wait()
        load(2, v_hbm, v_in, g + 1).wait()

    def end_states(g):
        k_taps, v_taps = taps_of(1, g), taps_of(2, g)
        decay = [per_mode(dec_n, g, m) for m in range(modes)]
        behind = range(SUB - taps + 1, SUB)

        def ahead(pair, half):
            after_it = jnp.minimum(g * pairs + pair + 1, groups * pairs - 1)
            g_next, pair_next = after_it // pairs, lax.rem(after_it, pairs)

            def one(s):
                src, dst = ((k_in, xk), (v_in, xv))[s % 2]
                if half is None:
                    relayout_tile(k_in, xk, g_next, pair_next, s)
                    relayout_tile(v_in, xv, g_next, pair_next, s)
                else:
                    relayout_tile(src, dst, g_next, pair_next, half * SUB // 2 + s // 2)

            return one

        start = block_of_z(
            2, g, [token(xk, 1, g, s) for s in behind], [token(xv, 1, g, s) for s in behind],
            [zero] * modes, k_taps, v_taps, decay, ahead(0, None),
        )

        def step(pair, carried):
            for half in range(2):
                carried = block_of_z(
                    2 * pair + 1 + half, g, *carried, k_taps, v_taps, decay, ahead(pair, half)
                )
            return carried

        _, _, state = lax.fori_loop(1, pairs, step, start)
        for m in range(modes):
            e_loc[pl.ds(g * SUB * modes + m, SUB, stride=modes), :] = state[m]

    side = 4

    def nth(i, j):
        near = lambda n: (n * (n + 1) // 2) % side
        y = lax.rem(spot // side + near(i), side)
        x = lax.rem(spot + near(j), side)
        return y * side + x

    def nth_of(n):
        return nth(n // side, lax.rem(n, side))

    @pl.loop(0, groups // 2)
    def _(g):
        end_states(g)

    owned = chans // PLANE
    for owner in range(PLANE):
        cols = slice(owner * owned, (owner + 1) * owned)
        edge[owner, 0] = k_in[tok - SUB : tok, cols]
        edge[owner, 1] = v_in[tok - SUB : tok, cols]
        edge[owner, 2] = k_in[0:SUB, cols]
        edge[owner, 3] = v_in[0:SUB, cols]

    crossing = ((spot + 1) // PLANE) * ((2 * planes - 3 - zed) // (planes - 1))
    crosses = crossing > 0
    pl.semaphore_wait(barrier, PLANE - 1 + planes - 1 + 1 + (2 * shards - 3 - me) // (shards - 1) + PLANE * crossing)

    def edge_copy(owner, slot, plane, kind):
        return pltpu.make_async_remote_copy(
            src_ref=edge.at[owner], dst_ref=edges.at[slot],
            send_sem=edge_send.at[kind, owner], recv_sem=edge_recv.at[slot],
            device_id=(plane * PLANE + owner, core), device_id_type=MESH,
        )

    @pl.loop(1, PLANE)
    def _(step):
        edge_copy(nth_of(PLANE - step), spot, zed, 0).start()

    @pl.when(crosses)
    def _():
        @pl.loop(0, PLANE)
        def _(owner):
            edge_copy(owner, PLANE, zed + 1, 1).start()

    edges[spot] = edge[spot]

    @pl.when(zed == 0)
    def _():
        edges[PLANE] = jnp.zeros_like(edges[PLANE])

    @pl.loop(groups // 2, groups)
    def _(g):
        end_states(g)

    def round_1(other):
        return pltpu.make_async_remote_copy(
            src_ref=e_out.at[other], dst_ref=e_buf.at[spot],
            send_sem=s1.at[other], recv_sem=r1.at[spot],
            device_id=(zed * PLANE + other, core), device_id_type=MESH,
        )

    def arrival_1(other):
        return pltpu.make_async_remote_copy(
            src_ref=e_out.at[other], dst_ref=e_buf.at[other],
            send_sem=s1.at[other], recv_sem=r1.at[other],
            device_id=(zed * PLANE + other, core), device_id_type=MESH,
        )

    for other in range(PLANE):
        e_out[other] = e_loc[other * part : (other + 1) * part, :].astype(jnp.bfloat16)

    @pl.loop(1, PLANE)
    def _(step):
        round_1(nth_of(PLANE - step)).start()

    def rim_copy(index, src, dst):
        return pltpu.make_async_remote_copy(
            src_ref=src.at[pl.ds(tok - SUB, SUB)], dst_ref=dst,
            send_sem=rim_send.at[index], recv_sem=rim_recv.at[index],
            device_id=(after, core), device_id_type=MESH,
        )

    rims = [rim_copy(0, k_hbm, rim_k), rim_copy(1, v_hbm, rim_v), rim_copy(2, q_hbm, rim_q)]
    @pl.when(me < shards - 1)
    def _():
        for copy in rims:
            copy.start()

    @pl.when(me == 0)
    def _():
        for rim in (rim_k, rim_v, rim_q):
            rim[...] = jnp.zeros_like(rim)

    e_buf[spot] = e_out[spot]

    begins = rows == 0
    for end in ends:
        begins = begins | (rows == end)
    keep_m[...] = jnp.where(begins, 0.0, 1.0)
    for t in range(tiles):
        taps_t[0, t * SUB : t * SUB + taps, :] = sf_in[0, :, t * LANES : (t + 1) * LANES]
    params[2].wait()
    params[3].wait()
    for t in range(tiles):
        x = -2.0 * rate_n[t * modes : (t + 1) * modes, :]
        series = 1.0 + x * (1.0 / 6.0)
        for n in (5.0, 4.0, 3.0, 2.0):
            series = 1.0 + x * (1.0 / n) * series
        coef_n[t * modes : (t + 1) * modes, :] = residue_in[:, t * LANES : (t + 1) * LANES] * jnp.sqrt(-x * series)

    @pl.loop(0, groups)
    def _(g):
        load(0, q_hbm, q_in, g).wait()
        relayout(q_in, xq, g)

    rising = (lax.broadcasted_iota(jnp.int32, (SUB, LANES), 0) + 1).astype(F32)

    @pl.loop(0, tiles)
    def _(t):
        for m in range(modes):
            rate = rate_n[pl.ds(t * modes + m, 1), :]
            coef = coef_n[pl.ds(t * modes + m, 1), :]
            here = pl.ds(pl.multiple_of((t * modes + m) * SUB, SUB), SUB)
            weights[here, :] = coef * jnp.exp(-rate * rising)
        whole = pl.ds(pl.multiple_of(t * modes, SUB), modes)
        dec8_n[whole, :] = jnp.exp(rate_n[whole, :] * float(-SUB))

    def tree(terms):
        while len(terms) > 1:
            terms = [a + b for a, b in zip(terms[::2], terms[1::2])]
        return terms[0]

    def conv_block(block, g, q_win, state, q_taps, decay, coef, z_of):
        q_win, state = list(q_win), list(state)
        for s in range(SUB):
            q_win.append(token(xq, block, g, s))
            qs = fir(q_win[-taps:], q_taps)
            t = (block - 1) * SUB + s
            z = z_of(t, s)
            keep = keep_m[pl.ds(t, 1), :]
            state = [(d * keep) * old + z for d, old in zip(decay, state)]
            out = tree([c * part for c, part in zip(coef, state)])
            there = pl.ds(row_of(block - 1, g * SUB) + s, SUB, stride=SUB)
            conv_std[there, :] = out * qs
            qs_std[there, :] = qs * carry_m[pl.ds(t, 1), :]
        return q_win[1 - taps :], state

    behind = range(SUB - taps + 1, SUB)

    def inner(g):
        q_taps = taps_of(0, g)
        decay = [per_mode(dec_n, g, m) for m in range(modes)]
        coef = [per_mode(coef_n, g, m) for m in range(modes)]

        def step(block, carried):
            return conv_block(block, g, *carried, q_taps, decay, coef, lambda t, s: zs[z_rows(t, g), :])

        lax.fori_loop(2, blocks + 1, step, ([token(xq, 1, g, s) for s in behind], [zero] * modes))

    def head(g):
        windows = [[token(x, 0, g, s) for s in behind] for x in (xk, xv)]
        weight = [taps_of(1, g), taps_of(2, g)]

        def z_of(t, s):
            for window, x in zip(windows, (xk, xv)):
                window.append(token(x, 1, g, s))
            return fir(windows[0][-taps:], weight[0]) * fir(windows[1][-taps:], weight[1])

        decay = [per_mode(dec_n, g, m) for m in range(modes)]
        coef = [per_mode(coef_n, g, m) for m in range(modes)]
        _, state = conv_block(
            1, g, [token(xq, 0, g, s) for s in behind], [zero] * modes, taps_of(0, g), decay, coef, z_of
        )
        for m in range(modes):
            head_n[pl.ds(g * SUB * modes + m, SUB, stride=modes), :] = state[m]

    inner(0)

    per = tiles // PLANE
    my_rate = at(rate_n, spot * part, part)[...]
    for i in range(SUB):
        source = pl.multiple_of((spot * per + i % per) * SUB, SUB)
        dec_own[i * SUB : (i + 1) * SUB, :] = dec_n[pl.ds(source, SUB), :]
        for a in (1, 2):
            taps_own[a - 1, i * SUB : (i + 1) * SUB, :] = taps_t[a, pl.ds(source, SUB), :]
    own_decay = [dec_own[pl.ds(m, SUB, stride=modes), :] for m in range(modes)]
    own_taps = [[taps_own[a, pl.ds(j, SUB, stride=SUB), :] for j in range(taps)] for a in range(2)]

    @pl.loop(1, PLANE)
    def _(step):
        source = lax.rem(spot + step, PLANE)
        edge_copy(source, source, zed, 0).wait_recv()

    @pl.when(zed > 0)
    def _():
        edge_copy(spot, PLANE, zed, 1).wait_recv()

    for j in range(PLANE):
        for a, dst in ((0, ek), (1, ev)):
            past = edges[(j + PLANE) % (PLANE + 1), a].astype(F32)
            here = edges[j, a + 2].astype(F32)
            for i in range(per):
                tile = j * per + i
                dst[row_of(0, tile) : row_of(0, tile) + SUB, :] = past[:, i * LANES : (i + 1) * LANES]
                dst[row_of(1, tile) : row_of(1, tile) + SUB, :] = here[:, i * LANES : (i + 1) * LANES]

    for g in range(groups):
        shard = zed * PLANE + (lax.broadcasted_iota(jnp.int32, (SUB, LANES), 0) + g * SUB) // per
        begin = shard * tok
        latest = jnp.full((SUB, LANES), -1, jnp.int32)
        for end in ends:
            latest = jnp.maximum(latest, jnp.where(end <= begin + (tok - 1), end, -1))
        window = [[token(x, 0, g, s) for s in range(SUB - taps + 1, SUB)] for x in (ek, ev)]
        state = [zero] * modes
        for s in range(SUB):
            window[0].append(token(ek, 1, g, s))
            window[1].append(token(ev, 1, g, s))
            z = fir(window[0][-taps:], own_taps[0]) * fir(window[1][-taps:], own_taps[1])
            z = jnp.where(begin + s >= latest, z, 0.0)
            state = [d * old + z for d, old in zip(own_decay, state)]
        for m in range(modes):
            e_first[pl.ds(g * SUB * modes + m, SUB, stride=modes), :] = state[m]

    @pl.loop(1, PLANE)
    def _(step):
        arrival_1(lax.rem(spot + step, PLANE)).wait_recv()

    span = jnp.exp(my_rate * float(-tok))
    spot_rows = lax.broadcasted_iota(jnp.int32, (PLANE, LANES), 0) + zed * PLANE
    plane_rows = lax.broadcasted_iota(jnp.int32, (SUB, LANES), 0)
    open_here = jnp.ones((PLANE, LANES), F32)
    open_plane = jnp.ones((SUB, LANES), F32)
    for end in ends:
        open_here = jnp.where(spot_rows == end // tok, 0.0, open_here)
        open_plane = jnp.where(plane_rows == end // (tok * PLANE), 0.0, open_plane)

    rest = jnp.exp(my_rate * float(SUB - tok))
    state = jnp.zeros_like(span)
    reach = jnp.ones_like(span)
    for other in range(PLANE):
        pre_buf[other] = state
        reach_buf[other] = reach
        factor = span * open_here[other : other + 1]
        state = factor * state + e_buf[other].astype(F32) + rest * e_first[other * part : (other + 1) * part, :]
        reach = factor * reach
    total_buf[...] = state

    def round_2(there, slot):
        return pltpu.make_async_remote_copy(
            src_ref=total_buf, dst_ref=plane_buf.at[slot],
            send_sem=s2.at[there], recv_sem=r2.at[slot],
            device_id=(there * PLANE + spot, core), device_id_type=MESH,
        )

    @pl.loop(zed + 1, planes)
    def _(there):
        round_2(there, zed).start()

    @pl.loop(1, groups - 1)
    def _(g):
        inner(g)

    plane_span = jnp.exp(my_rate * float(-tok * PLANE))

    def plane_step(there, state):
        round_2(there, there).wait_recv()
        row = jnp.sum(jnp.where(plane_rows == there, open_plane, 0.0), axis=0, keepdims=True)
        return plane_span * row * state + plane_buf[there]

    state = lax.fori_loop(0, zed, plane_step, jnp.zeros_like(span))
    def round_3(other, slot):
        return pltpu.make_async_remote_copy(
            src_ref=inc_out.at[other], dst_ref=inc_buf.at[slot],
            send_sem=s3.at[other], recv_sem=r3.at[slot],
            device_id=(zed * PLANE + other, core), device_id_type=MESH,
        )

    @pl.loop(1, PLANE)
    def _(step):
        other = nth_of(PLANE - step)
        inc_out[other] = (pre_buf[other] + reach_buf[other] * state).astype(jnp.bfloat16)
        round_3(other, spot).start()

    inc_buf[spot] = (pre_buf[spot] + reach_buf[spot] * state).astype(jnp.bfloat16)

    inner(groups - 1)

    @pl.when(me > 0)
    def _():
        for copy in rims:
            copy.wait_recv()

    relayout_rim(rim_k, xk)
    relayout_rim(rim_v, xv)
    relayout_rim(rim_q, xq)

    @pl.loop(0, groups)
    def _(g):
        head(g)

    for g in range(groups):
        load(3, r_hbm, r_in, g).wait()

    @pl.loop(0, tiles)
    def _(t):
        cols = pl.ds(pl.multiple_of(t * LANES, LANES), LANES)
        for pair in range(pairs):
            x = r_in[pair * 2 * SUB : (pair + 1) * 2 * SUB, cols].astype(F32)
            for half in range(2):
                here = pl.ds(pl.multiple_of(row_of(2 * pair + half, t), SUB), SUB)
                conv_std[here, :] = conv_std[here, :] + x[half * SUB : (half + 1) * SUB]

    sq_loc[...] = jnp.zeros_like(sq_loc)


    def tile_of(slot, local):
        t = slot * per + local
        whole = pl.ds(pl.multiple_of(t * modes, SUB), modes)
        incoming = inc_buf[slot].astype(F32)[local * modes : (local + 1) * modes]
        at_8 = dec8_n[whole, :] * carry_m[SUB - 1 : SUB, :] * incoming + head_n[whole, :]
        value, later, decay = [], [], []
        for m in range(modes):
            here = pl.ds(pl.multiple_of((t * modes + m) * SUB, SUB), SUB)
            weight = weights[here, :]
            value.append(weight * incoming[m : m + 1])
            later.append(weight * at_8[m : m + 1])
            decay.append(jnp.broadcast_to(dec8_n[pl.ds(t * modes + m, 1), :], (SUB, LANES)))
        cols = pl.ds(pl.multiple_of(t * LANES, LANES), LANES)
        for pair in range(pairs):
            halves = []
            for block in (2 * pair, 2 * pair + 1):
                carried = tree(value)
                if block == 0:
                    value = later
                elif block < blocks - 1:
                    value = [v * d for v, d in zip(value, decay)]
                here = pl.ds(pl.multiple_of(row_of(block, t), SUB), SUB)
                halves.append(conv_std[here, :] + qs_std[here, :] * carried)
            both = pl.ds(pair * 2 * SUB, 2 * SUB)
            stream = jnp.concatenate(halves, axis=0).astype(jnp.bfloat16)
            stream_ref[both, cols] = stream
            back = stream.astype(F32)
            sq_loc[both, :] = sq_loc[both, :] + back * back

    @pl.loop(0, PLANE)
    def _(n):
        slot = nth_of(n)

        @pl.when(n > 0)
        def _():
            round_3(slot, slot).wait_recv()

        for local in range(per):
            tile_of(slot, local)

    swap = pltpu.make_async_remote_copy(
        src_ref=sq_loc, dst_ref=sq_far, send_sem=sq_send, recv_sem=sq_recv,
        device_id=(me, 1 - core), device_id_type=MESH,
    )
    swap.start()

    @pl.when(me < shards - 1)
    def _():
        for copy in rims:
            copy.wait_send()

    @pl.loop(1, PLANE)
    def _(step):
        other = lax.rem(spot + step, PLANE)
        round_1(other).wait_send()
        round_3(other, spot).wait_send()
        edge_copy(other, spot, zed, 0).wait_send()

    @pl.when(crosses)
    def _():
        @pl.loop(0, PLANE)
        def _(owner):
            edge_copy(owner, PLANE, zed + 1, 1).wait_send()

    @pl.loop(zed + 1, planes)
    def _(there):
        round_2(there, zed).wait_send()

    swap.wait()
    total = jnp.sum(sq_loc[...] + sq_far[...], axis=1, keepdims=True)
    scale = lax.rsqrt(total * (1.0 / (2 * chans)) + 1e-6)
    scale_ref[...] = jnp.broadcast_to(scale, (tok, LANES))


def finish(tok, chans, stream_ref, scale_ref, gain_ref, stream_hbm, normed_hbm, normed, sem):
    wide = SUB * LANES
    groups = chans // wide
    copies = [pltpu.make_async_copy(stream_ref, stream_hbm, sem.at[groups])]
    copies[0].start()
    scales = [scale_ref[pair * 2 * SUB : (pair + 1) * 2 * SUB, :] for pair in range(tok // (2 * SUB))]
    for g in range(groups):
        @pl.loop(g * SUB, (g + 1) * SUB)
        def _(t):
            cols = pl.ds(pl.multiple_of(t * LANES, LANES), LANES)
            gain = gain_ref[pl.ds(t, 1), :]
            for pair, scale in enumerate(scales):
                both = slice(pair * 2 * SUB, (pair + 1) * 2 * SUB)
                x = stream_ref[both, cols].astype(F32)
                normed[both, cols] = (x * scale * gain).astype(jnp.bfloat16)

        part = slice(g * wide, (g + 1) * wide)
        copy = pltpu.make_async_copy(normed.at[:, part], normed_hbm.at[:, part], sem.at[g])
        copy.start()
        copies.append(copy)
    for copy in copies:
        copy.wait()


def body(q_proj, k_proj, v_proj, resid, short_filter, residue, rate, gain, seg_lengths):
    tok, chans = q_proj.shape
    taps = short_filter.shape[1]
    modes = rate.shape[0]
    segs = seg_lengths.shape[0]
    shards = lax.axis_size("seq")
    planes = shards // PLANE
    tiles = chans // LANES
    groups = tiles // SUB
    blocks = tok // SUB
    part = tiles * modes // PLANE
    bf16 = jnp.bfloat16
    dims = (shards, planes, tok, chans, modes, taps, segs)
    vmem = pltpu.VMEM
    sem = pltpu.SemaphoreType.DMA
    hbm_spec = pl.BlockSpec(memory_space=pltpu.HBM)
    stream, scale, gain = pl.pallas_call(
        functools.partial(kernel, dims),
        out_shape=(
            jax.ShapeDtypeStruct((tok, chans), bf16),
            jax.ShapeDtypeStruct((tok, LANES), F32),
            jax.ShapeDtypeStruct((tiles, LANES), F32),
        ),
        in_specs=[hbm_spec] * 9,
        out_specs=(pl.BlockSpec(memory_space=vmem),) * 3,
        scratch_shapes=[
            vmem((tok, chans), bf16), vmem((tok, chans), bf16), vmem((tok, chans), bf16), vmem((tok, chans), bf16),
            vmem((3, taps, chans), F32), vmem((modes, chans), F32), vmem((modes, chans), F32),
            pltpu.SMEM((segs,), jnp.int32),
            vmem((SUB, chans), bf16), vmem((SUB, chans), bf16), vmem((SUB, chans), bf16),
            vmem((PLANE, 4, SUB, chans // PLANE), bf16), vmem((PLANE + 1, 4, SUB, chans // PLANE), bf16),
            vmem((2 * tiles * SUB, LANES), F32), vmem((2 * tiles * SUB, LANES), F32),
            vmem((tiles * modes, LANES), F32), vmem((tiles * modes, LANES), F32),
            vmem((SUB * modes, LANES), F32), vmem((2, SUB * SUB, LANES), F32),
            vmem(((blocks + 1) * tiles * SUB, LANES), F32),
            vmem(((blocks + 1) * tiles * SUB, LANES), F32),
            vmem(((blocks + 1) * tiles * SUB, LANES), F32),
            vmem((blocks * tiles * SUB, LANES), F32),
            vmem((blocks * tiles * SUB, LANES), F32),
            vmem((blocks * tiles * SUB, LANES), F32),
            vmem((3, tiles * SUB, LANES), F32),
            vmem((tiles * modes, LANES), F32), vmem((tiles * modes, LANES), F32), vmem((tiles * modes, LANES), F32),
            vmem((tiles * modes * SUB, LANES), F32), vmem((tiles * modes, LANES), F32),
            vmem((tok, LANES), F32), vmem((tok, LANES), F32), vmem((tok, LANES), F32),
            vmem((tiles * modes, LANES), F32),
            vmem((PLANE, part, LANES), bf16), vmem((PLANE, part, LANES), bf16),
            vmem((PLANE, part, LANES), F32), vmem((PLANE, part, LANES), F32),
            vmem((part, LANES), F32), vmem((planes, part, LANES), F32),
            vmem((PLANE, part, LANES), bf16), vmem((PLANE, part, LANES), bf16),
            vmem((tok, LANES), F32), vmem((tok, LANES), F32),
            sem((4, groups)), sem((5,)), sem((3,)), sem((3,)), sem((2, PLANE)), sem((PLANE + 1,)),
            sem((PLANE,)), sem((PLANE,)), sem((planes,)), sem((planes,)), sem((PLANE,)), sem((PLANE,)),
            sem, sem,
        ],
        compiler_params=pltpu.CompilerParams(
            collective_id=0, has_side_effects=True, vmem_limit_bytes=40 * 1024 * 1024
        ),
        name="hyena",
    )(*(pltpu.with_memory_space_constraint(x, pltpu.HBM) for x in (
        q_proj, k_proj, v_proj, resid, short_filter, residue, rate, gain.reshape(tiles, LANES), seg_lengths
    )))
    return pl.pallas_call(
        functools.partial(finish, tok, chans),
        out_shape=(jax.ShapeDtypeStruct((tok, chans), bf16),) * 2,
        in_specs=[pl.BlockSpec(memory_space=vmem)] * 3,
        out_specs=(hbm_spec,) * 2,
        scratch_shapes=[vmem((tok, chans), bf16), sem((chans // (SUB * LANES) + 1,))],
        compiler_params=pltpu.CompilerParams(vmem_limit_bytes=16 * 1024 * 1024),
        name="finish",
    )(stream, scale, gain)


def solution(mesh):
    placed = (
        P("seq", "chan"),
        P("seq", "chan"),
        P("seq", "chan"),
        P("seq", "chan"),
        P(None, None, "chan"),
        P(None, "chan"),
        P(None, "chan"),
        P("chan"),
        P(),
    )
    return jax.shard_map(
        body,
        mesh=mesh,
        in_specs=placed,
        out_specs=(P("seq", "chan"), P("seq", "chan")),
        check_vma=False,
    )
```

```python
import functools
import jax
import jax.numpy as jnp
from jax import lax
from jax.experimental import pallas as pl
from jax.experimental.pallas import tpu as pltpu
from jax.sharding import PartitionSpec as P

MESH = pl.DeviceIdType.MESH
PLANE = 16
LANES = 128
SUB = 8
F32 = jnp.float32


def kernel(
    dims,
    q_hbm, k_hbm, v_hbm, r_hbm, sf_hbm, residue_hbm, rate_hbm, gain_hbm, seg_hbm,
    stream_ref, scale_ref, gain_in,
    q_in, k_in, v_in, r_in, sf_in, residue_in, rate_in, seg_ref,
    rim_q, rim_k, rim_v, edge, edges, ek, ev, e_first, head_n, dec_own, taps_own,
    xq, xk, xv, zs, conv_std, qs_std,
    taps_t, rate_n, coef_n, dec_n, weights, dec8_n,
    keep_m, last_m, carry_m,
    e_loc, e_out, e_buf, pre_buf, reach_buf, total_buf, plane_buf, inc_out, inc_buf, sq_loc, sq_far,
    in_sem, param_sem, rim_send, rim_recv, edge_send, edge_recv, s1, r1, s2, r2, s3, r3, sq_send, sq_recv,
):
    shards, planes, tok, chans, modes, taps, segs = dims
    blocks = tok // SUB
    pairs = blocks // 2
    tiles = chans // LANES
    groups = tiles // SUB
    wide = SUB * LANES
    part = tiles * modes // PLANE
    me = lax.axis_index("seq")
    core = lax.axis_index("chan")
    zed = me // PLANE
    spot = lax.rem(me, PLANE)
    after = lax.rem(me + 1, shards)
    before = lax.rem(me + shards - 1, shards)

    def at(ref, start, size):
        return ref.at[pl.ds(pl.multiple_of(start, SUB), size)]

    params = [
        pltpu.make_async_copy(rate_hbm, rate_in, param_sem.at[0]),
        pltpu.make_async_copy(sf_hbm, sf_in, param_sem.at[1]),
        pltpu.make_async_copy(residue_hbm, residue_in, param_sem.at[2]),
        pltpu.make_async_copy(gain_hbm, gain_in, param_sem.at[3]),
        pltpu.make_async_copy(seg_hbm, seg_ref, param_sem.at[4]),
    ]

    def load(index, src, dst, g):
        cols = pl.ds(g * wide, wide)
        return pltpu.make_async_copy(src.at[:, cols], dst.at[:, cols], in_sem.at[index, g])

    for index in (4, 0, 1):
        params[index].start()
    for g in range(groups):
        load(1, k_hbm, k_in, g).start()
        load(2, v_hbm, v_in, g).start()
    for index in (2, 3):
        params[index].start()
    for g in range(groups):
        load(0, q_hbm, q_in, g).start()
    for g in range(groups):
        load(3, r_hbm, r_in, g).start()

    barrier = pltpu.get_barrier_semaphore()

    @pl.loop(1, PLANE)
    def _(step):
        other = zed * PLANE + lax.rem(spot + step, PLANE)
        pl.semaphore_signal(barrier, inc=1, device_id=(other, core), device_id_type=MESH)

    @pl.loop(1, planes)
    def _(step):
        other = lax.rem(zed + step, planes) * PLANE + spot
        pl.semaphore_signal(barrier, inc=1, device_id=(other, core), device_id_type=MESH)

    @pl.when(zed > 0)
    def _():
        last = (zed - 1) * PLANE + PLANE - 1
        pl.semaphore_signal(barrier, inc=1, device_id=(last, core), device_id_type=MESH)

    @pl.when(me > 0)
    def _():
        pl.semaphore_signal(barrier, inc=1, device_id=(before, core), device_id_type=MESH)

    pl.semaphore_signal(barrier, inc=1, device_id=(me, 1 - core), device_id_type=MESH)

    params[4].wait()
    first = me * tok
    ends = []
    running = seg_ref[0]
    ends.append(running)
    for j in range(1, segs):
        running = running + seg_ref[j]
        ends.append(running)
    big = jnp.int32(1 << 30)
    low = big
    low8 = big
    high = jnp.int32(-1)
    for end in ends:
        low = jnp.minimum(low, jnp.where(end >= first, end, big))
        low8 = jnp.minimum(low8, jnp.where(end >= first + SUB, end, big))
        high = jnp.maximum(high, jnp.where(end <= first + tok - 1, end, -1))
    rows = lax.broadcasted_iota(jnp.int32, (tok, LANES), 0) + first
    last_m[...] = jnp.where(rows >= high, 1.0, 0.0)
    carry_m[...] = jnp.where(rows < low8, 1.0, 0.0)
    carry_m[:SUB, :] = jnp.where(rows[:SUB] < low, 1.0, 0.0)

    params[0].wait()
    for t in range(tiles):
        rate = rate_in[:, t * LANES : (t + 1) * LANES]
        rate_n[t * modes : (t + 1) * modes, :] = rate
        dec_n[t * modes : (t + 1) * modes, :] = jnp.exp(-rate)
    params[1].wait()
    for a in (1, 2):
        for t in range(tiles):
            taps_t[a, t * SUB : t * SUB + taps, :] = sf_in[a, :, t * LANES : (t + 1) * LANES]

    def row_of(block, tile):
        return (block * tiles + tile) * SUB

    def relayout_tile(src, dst, g, pair, j):
        x = src[pl.ds(pl.multiple_of(pair * 2 * SUB, 2 * SUB), 2 * SUB),
                pl.ds(pl.multiple_of(g * wide + j * LANES, LANES), LANES)].astype(F32)
        lower = pl.multiple_of(row_of(2 * pair + 1, g * SUB + j), SUB)
        dst[pl.ds(lower, SUB), :] = x[:SUB]
        upper = pl.multiple_of(row_of(2 * pair + 2, g * SUB + j), SUB)
        dst[pl.ds(upper, SUB), :] = x[SUB:]

    def relayout(src, dst, g):
        @pl.loop(0, pairs)
        def _(pair):
            for j in range(SUB):
                relayout_tile(src, dst, g, pair, j)

    def relayout_rim(src, dst):
        for t in range(tiles):
            x = src[:, t * LANES : (t + 1) * LANES].astype(F32)
            dst[t * SUB : (t + 1) * SUB, :] = jnp.where(me > 0, x, 0.0)

    def token(ref, block, g, s):
        return ref[pl.ds(row_of(block, g * SUB) + s, SUB, stride=SUB), :]

    def per_mode(ref, g, m):
        return ref[pl.ds(g * SUB * modes + m, SUB, stride=modes), :]

    def taps_of(a, g):
        return [taps_t[a, pl.ds(g * SUB * SUB + j, SUB, stride=SUB), :] for j in range(taps)]

    def fir(window, weight):
        out = weight[0] * window[-1]
        for j in range(1, taps):
            out = out + weight[j] * window[-1 - j]
        return out

    def z_rows(t, g):
        return pl.ds(pl.multiple_of((t * groups + g) * SUB, SUB), SUB)

    def block_of_z(block, g, k_win, v_win, state, k_taps, v_taps, decay, beside=None):
        k_win, v_win, state = list(k_win), list(v_win), list(state)
        for s in range(SUB):
            if beside is not None:
                beside(s)
            k_win.append(token(xk, block, g, s))
            v_win.append(token(xv, block, g, s))
            z = fir(k_win[-taps:], k_taps) * fir(v_win[-taps:], v_taps)
            t = (block - 1) * SUB + s
            zs[z_rows(t, g), :] = z
            z = z * last_m[pl.ds(t, 1), :]
            state = [d * old + z for d, old in zip(decay, state)]
        return k_win[1 - taps :], v_win[1 - taps :], state

    zero = jnp.zeros((SUB, LANES), F32)

    load(1, k_hbm, k_in, 0).wait()
    load(2, v_hbm, v_in, 0).wait()
    for j in range(SUB):
        relayout_tile(k_in, xk, 0, 0, j)
        relayout_tile(v_in, xv, 0, 0, j)

    for g in range(groups - 1):
        load(1, k_hbm, k_in, g + 1).wait()
        load(2, v_hbm, v_in, g + 1).wait()

    def end_states(g):
        k_taps, v_taps = taps_of(1, g), taps_of(2, g)
        decay = [per_mode(dec_n, g, m) for m in range(modes)]
        behind = range(SUB - taps + 1, SUB)

        def ahead(pair, half):
            after_it = jnp.minimum(g * pairs + pair + 1, groups * pairs - 1)
            g_next, pair_next = after_it // pairs, lax.rem(after_it, pairs)

            def one(s):
                src, dst = ((k_in, xk), (v_in, xv))[s % 2]
                if half is None:
                    relayout_tile(k_in, xk, g_next, pair_next, s)
                    relayout_tile(v_in, xv, g_next, pair_next, s)
                else:
                    relayout_tile(src, dst, g_next, pair_next, half * SUB // 2 + s // 2)

            return one

        start = block_of_z(
            2, g, [token(xk, 1, g, s) for s in behind], [token(xv, 1, g, s) for s in behind],
            [zero] * modes, k_taps, v_taps, decay, ahead(0, None),
        )

        def step(pair, carried):
            for half in range(2):
                carried = block_of_z(
                    2 * pair + 1 + half, g, *carried, k_taps, v_taps, decay, ahead(pair, half)
                )
            return carried

        _, _, state = lax.fori_loop(1, pairs, step, start)
        for m in range(modes):
            e_loc[pl.ds(g * SUB * modes + m, SUB, stride=modes), :] = state[m]

    side = 4

    def nth(i, j):
        near = lambda n: (n * (n + 1) // 2) % side
        y = lax.rem(spot // side + near(i), side)
        x = lax.rem(spot + near(j), side)
        return y * side + x

    def nth_of(n):
        return nth(n // side, lax.rem(n, side))

    @pl.loop(0, groups // 2)
    def _(g):
        end_states(g)

    owned = chans // PLANE
    for owner in range(PLANE):
        cols = slice(owner * owned, (owner + 1) * owned)
        edge[owner, 0] = k_in[tok - SUB : tok, cols]
        edge[owner, 1] = v_in[tok - SUB : tok, cols]
        edge[owner, 2] = k_in[0:SUB, cols]
        edge[owner, 3] = v_in[0:SUB, cols]

    crossing = ((spot + 1) // PLANE) * ((2 * planes - 3 - zed) // (planes - 1))
    crosses = crossing > 0
    pl.semaphore_wait(barrier, PLANE - 1 + planes - 1 + 1 + (2 * shards - 3 - me) // (shards - 1) + PLANE * crossing)

    def edge_copy(owner, slot, plane, kind):
        return pltpu.make_async_remote_copy(
            src_ref=edge.at[owner], dst_ref=edges.at[slot],
            send_sem=edge_send.at[kind, owner], recv_sem=edge_recv.at[slot],
            device_id=(plane * PLANE + owner, core), device_id_type=MESH,
        )

    @pl.loop(1, PLANE)
    def _(step):
        edge_copy(nth_of(PLANE - step), spot, zed, 0).start()

    @pl.when(crosses)
    def _():
        @pl.loop(0, PLANE)
        def _(owner):
            edge_copy(owner, PLANE, zed + 1, 1).start()

    edges[spot] = edge[spot]

    @pl.when(zed == 0)
    def _():
        edges[PLANE] = jnp.zeros_like(edges[PLANE])

    @pl.loop(groups // 2, groups)
    def _(g):
        end_states(g)

    def round_1(other):
        return pltpu.make_async_remote_copy(
            src_ref=e_out.at[other], dst_ref=e_buf.at[spot],
            send_sem=s1.at[other], recv_sem=r1.at[spot],
            device_id=(zed * PLANE + other, core), device_id_type=MESH,
        )

    def arrival_1(other):
        return pltpu.make_async_remote_copy(
            src_ref=e_out.at[other], dst_ref=e_buf.at[other],
            send_sem=s1.at[other], recv_sem=r1.at[other],
            device_id=(zed * PLANE + other, core), device_id_type=MESH,
        )

    for other in range(PLANE):
        e_out[other] = e_loc[other * part : (other + 1) * part, :].astype(jnp.bfloat16)

    @pl.loop(1, PLANE)
    def _(step):
        round_1(nth_of(PLANE - step)).start()

    def rim_copy(index, src, dst):
        return pltpu.make_async_remote_copy(
            src_ref=src.at[pl.ds(tok - SUB, SUB)], dst_ref=dst,
            send_sem=rim_send.at[index], recv_sem=rim_recv.at[index],
            device_id=(after, core), device_id_type=MESH,
        )

    rims = [rim_copy(0, k_hbm, rim_k), rim_copy(1, v_hbm, rim_v), rim_copy(2, q_hbm, rim_q)]
    @pl.when(me < shards - 1)
    def _():
        for copy in rims:
            copy.start()

    @pl.when(me == 0)
    def _():
        for rim in (rim_k, rim_v, rim_q):
            rim[...] = jnp.zeros_like(rim)

    e_buf[spot] = e_out[spot]

    begins = rows == 0
    for end in ends:
        begins = begins | (rows == end)
    keep_m[...] = jnp.where(begins, 0.0, 1.0)
    for t in range(tiles):
        taps_t[0, t * SUB : t * SUB + taps, :] = sf_in[0, :, t * LANES : (t + 1) * LANES]
    params[2].wait()
    params[3].wait()
    for t in range(tiles):
        x = -2.0 * rate_n[t * modes : (t + 1) * modes, :]
        series = 1.0 + x * (1.0 / 6.0)
        for n in (5.0, 4.0, 3.0, 2.0):
            series = 1.0 + x * (1.0 / n) * series
        coef_n[t * modes : (t + 1) * modes, :] = residue_in[:, t * LANES : (t + 1) * LANES] * jnp.sqrt(-x * series)

    @pl.loop(0, groups)
    def _(g):
        load(0, q_hbm, q_in, g).wait()
        relayout(q_in, xq, g)

    rising = (lax.broadcasted_iota(jnp.int32, (SUB, LANES), 0) + 1).astype(F32)

    @pl.loop(0, tiles)
    def _(t):
        for m in range(modes):
            rate = rate_n[pl.ds(t * modes + m, 1), :]
            coef = coef_n[pl.ds(t * modes + m, 1), :]
            here = pl.ds(pl.multiple_of((t * modes + m) * SUB, SUB), SUB)
            weights[here, :] = coef * jnp.exp(-rate * rising)
        whole = pl.ds(pl.multiple_of(t * modes, SUB), modes)
        dec8_n[whole, :] = jnp.exp(rate_n[whole, :] * float(-SUB))

    def tree(terms):
        while len(terms) > 1:
            terms = [a + b for a, b in zip(terms[::2], terms[1::2])]
        return terms[0]

    def conv_block(block, g, q_win, state, q_taps, decay, coef, z_of):
        q_win, state = list(q_win), list(state)
        for s in range(SUB):
            q_win.append(token(xq, block, g, s))
            qs = fir(q_win[-taps:], q_taps)
            t = (block - 1) * SUB + s
            z = z_of(t, s)
            keep = keep_m[pl.ds(t, 1), :]
            state = [(d * keep) * old + z for d, old in zip(decay, state)]
            out = tree([c * part for c, part in zip(coef, state)])
            there = pl.ds(row_of(block - 1, g * SUB) + s, SUB, stride=SUB)
            conv_std[there, :] = out * qs
            qs_std[there, :] = qs * carry_m[pl.ds(t, 1), :]
        return q_win[1 - taps :], state

    behind = range(SUB - taps + 1, SUB)

    def inner(g):
        q_taps = taps_of(0, g)
        decay = [per_mode(dec_n, g, m) for m in range(modes)]
        coef = [per_mode(coef_n, g, m) for m in range(modes)]

        def step(block, carried):
            return conv_block(block, g, *carried, q_taps, decay, coef, lambda t, s: zs[z_rows(t, g), :])

        lax.fori_loop(2, blocks + 1, step, ([token(xq, 1, g, s) for s in behind], [zero] * modes))

    def head(g):
        windows = [[token(x, 0, g, s) for s in behind] for x in (xk, xv)]
        weight = [taps_of(1, g), taps_of(2, g)]

        def z_of(t, s):
            for window, x in zip(windows, (xk, xv)):
                window.append(token(x, 1, g, s))
            return fir(windows[0][-taps:], weight[0]) * fir(windows[1][-taps:], weight[1])

        decay = [per_mode(dec_n, g, m) for m in range(modes)]
        coef = [per_mode(coef_n, g, m) for m in range(modes)]
        _, state = conv_block(
            1, g, [token(xq, 0, g, s) for s in behind], [zero] * modes, taps_of(0, g), decay, coef, z_of
        )
        for m in range(modes):
            head_n[pl.ds(g * SUB * modes + m, SUB, stride=modes), :] = state[m]

    inner(0)

    per = tiles // PLANE
    my_rate = at(rate_n, spot * part, part)[...]
    for i in range(SUB):
        source = pl.multiple_of((spot * per + i % per) * SUB, SUB)
        dec_own[i * SUB : (i + 1) * SUB, :] = dec_n[pl.ds(source, SUB), :]
        for a in (1, 2):
            taps_own[a - 1, i * SUB : (i + 1) * SUB, :] = taps_t[a, pl.ds(source, SUB), :]
    own_decay = [dec_own[pl.ds(m, SUB, stride=modes), :] for m in range(modes)]
    own_taps = [[taps_own[a, pl.ds(j, SUB, stride=SUB), :] for j in range(taps)] for a in range(2)]

    @pl.loop(1, PLANE)
    def _(step):
        source = lax.rem(spot + step, PLANE)
        edge_copy(source, source, zed, 0).wait_recv()

    @pl.when(zed > 0)
    def _():
        edge_copy(spot, PLANE, zed, 1).wait_recv()

    for j in range(PLANE):
        for a, dst in ((0, ek), (1, ev)):
            past = edges[(j + PLANE) % (PLANE + 1), a].astype(F32)
            here = edges[j, a + 2].astype(F32)
            for i in range(per):
                tile = j * per + i
                dst[row_of(0, tile) : row_of(0, tile) + SUB, :] = past[:, i * LANES : (i + 1) * LANES]
                dst[row_of(1, tile) : row_of(1, tile) + SUB, :] = here[:, i * LANES : (i + 1) * LANES]

    for g in range(groups):
        shard = zed * PLANE + (lax.broadcasted_iota(jnp.int32, (SUB, LANES), 0) + g * SUB) // per
        begin = shard * tok
        latest = jnp.full((SUB, LANES), -1, jnp.int32)
        for end in ends:
            latest = jnp.maximum(latest, jnp.where(end <= begin + (tok - 1), end, -1))
        window = [[token(x, 0, g, s) for s in range(SUB - taps + 1, SUB)] for x in (ek, ev)]
        state = [zero] * modes
        for s in range(SUB):
            window[0].append(token(ek, 1, g, s))
            window[1].append(token(ev, 1, g, s))
            z = fir(window[0][-taps:], own_taps[0]) * fir(window[1][-taps:], own_taps[1])
            z = jnp.where(begin + s >= latest, z, 0.0)
            state = [d * old + z for d, old in zip(own_decay, state)]
        for m in range(modes):
            e_first[pl.ds(g * SUB * modes + m, SUB, stride=modes), :] = state[m]

    @pl.loop(1, PLANE)
    def _(step):
        arrival_1(lax.rem(spot + step, PLANE)).wait_recv()

    span = jnp.exp(my_rate * float(-tok))
    spot_rows = lax.broadcasted_iota(jnp.int32, (PLANE, LANES), 0) + zed * PLANE
    plane_rows = lax.broadcasted_iota(jnp.int32, (SUB, LANES), 0)
    open_here = jnp.ones((PLANE, LANES), F32)
    open_plane = jnp.ones((SUB, LANES), F32)
    for end in ends:
        open_here = jnp.where(spot_rows == end // tok, 0.0, open_here)
        open_plane = jnp.where(plane_rows == end // (tok * PLANE), 0.0, open_plane)

    rest = jnp.exp(my_rate * float(SUB - tok))
    state = jnp.zeros_like(span)
    reach = jnp.ones_like(span)
    for other in range(PLANE):
        pre_buf[other] = state
        reach_buf[other] = reach
        factor = span * open_here[other : other + 1]
        state = factor * state + e_buf[other].astype(F32) + rest * e_first[other * part : (other + 1) * part, :]
        reach = factor * reach
    total_buf[...] = state

    def round_2(there, slot):
        return pltpu.make_async_remote_copy(
            src_ref=total_buf, dst_ref=plane_buf.at[slot],
            send_sem=s2.at[there], recv_sem=r2.at[slot],
            device_id=(there * PLANE + spot, core), device_id_type=MESH,
        )

    @pl.loop(zed + 1, planes)
    def _(there):
        round_2(there, zed).start()

    @pl.loop(1, groups - 1)
    def _(g):
        inner(g)

    plane_span = jnp.exp(my_rate * float(-tok * PLANE))

    def plane_step(there, state):
        round_2(there, there).wait_recv()
        row = jnp.sum(jnp.where(plane_rows == there, open_plane, 0.0), axis=0, keepdims=True)
        return plane_span * row * state + plane_buf[there]

    state = lax.fori_loop(0, zed, plane_step, jnp.zeros_like(span))
    def round_3(other, slot):
        return pltpu.make_async_remote_copy(
            src_ref=inc_out.at[other], dst_ref=inc_buf.at[slot],
            send_sem=s3.at[other], recv_sem=r3.at[slot],
            device_id=(zed * PLANE + other, core), device_id_type=MESH,
        )

    @pl.loop(1, PLANE)
    def _(step):
        other = nth_of(PLANE - step)
        inc_out[other] = (pre_buf[other] + reach_buf[other] * state).astype(jnp.bfloat16)
        round_3(other, spot).start()

    inc_buf[spot] = (pre_buf[spot] + reach_buf[spot] * state).astype(jnp.bfloat16)

    inner(groups - 1)

    for g in range(groups):
        load(3, r_hbm, r_in, g).wait()

    def add_residual(begin, end):
        @pl.loop(0, tiles)
        def _(t):
            cols = pl.ds(pl.multiple_of(t * LANES, LANES), LANES)
            for pair in range(begin, end):
                x = r_in[pair * 2 * SUB : (pair + 1) * 2 * SUB, cols].astype(F32)
                for half in range(2):
                    here = pl.ds(pl.multiple_of(row_of(2 * pair + half, t), SUB), SUB)
                    conv_std[here, :] = conv_std[here, :] + x[half * SUB : (half + 1) * SUB]

    add_residual(1, pairs)
    sq_loc[...] = jnp.zeros_like(sq_loc)

    @pl.when(me > 0)
    def _():
        for copy in rims:
            copy.wait_recv()

    relayout_rim(rim_k, xk)
    relayout_rim(rim_v, xv)
    relayout_rim(rim_q, xq)

    @pl.loop(0, groups)
    def _(g):
        head(g)

    add_residual(0, 1)


    def tile_of(slot, local):
        t = slot * per + local
        whole = pl.ds(pl.multiple_of(t * modes, SUB), modes)
        incoming = inc_buf[slot].astype(F32)[local * modes : (local + 1) * modes]
        at_8 = dec8_n[whole, :] * carry_m[SUB - 1 : SUB, :] * incoming + head_n[whole, :]
        value, later, decay = [], [], []
        for m in range(modes):
            here = pl.ds(pl.multiple_of((t * modes + m) * SUB, SUB), SUB)
            weight = weights[here, :]
            value.append(weight * incoming[m : m + 1])
            later.append(weight * at_8[m : m + 1])
            decay.append(jnp.broadcast_to(dec8_n[pl.ds(t * modes + m, 1), :], (SUB, LANES)))
        cols = pl.ds(pl.multiple_of(t * LANES, LANES), LANES)
        for pair in range(pairs):
            halves = []
            for block in (2 * pair, 2 * pair + 1):
                carried = tree(value)
                if block == 0:
                    value = later
                elif block < blocks - 1:
                    value = [v * d for v, d in zip(value, decay)]
                here = pl.ds(pl.multiple_of(row_of(block, t), SUB), SUB)
                halves.append(conv_std[here, :] + qs_std[here, :] * carried)
            both = pl.ds(pair * 2 * SUB, 2 * SUB)
            stream = jnp.concatenate(halves, axis=0).astype(jnp.bfloat16)
            stream_ref[both, cols] = stream
            back = stream.astype(F32)
            sq_loc[both, :] = sq_loc[both, :] + back * back

    @pl.loop(0, PLANE)
    def _(n):
        slot = nth_of(n)

        @pl.when(n > 0)
        def _():
            round_3(slot, slot).wait_recv()

        for local in range(per):
            tile_of(slot, local)

    swap = pltpu.make_async_remote_copy(
        src_ref=sq_loc, dst_ref=sq_far, send_sem=sq_send, recv_sem=sq_recv,
        device_id=(me, 1 - core), device_id_type=MESH,
    )
    swap.start()

    @pl.when(me < shards - 1)
    def _():
        for copy in rims:
            copy.wait_send()

    @pl.loop(1, PLANE)
    def _(step):
        other = lax.rem(spot + step, PLANE)
        round_1(other).wait_send()
        round_3(other, spot).wait_send()
        edge_copy(other, spot, zed, 0).wait_send()

    @pl.when(crosses)
    def _():
        @pl.loop(0, PLANE)
        def _(owner):
            edge_copy(owner, PLANE, zed + 1, 1).wait_send()

    @pl.loop(zed + 1, planes)
    def _(there):
        round_2(there, zed).wait_send()

    swap.wait()
    total = jnp.sum(sq_loc[...] + sq_far[...], axis=1, keepdims=True)
    scale = lax.rsqrt(total * (1.0 / (2 * chans)) + 1e-6)
    scale_ref[...] = jnp.broadcast_to(scale, (tok, LANES))


def finish(tok, chans, stream_ref, scale_ref, gain_ref, stream_hbm, normed_hbm, normed, sem):
    wide = SUB * LANES
    groups = chans // wide
    copies = [pltpu.make_async_copy(stream_ref, stream_hbm, sem.at[groups])]
    copies[0].start()
    scales = [scale_ref[pair * 2 * SUB : (pair + 1) * 2 * SUB, :] for pair in range(tok // (2 * SUB))]
    for g in range(groups):
        @pl.loop(g * SUB, (g + 1) * SUB)
        def _(t):
            cols = pl.ds(pl.multiple_of(t * LANES, LANES), LANES)
            gain = gain_ref[pl.ds(t, 1), :]
            for pair, scale in enumerate(scales):
                both = slice(pair * 2 * SUB, (pair + 1) * 2 * SUB)
                x = stream_ref[both, cols].astype(F32)
                normed[both, cols] = (x * scale * gain).astype(jnp.bfloat16)

        part = slice(g * wide, (g + 1) * wide)
        copy = pltpu.make_async_copy(normed.at[:, part], normed_hbm.at[:, part], sem.at[g])
        copy.start()
        copies.append(copy)
    for copy in copies:
        copy.wait()


def body(q_proj, k_proj, v_proj, resid, short_filter, residue, rate, gain, seg_lengths):
    tok, chans = q_proj.shape
    taps = short_filter.shape[1]
    modes = rate.shape[0]
    segs = seg_lengths.shape[0]
    shards = lax.axis_size("seq")
    planes = shards // PLANE
    tiles = chans // LANES
    groups = tiles // SUB
    blocks = tok // SUB
    part = tiles * modes // PLANE
    bf16 = jnp.bfloat16
    dims = (shards, planes, tok, chans, modes, taps, segs)
    vmem = pltpu.VMEM
    sem = pltpu.SemaphoreType.DMA
    hbm_spec = pl.BlockSpec(memory_space=pltpu.HBM)
    stream, scale, gain = pl.pallas_call(
        functools.partial(kernel, dims),
        out_shape=(
            jax.ShapeDtypeStruct((tok, chans), bf16),
            jax.ShapeDtypeStruct((tok, LANES), F32),
            jax.ShapeDtypeStruct((tiles, LANES), F32),
        ),
        in_specs=[hbm_spec] * 9,
        out_specs=(pl.BlockSpec(memory_space=vmem),) * 3,
        scratch_shapes=[
            vmem((tok, chans), bf16), vmem((tok, chans), bf16), vmem((tok, chans), bf16), vmem((tok, chans), bf16),
            vmem((3, taps, chans), F32), vmem((modes, chans), F32), vmem((modes, chans), F32),
            pltpu.SMEM((segs,), jnp.int32),
            vmem((SUB, chans), bf16), vmem((SUB, chans), bf16), vmem((SUB, chans), bf16),
            vmem((PLANE, 4, SUB, chans // PLANE), bf16), vmem((PLANE + 1, 4, SUB, chans // PLANE), bf16),
            vmem((2 * tiles * SUB, LANES), F32), vmem((2 * tiles * SUB, LANES), F32),
            vmem((tiles * modes, LANES), F32), vmem((tiles * modes, LANES), F32),
            vmem((SUB * modes, LANES), F32), vmem((2, SUB * SUB, LANES), F32),
            vmem(((blocks + 1) * tiles * SUB, LANES), F32),
            vmem(((blocks + 1) * tiles * SUB, LANES), F32),
            vmem(((blocks + 1) * tiles * SUB, LANES), F32),
            vmem((blocks * tiles * SUB, LANES), F32),
            vmem((blocks * tiles * SUB, LANES), F32),
            vmem((blocks * tiles * SUB, LANES), F32),
            vmem((3, tiles * SUB, LANES), F32),
            vmem((tiles * modes, LANES), F32), vmem((tiles * modes, LANES), F32), vmem((tiles * modes, LANES), F32),
            vmem((tiles * modes * SUB, LANES), F32), vmem((tiles * modes, LANES), F32),
            vmem((tok, LANES), F32), vmem((tok, LANES), F32), vmem((tok, LANES), F32),
            vmem((tiles * modes, LANES), F32),
            vmem((PLANE, part, LANES), bf16), vmem((PLANE, part, LANES), bf16),
            vmem((PLANE, part, LANES), F32), vmem((PLANE, part, LANES), F32),
            vmem((part, LANES), F32), vmem((planes, part, LANES), F32),
            vmem((PLANE, part, LANES), bf16), vmem((PLANE, part, LANES), bf16),
            vmem((tok, LANES), F32), vmem((tok, LANES), F32),
            sem((4, groups)), sem((5,)), sem((3,)), sem((3,)), sem((2, PLANE)), sem((PLANE + 1,)),
            sem((PLANE,)), sem((PLANE,)), sem((planes,)), sem((planes,)), sem((PLANE,)), sem((PLANE,)),
            sem, sem,
        ],
        compiler_params=pltpu.CompilerParams(
            collective_id=0, has_side_effects=True, vmem_limit_bytes=40 * 1024 * 1024
        ),
        name="hyena",
    )(*(pltpu.with_memory_space_constraint(x, pltpu.HBM) for x in (
        q_proj, k_proj, v_proj, resid, short_filter, residue, rate, gain.reshape(tiles, LANES), seg_lengths
    )))
    return pl.pallas_call(
        functools.partial(finish, tok, chans),
        out_shape=(jax.ShapeDtypeStruct((tok, chans), bf16),) * 2,
        in_specs=[pl.BlockSpec(memory_space=vmem)] * 3,
        out_specs=(hbm_spec,) * 2,
        scratch_shapes=[vmem((tok, chans), bf16), sem((chans // (SUB * LANES) + 1,))],
        compiler_params=pltpu.CompilerParams(vmem_limit_bytes=16 * 1024 * 1024),
        name="finish",
    )(stream, scale, gain)


def solution(mesh):
    placed = (
        P("seq", "chan"),
        P("seq", "chan"),
        P("seq", "chan"),
        P("seq", "chan"),
        P(None, None, "chan"),
        P(None, "chan"),
        P(None, "chan"),
        P("chan"),
        P(),
    )
    return jax.shard_map(
        body,
        mesh=mesh,
        in_specs=placed,
        out_specs=(P("seq", "chan"), P("seq", "chan")),
        check_vma=False,
    )
```

```python
import functools
import jax
import jax.numpy as jnp
from jax import lax
from jax.experimental import pallas as pl
from jax.experimental.pallas import tpu as pltpu
from jax.sharding import PartitionSpec as P

MESH = pl.DeviceIdType.MESH
PLANE = 16
LANES = 128
SUB = 8
F32 = jnp.float32


def kernel(
    dims,
    q_hbm, k_hbm, v_hbm, r_hbm, sf_hbm, residue_hbm, rate_hbm, gain_hbm, seg_hbm,
    stream_ref, scale_ref, gain_in,
    q_in, k_in, v_in, r_in, sf_in, residue_in, rate_in, seg_ref,
    rim_q, rim_k, rim_v, edge, edges, ek, ev, e_first, head_n, dec_own, taps_own,
    xq, xk, xv, zs, conv_std, qs_std,
    taps_t, rate_n, coef_n, dec_n, weights, dec8_n,
    keep_m, last_m, carry_m,
    e_loc, e_out, e_buf, pre_buf, reach_buf, total_buf, plane_buf, inc_out, inc_buf, sq_loc, sq_far,
    in_sem, param_sem, rim_send, rim_recv, edge_send, edge_recv, s1, r1, s2, r2, s3, r3, sq_send, sq_recv,
):
    shards, planes, tok, chans, modes, taps, segs = dims
    blocks = tok // SUB
    pairs = blocks // 2
    tiles = chans // LANES
    groups = tiles // SUB
    wide = SUB * LANES
    part = tiles * modes // PLANE
    me = lax.axis_index("seq")
    core = lax.axis_index("chan")
    zed = me // PLANE
    spot = lax.rem(me, PLANE)
    after = lax.rem(me + 1, shards)
    before = lax.rem(me + shards - 1, shards)

    def at(ref, start, size):
        return ref.at[pl.ds(pl.multiple_of(start, SUB), size)]

    params = [
        pltpu.make_async_copy(rate_hbm, rate_in, param_sem.at[0]),
        pltpu.make_async_copy(sf_hbm, sf_in, param_sem.at[1]),
        pltpu.make_async_copy(residue_hbm, residue_in, param_sem.at[2]),
        pltpu.make_async_copy(gain_hbm, gain_in, param_sem.at[3]),
        pltpu.make_async_copy(seg_hbm, seg_ref, param_sem.at[4]),
    ]

    def load(index, src, dst, g):
        cols = pl.ds(g * wide, wide)
        return pltpu.make_async_copy(src.at[:, cols], dst.at[:, cols], in_sem.at[index, g])

    for index in (4, 0, 1):
        params[index].start()
    for g in range(groups):
        load(1, k_hbm, k_in, g).start()
        load(2, v_hbm, v_in, g).start()
    for index in (2, 3):
        params[index].start()
    for g in range(groups):
        load(0, q_hbm, q_in, g).start()
    for g in range(groups):
        load(3, r_hbm, r_in, g).start()

    barrier = pltpu.get_barrier_semaphore()

    @pl.loop(1, PLANE)
    def _(step):
        other = zed * PLANE + lax.rem(spot + step, PLANE)
        pl.semaphore_signal(barrier, inc=1, device_id=(other, core), device_id_type=MESH)

    @pl.loop(1, planes)
    def _(step):
        other = lax.rem(zed + step, planes) * PLANE + spot
        pl.semaphore_signal(barrier, inc=1, device_id=(other, core), device_id_type=MESH)

    @pl.when(zed > 0)
    def _():
        last = (zed - 1) * PLANE + PLANE - 1
        pl.semaphore_signal(barrier, inc=1, device_id=(last, core), device_id_type=MESH)

    @pl.when(me > 0)
    def _():
        pl.semaphore_signal(barrier, inc=1, device_id=(before, core), device_id_type=MESH)

    pl.semaphore_signal(barrier, inc=1, device_id=(me, 1 - core), device_id_type=MESH)

    params[4].wait()
    first = me * tok
    ends = []
    running = seg_ref[0]
    ends.append(running)
    for j in range(1, segs):
        running = running + seg_ref[j]
        ends.append(running)
    big = jnp.int32(1 << 30)
    low = big
    low8 = big
    high = jnp.int32(-1)
    for end in ends:
        low = jnp.minimum(low, jnp.where(end >= first, end, big))
        low8 = jnp.minimum(low8, jnp.where(end >= first + SUB, end, big))
        high = jnp.maximum(high, jnp.where(end <= first + tok - 1, end, -1))
    rows = lax.broadcasted_iota(jnp.int32, (tok, LANES), 0) + first
    last_m[...] = jnp.where(rows >= high, 1.0, 0.0)
    carry_m[...] = jnp.where(rows < low8, 1.0, 0.0)
    carry_m[:SUB, :] = jnp.where(rows[:SUB] < low, 1.0, 0.0)

    params[0].wait()
    for t in range(tiles):
        rate = rate_in[:, t * LANES : (t + 1) * LANES]
        rate_n[t * modes : (t + 1) * modes, :] = rate
        dec_n[t * modes : (t + 1) * modes, :] = jnp.exp(-rate)
    params[1].wait()
    for a in (1, 2):
        for t in range(tiles):
            taps_t[a, t * SUB : t * SUB + taps, :] = sf_in[a, :, t * LANES : (t + 1) * LANES]

    def row_of(block, tile):
        return (block * tiles + tile) * SUB

    def relayout_tile(src, dst, g, pair, j):
        x = src[pl.ds(pl.multiple_of(pair * 2 * SUB, 2 * SUB), 2 * SUB),
                pl.ds(pl.multiple_of(g * wide + j * LANES, LANES), LANES)].astype(F32)
        lower = pl.multiple_of(row_of(2 * pair + 1, g * SUB + j), SUB)
        dst[pl.ds(lower, SUB), :] = x[:SUB]
        upper = pl.multiple_of(row_of(2 * pair + 2, g * SUB + j), SUB)
        dst[pl.ds(upper, SUB), :] = x[SUB:]

    def relayout(src, dst, g):
        @pl.loop(0, pairs)
        def _(pair):
            for j in range(SUB):
                relayout_tile(src, dst, g, pair, j)

    def relayout_rim(src, dst):
        for t in range(tiles):
            x = src[:, t * LANES : (t + 1) * LANES].astype(F32)
            dst[t * SUB : (t + 1) * SUB, :] = jnp.where(me > 0, x, 0.0)

    def token(ref, block, g, s):
        return ref[pl.ds(row_of(block, g * SUB) + s, SUB, stride=SUB), :]

    def per_mode(ref, g, m):
        return ref[pl.ds(g * SUB * modes + m, SUB, stride=modes), :]

    def taps_of(a, g):
        return [taps_t[a, pl.ds(g * SUB * SUB + j, SUB, stride=SUB), :] for j in range(taps)]

    def fir(window, weight):
        out = weight[0] * window[-1]
        for j in range(1, taps):
            out = out + weight[j] * window[-1 - j]
        return out

    def z_rows(t, g):
        return pl.ds(pl.multiple_of((t * groups + g) * SUB, SUB), SUB)

    def block_of_z(block, g, k_win, v_win, state, k_taps, v_taps, decay, beside=None):
        k_win, v_win, state = list(k_win), list(v_win), list(state)
        for s in range(SUB):
            if beside is not None:
                beside(s)
            k_win.append(token(xk, block, g, s))
            v_win.append(token(xv, block, g, s))
            z = fir(k_win[-taps:], k_taps) * fir(v_win[-taps:], v_taps)
            t = (block - 1) * SUB + s
            zs[z_rows(t, g), :] = z
            z = z * last_m[pl.ds(t, 1), :]
            state = [d * old + z for d, old in zip(decay, state)]
        return k_win[1 - taps :], v_win[1 - taps :], state

    zero = jnp.zeros((SUB, LANES), F32)

    load(1, k_hbm, k_in, 0).wait()
    load(2, v_hbm, v_in, 0).wait()
    for j in range(SUB):
        relayout_tile(k_in, xk, 0, 0, j)
        relayout_tile(v_in, xv, 0, 0, j)

    for g in range(groups - 1):
        load(1, k_hbm, k_in, g + 1).wait()
        load(2, v_hbm, v_in, g + 1).wait()

    def end_states(g):
        k_taps, v_taps = taps_of(1, g), taps_of(2, g)
        decay = [per_mode(dec_n, g, m) for m in range(modes)]
        behind = range(SUB - taps + 1, SUB)

        def ahead(pair, half):
            after_it = jnp.minimum(g * pairs + pair + 1, groups * pairs - 1)
            g_next, pair_next = after_it // pairs, lax.rem(after_it, pairs)

            def one(s):
                src, dst = ((k_in, xk), (v_in, xv))[s % 2]
                if half is None:
                    relayout_tile(k_in, xk, g_next, pair_next, s)
                    relayout_tile(v_in, xv, g_next, pair_next, s)
                else:
                    relayout_tile(src, dst, g_next, pair_next, half * SUB // 2 + s // 2)

            return one

        start = block_of_z(
            2, g, [token(xk, 1, g, s) for s in behind], [token(xv, 1, g, s) for s in behind],
            [zero] * modes, k_taps, v_taps, decay, ahead(0, None),
        )

        def step(pair, carried):
            for half in range(2):
                carried = block_of_z(
                    2 * pair + 1 + half, g, *carried, k_taps, v_taps, decay, ahead(pair, half)
                )
            return carried

        _, _, state = lax.fori_loop(1, pairs, step, start)
        for m in range(modes):
            e_loc[pl.ds(g * SUB * modes + m, SUB, stride=modes), :] = state[m]

    side = 4

    def nth(i, j):
        near = lambda n: (n * (n + 1) // 2) % side
        y = lax.rem(spot // side + near(i), side)
        x = lax.rem(spot + near(j), side)
        return y * side + x

    def nth_of(n):
        return nth(n // side, lax.rem(n, side))

    @pl.loop(0, groups // 2)
    def _(g):
        end_states(g)

    owned = chans // PLANE
    for owner in range(PLANE):
        cols = slice(owner * owned, (owner + 1) * owned)
        edge[owner, 0] = k_in[tok - SUB : tok, cols]
        edge[owner, 1] = v_in[tok - SUB : tok, cols]
        edge[owner, 2] = k_in[0:SUB, cols]
        edge[owner, 3] = v_in[0:SUB, cols]

    crossing = ((spot + 1) // PLANE) * ((2 * planes - 3 - zed) // (planes - 1))
    crosses = crossing > 0
    pl.semaphore_wait(barrier, PLANE - 1 + planes - 1 + 1 + (2 * shards - 3 - me) // (shards - 1) + PLANE * crossing)

    def edge_copy(owner, slot, plane, kind):
        return pltpu.make_async_remote_copy(
            src_ref=edge.at[owner], dst_ref=edges.at[slot],
            send_sem=edge_send.at[kind, owner], recv_sem=edge_recv.at[slot],
            device_id=(plane * PLANE + owner, core), device_id_type=MESH,
        )

    @pl.loop(1, PLANE)
    def _(step):
        edge_copy(nth_of(PLANE - step), spot, zed, 0).start()

    @pl.when(crosses)
    def _():
        @pl.loop(0, PLANE)
        def _(owner):
            edge_copy(owner, PLANE, zed + 1, 1).start()

    edges[spot] = edge[spot]

    @pl.when(zed == 0)
    def _():
        edges[PLANE] = jnp.zeros_like(edges[PLANE])

    @pl.loop(groups // 2, groups)
    def _(g):
        end_states(g)

    def round_1(other):
        return pltpu.make_async_remote_copy(
            src_ref=e_out.at[other], dst_ref=e_buf.at[spot],
            send_sem=s1.at[other], recv_sem=r1.at[spot],
            device_id=(zed * PLANE + other, core), device_id_type=MESH,
        )

    def arrival_1(other):
        return pltpu.make_async_remote_copy(
            src_ref=e_out.at[other], dst_ref=e_buf.at[other],
            send_sem=s1.at[other], recv_sem=r1.at[other],
            device_id=(zed * PLANE + other, core), device_id_type=MESH,
        )

    for other in range(PLANE):
        e_out[other] = e_loc[other * part : (other + 1) * part, :].astype(jnp.bfloat16)

    @pl.loop(1, PLANE)
    def _(step):
        round_1(nth_of(PLANE - step)).start()

    def rim_copy(index, src, dst):
        return pltpu.make_async_remote_copy(
            src_ref=src.at[pl.ds(tok - SUB, SUB)], dst_ref=dst,
            send_sem=rim_send.at[index], recv_sem=rim_recv.at[index],
            device_id=(after, core), device_id_type=MESH,
        )

    rims = [rim_copy(0, k_hbm, rim_k), rim_copy(1, v_hbm, rim_v), rim_copy(2, q_hbm, rim_q)]
    @pl.when(me < shards - 1)
    def _():
        for copy in rims:
            copy.start()

    @pl.when(me == 0)
    def _():
        for rim in (rim_k, rim_v, rim_q):
            rim[...] = jnp.zeros_like(rim)

    e_buf[spot] = e_out[spot]

    begins = rows == 0
    for end in ends:
        begins = begins | (rows == end)
    keep_m[...] = jnp.where(begins, 0.0, 1.0)
    for t in range(tiles):
        taps_t[0, t * SUB : t * SUB + taps, :] = sf_in[0, :, t * LANES : (t + 1) * LANES]
    params[2].wait()
    params[3].wait()
    for t in range(tiles):
        x = -2.0 * rate_n[t * modes : (t + 1) * modes, :]
        series = 1.0 + x * (1.0 / 6.0)
        for n in (5.0, 4.0, 3.0, 2.0):
            series = 1.0 + x * (1.0 / n) * series
        coef_n[t * modes : (t + 1) * modes, :] = residue_in[:, t * LANES : (t + 1) * LANES] * jnp.sqrt(-x * series)

    @pl.loop(0, groups)
    def _(g):
        load(0, q_hbm, q_in, g).wait()
        relayout(q_in, xq, g)

    rising = (lax.broadcasted_iota(jnp.int32, (SUB, LANES), 0) + 1).astype(F32)

    @pl.loop(0, tiles)
    def _(t):
        for m in range(modes):
            rate = rate_n[pl.ds(t * modes + m, 1), :]
            coef = coef_n[pl.ds(t * modes + m, 1), :]
            here = pl.ds(pl.multiple_of((t * modes + m) * SUB, SUB), SUB)
            weights[here, :] = coef * jnp.exp(-rate * rising)
        whole = pl.ds(pl.multiple_of(t * modes, SUB), modes)
        dec8_n[whole, :] = jnp.exp(rate_n[whole, :] * float(-SUB))

    def tree(terms):
        while len(terms) > 1:
            terms = [a + b for a, b in zip(terms[::2], terms[1::2])]
        return terms[0]

    def conv_block(block, g, q_win, state, q_taps, decay, coef, z_of):
        q_win, state = list(q_win), list(state)
        for s in range(SUB):
            q_win.append(token(xq, block, g, s))
            qs = fir(q_win[-taps:], q_taps)
            t = (block - 1) * SUB + s
            z = z_of(t, s)
            keep = keep_m[pl.ds(t, 1), :]
            state = [(d * keep) * old + z for d, old in zip(decay, state)]
            out = tree([c * part for c, part in zip(coef, state)])
            there = pl.ds(row_of(block - 1, g * SUB) + s, SUB, stride=SUB)
            conv_std[there, :] = out * qs
            qs_std[there, :] = qs * carry_m[pl.ds(t, 1), :]
        return q_win[1 - taps :], state

    behind = range(SUB - taps + 1, SUB)

    def inner(g):
        q_taps = taps_of(0, g)
        decay = [per_mode(dec_n, g, m) for m in range(modes)]
        coef = [per_mode(coef_n, g, m) for m in range(modes)]

        def step(block, carried):
            return conv_block(block, g, *carried, q_taps, decay, coef, lambda t, s: zs[z_rows(t, g), :])

        lax.fori_loop(2, blocks + 1, step, ([token(xq, 1, g, s) for s in behind], [zero] * modes))

    def head(g):
        windows = [[token(x, 0, g, s) for s in behind] for x in (xk, xv)]
        weight = [taps_of(1, g), taps_of(2, g)]

        def z_of(t, s):
            for window, x in zip(windows, (xk, xv)):
                window.append(token(x, 1, g, s))
            return fir(windows[0][-taps:], weight[0]) * fir(windows[1][-taps:], weight[1])

        decay = [per_mode(dec_n, g, m) for m in range(modes)]
        coef = [per_mode(coef_n, g, m) for m in range(modes)]
        _, state = conv_block(
            1, g, [token(xq, 0, g, s) for s in behind], [zero] * modes, taps_of(0, g), decay, coef, z_of
        )
        for m in range(modes):
            head_n[pl.ds(g * SUB * modes + m, SUB, stride=modes), :] = state[m]

    inner(0)

    per = tiles // PLANE
    my_rate = at(rate_n, spot * part, part)[...]
    for i in range(SUB):
        source = pl.multiple_of((spot * per + i % per) * SUB, SUB)
        dec_own[i * SUB : (i + 1) * SUB, :] = dec_n[pl.ds(source, SUB), :]
        for a in (1, 2):
            taps_own[a - 1, i * SUB : (i + 1) * SUB, :] = taps_t[a, pl.ds(source, SUB), :]
    own_decay = [dec_own[pl.ds(m, SUB, stride=modes), :] for m in range(modes)]
    own_taps = [[taps_own[a, pl.ds(j, SUB, stride=SUB), :] for j in range(taps)] for a in range(2)]

    @pl.loop(1, PLANE)
    def _(step):
        source = lax.rem(spot + step, PLANE)
        edge_copy(source, source, zed, 0).wait_recv()

    @pl.when(zed > 0)
    def _():
        edge_copy(spot, PLANE, zed, 1).wait_recv()

    for j in range(PLANE):
        for a, dst in ((0, ek), (1, ev)):
            past = edges[(j + PLANE) % (PLANE + 1), a].astype(F32)
            here = edges[j, a + 2].astype(F32)
            for i in range(per):
                tile = j * per + i
                dst[row_of(0, tile) : row_of(0, tile) + SUB, :] = past[:, i * LANES : (i + 1) * LANES]
                dst[row_of(1, tile) : row_of(1, tile) + SUB, :] = here[:, i * LANES : (i + 1) * LANES]

    for g in range(groups):
        shard = zed * PLANE + (lax.broadcasted_iota(jnp.int32, (SUB, LANES), 0) + g * SUB) // per
        begin = shard * tok
        latest = jnp.full((SUB, LANES), -1, jnp.int32)
        for end in ends:
            latest = jnp.maximum(latest, jnp.where(end <= begin + (tok - 1), end, -1))
        window = [[token(x, 0, g, s) for s in range(SUB - taps + 1, SUB)] for x in (ek, ev)]
        state = [zero] * modes
        for s in range(SUB):
            window[0].append(token(ek, 1, g, s))
            window[1].append(token(ev, 1, g, s))
            z = fir(window[0][-taps:], own_taps[0]) * fir(window[1][-taps:], own_taps[1])
            z = jnp.where(begin + s >= latest, z, 0.0)
            state = [d * old + z for d, old in zip(own_decay, state)]
        for m in range(modes):
            e_first[pl.ds(g * SUB * modes + m, SUB, stride=modes), :] = state[m]

    @pl.loop(1, PLANE)
    def _(step):
        arrival_1(lax.rem(spot + step, PLANE)).wait_recv()

    span = jnp.exp(my_rate * float(-tok))
    spot_rows = lax.broadcasted_iota(jnp.int32, (PLANE, LANES), 0) + zed * PLANE
    plane_rows = lax.broadcasted_iota(jnp.int32, (SUB, LANES), 0)
    open_here = jnp.ones((PLANE, LANES), F32)
    open_plane = jnp.ones((SUB, LANES), F32)
    for end in ends:
        open_here = jnp.where(spot_rows == end // tok, 0.0, open_here)
        open_plane = jnp.where(plane_rows == end // (tok * PLANE), 0.0, open_plane)

    rest = jnp.exp(my_rate * float(SUB - tok))
    state = jnp.zeros_like(span)
    reach = jnp.ones_like(span)
    for other in range(PLANE):
        pre_buf[other] = state
        reach_buf[other] = reach
        factor = span * open_here[other : other + 1]
        state = factor * state + e_buf[other].astype(F32) + rest * e_first[other * part : (other + 1) * part, :]
        reach = factor * reach
    total_buf[...] = state

    def round_2(there, slot):
        return pltpu.make_async_remote_copy(
            src_ref=total_buf, dst_ref=plane_buf.at[slot],
            send_sem=s2.at[there], recv_sem=r2.at[slot],
            device_id=(there * PLANE + spot, core), device_id_type=MESH,
        )

    @pl.loop(zed + 1, planes)
    def _(there):
        round_2(there, zed).start()

    @pl.loop(1, groups - 1)
    def _(g):
        inner(g)

    plane_span = jnp.exp(my_rate * float(-tok * PLANE))

    def plane_step(there, state):
        round_2(there, there).wait_recv()
        row = jnp.sum(jnp.where(plane_rows == there, open_plane, 0.0), axis=0, keepdims=True)
        return plane_span * row * state + plane_buf[there]

    state = lax.fori_loop(0, zed, plane_step, jnp.zeros_like(span))
    def round_3(other, slot):
        return pltpu.make_async_remote_copy(
            src_ref=inc_out.at[other], dst_ref=inc_buf.at[slot],
            send_sem=s3.at[other], recv_sem=r3.at[slot],
            device_id=(zed * PLANE + other, core), device_id_type=MESH,
        )

    @pl.loop(1, PLANE)
    def _(step):
        other = nth_of(PLANE - step)
        inc_out[other] = (pre_buf[other] + reach_buf[other] * state).astype(jnp.bfloat16)
        round_3(other, spot).start()

    inc_buf[spot] = (pre_buf[spot] + reach_buf[spot] * state).astype(jnp.bfloat16)

    inner(groups - 1)

    for g in range(groups):
        load(3, r_hbm, r_in, g).wait()

    def add_residual(begin, end):
        @pl.loop(0, tiles)
        def _(t):
            cols = pl.ds(pl.multiple_of(t * LANES, LANES), LANES)
            for pair in range(begin, end):
                x = r_in[pair * 2 * SUB : (pair + 1) * 2 * SUB, cols].astype(F32)
                for half in range(2):
                    here = pl.ds(pl.multiple_of(row_of(2 * pair + half, t), SUB), SUB)
                    conv_std[here, :] = conv_std[here, :] + x[half * SUB : (half + 1) * SUB]

    add_residual(1, pairs)
    sq_loc[...] = jnp.zeros_like(sq_loc)

    @pl.loop(1, PLANE)
    def _(step):
        other = lax.rem(spot + step, PLANE)
        round_1(other).wait_send()
        edge_copy(other, spot, zed, 0).wait_send()

    @pl.when(crosses)
    def _():
        @pl.loop(0, PLANE)
        def _(owner):
            edge_copy(owner, PLANE, zed + 1, 1).wait_send()

    @pl.loop(zed + 1, planes)
    def _(there):
        round_2(there, zed).wait_send()

    for copy, rim, dst in zip(rims, (rim_k, rim_v, rim_q), (xk, xv, xq)):
        pl.when(me > 0)(copy.wait_recv)
        relayout_rim(rim, dst)

    @pl.loop(0, groups)
    def _(g):
        head(g)

    add_residual(0, 1)


    def tile_of(slot, local):
        t = slot * per + local
        whole = pl.ds(pl.multiple_of(t * modes, SUB), modes)
        incoming = inc_buf[slot].astype(F32)[local * modes : (local + 1) * modes]
        at_8 = dec8_n[whole, :] * carry_m[SUB - 1 : SUB, :] * incoming + head_n[whole, :]
        value, later, decay = [], [], []
        for m in range(modes):
            here = pl.ds(pl.multiple_of((t * modes + m) * SUB, SUB), SUB)
            weight = weights[here, :]
            value.append(weight * incoming[m : m + 1])
            later.append(weight * at_8[m : m + 1])
            decay.append(jnp.broadcast_to(dec8_n[pl.ds(t * modes + m, 1), :], (SUB, LANES)))
        cols = pl.ds(pl.multiple_of(t * LANES, LANES), LANES)
        for pair in range(pairs):
            halves = []
            for block in (2 * pair, 2 * pair + 1):
                carried = tree(value)
                if block == 0:
                    value = later
                elif block < blocks - 1:
                    value = [v * d for v, d in zip(value, decay)]
                here = pl.ds(pl.multiple_of(row_of(block, t), SUB), SUB)
                halves.append(conv_std[here, :] + qs_std[here, :] * carried)
            both = pl.ds(pair * 2 * SUB, 2 * SUB)
            stream = jnp.concatenate(halves, axis=0).astype(jnp.bfloat16)
            stream_ref[both, cols] = stream
            back = stream.astype(F32)
            sq_loc[both, :] = sq_loc[both, :] + back * back

    @pl.loop(0, PLANE)
    def _(n):
        slot = nth_of(n)

        @pl.when(n > 0)
        def _():
            round_3(slot, slot).wait_recv()

        for local in range(per):
            tile_of(slot, local)

    swap = pltpu.make_async_remote_copy(
        src_ref=sq_loc, dst_ref=sq_far, send_sem=sq_send, recv_sem=sq_recv,
        device_id=(me, 1 - core), device_id_type=MESH,
    )
    swap.start()

    @pl.when(me < shards - 1)
    def _():
        for copy in rims:
            copy.wait_send()

    @pl.loop(1, PLANE)
    def _(step):
        other = lax.rem(spot + step, PLANE)
        round_3(other, spot).wait_send()

    swap.wait()
    total = jnp.sum(sq_loc[...] + sq_far[...], axis=1, keepdims=True)
    scale = lax.rsqrt(total * (1.0 / (2 * chans)) + 1e-6)
    scale_ref[...] = jnp.broadcast_to(scale, (tok, LANES))


def finish(tok, chans, stream_ref, scale_ref, gain_ref, stream_hbm, normed_hbm, normed, sem):
    wide = SUB * LANES
    groups = chans // wide
    copies = [pltpu.make_async_copy(stream_ref, stream_hbm, sem.at[groups])]
    copies[0].start()
    scales = [scale_ref[pair * 2 * SUB : (pair + 1) * 2 * SUB, :] for pair in range(tok // (2 * SUB))]
    for g in range(groups):
        @pl.loop(g * SUB, (g + 1) * SUB)
        def _(t):
            cols = pl.ds(pl.multiple_of(t * LANES, LANES), LANES)
            gain = gain_ref[pl.ds(t, 1), :]
            for pair, scale in enumerate(scales):
                both = slice(pair * 2 * SUB, (pair + 1) * 2 * SUB)
                x = stream_ref[both, cols].astype(F32)
                normed[both, cols] = (x * scale * gain).astype(jnp.bfloat16)

        part = slice(g * wide, (g + 1) * wide)
        copy = pltpu.make_async_copy(normed.at[:, part], normed_hbm.at[:, part], sem.at[g])
        copy.start()
        copies.append(copy)
    for copy in copies:
        copy.wait()


def body(q_proj, k_proj, v_proj, resid, short_filter, residue, rate, gain, seg_lengths):
    tok, chans = q_proj.shape
    taps = short_filter.shape[1]
    modes = rate.shape[0]
    segs = seg_lengths.shape[0]
    shards = lax.axis_size("seq")
    planes = shards // PLANE
    tiles = chans // LANES
    groups = tiles // SUB
    blocks = tok // SUB
    part = tiles * modes // PLANE
    bf16 = jnp.bfloat16
    dims = (shards, planes, tok, chans, modes, taps, segs)
    vmem = pltpu.VMEM
    sem = pltpu.SemaphoreType.DMA
    hbm_spec = pl.BlockSpec(memory_space=pltpu.HBM)
    stream, scale, gain = pl.pallas_call(
        functools.partial(kernel, dims),
        out_shape=(
            jax.ShapeDtypeStruct((tok, chans), bf16),
            jax.ShapeDtypeStruct((tok, LANES), F32),
            jax.ShapeDtypeStruct((tiles, LANES), F32),
        ),
        in_specs=[hbm_spec] * 9,
        out_specs=(pl.BlockSpec(memory_space=vmem),) * 3,
        scratch_shapes=[
            vmem((tok, chans), bf16), vmem((tok, chans), bf16), vmem((tok, chans), bf16), vmem((tok, chans), bf16),
            vmem((3, taps, chans), F32), vmem((modes, chans), F32), vmem((modes, chans), F32),
            pltpu.SMEM((segs,), jnp.int32),
            vmem((SUB, chans), bf16), vmem((SUB, chans), bf16), vmem((SUB, chans), bf16),
            vmem((PLANE, 4, SUB, chans // PLANE), bf16), vmem((PLANE + 1, 4, SUB, chans // PLANE), bf16),
            vmem((2 * tiles * SUB, LANES), F32), vmem((2 * tiles * SUB, LANES), F32),
            vmem((tiles * modes, LANES), F32), vmem((tiles * modes, LANES), F32),
            vmem((SUB * modes, LANES), F32), vmem((2, SUB * SUB, LANES), F32),
            vmem(((blocks + 1) * tiles * SUB, LANES), F32),
            vmem(((blocks + 1) * tiles * SUB, LANES), F32),
            vmem(((blocks + 1) * tiles * SUB, LANES), F32),
            vmem((blocks * tiles * SUB, LANES), F32),
            vmem((blocks * tiles * SUB, LANES), F32),
            vmem((blocks * tiles * SUB, LANES), F32),
            vmem((3, tiles * SUB, LANES), F32),
            vmem((tiles * modes, LANES), F32), vmem((tiles * modes, LANES), F32), vmem((tiles * modes, LANES), F32),
            vmem((tiles * modes * SUB, LANES), F32), vmem((tiles * modes, LANES), F32),
            vmem((tok, LANES), F32), vmem((tok, LANES), F32), vmem((tok, LANES), F32),
            vmem((tiles * modes, LANES), F32),
            vmem((PLANE, part, LANES), bf16), vmem((PLANE, part, LANES), bf16),
            vmem((PLANE, part, LANES), F32), vmem((PLANE, part, LANES), F32),
            vmem((part, LANES), F32), vmem((planes, part, LANES), F32),
            vmem((PLANE, part, LANES), bf16), vmem((PLANE, part, LANES), bf16),
            vmem((tok, LANES), F32), vmem((tok, LANES), F32),
            sem((4, groups)), sem((5,)), sem((3,)), sem((3,)), sem((2, PLANE)), sem((PLANE + 1,)),
            sem((PLANE,)), sem((PLANE,)), sem((planes,)), sem((planes,)), sem((PLANE,)), sem((PLANE,)),
            sem, sem,
        ],
        compiler_params=pltpu.CompilerParams(
            collective_id=0, has_side_effects=True, vmem_limit_bytes=40 * 1024 * 1024
        ),
        name="hyena",
    )(*(pltpu.with_memory_space_constraint(x, pltpu.HBM) for x in (
        q_proj, k_proj, v_proj, resid, short_filter, residue, rate, gain.reshape(tiles, LANES), seg_lengths
    )))
    return pl.pallas_call(
        functools.partial(finish, tok, chans),
        out_shape=(jax.ShapeDtypeStruct((tok, chans), bf16),) * 2,
        in_specs=[pl.BlockSpec(memory_space=vmem)] * 3,
        out_specs=(hbm_spec,) * 2,
        scratch_shapes=[vmem((tok, chans), bf16), sem((chans // (SUB * LANES) + 1,))],
        compiler_params=pltpu.CompilerParams(vmem_limit_bytes=16 * 1024 * 1024),
        name="finish",
    )(stream, scale, gain)


def solution(mesh):
    placed = (
        P("seq", "chan"),
        P("seq", "chan"),
        P("seq", "chan"),
        P("seq", "chan"),
        P(None, None, "chan"),
        P(None, "chan"),
        P(None, "chan"),
        P("chan"),
        P(),
    )
    return jax.shard_map(
        body,
        mesh=mesh,
        in_specs=placed,
        out_specs=(P("seq", "chan"), P("seq", "chan")),
        check_vma=False,
    )
```

```python
import functools
import jax
import jax.numpy as jnp
from jax import lax
from jax.experimental import pallas as pl
from jax.experimental.pallas import tpu as pltpu
from jax.sharding import PartitionSpec as P

MESH = pl.DeviceIdType.MESH
PLANE = 16
LANES = 128
SUB = 8
F32 = jnp.float32


def kernel(
    dims,
    q_hbm, k_hbm, v_hbm, r_hbm, sf_hbm, residue_hbm, rate_hbm, gain_hbm, seg_hbm,
    stream_ref, scale_ref, gain_in,
    q_in, k_in, v_in, r_in, sf_in, residue_in, rate_in, seg_ref,
    rim_q, rim_k, rim_v, edge, edges, ek, ev, e_first, head_n, dec_own, taps_own,
    xq, xk, xv, zs, conv_std, qs_std,
    taps_t, rate_n, coef_n, dec_n, weights, dec8_n,
    keep_m, last_m, carry_m,
    e_loc, e_out, e_buf, pre_buf, reach_buf, total_buf, plane_buf, inc_out, inc_buf, sq_loc, sq_far,
    in_sem, param_sem, rim_send, rim_recv, edge_send, edge_recv, s1, r1, s2, r2, s3, r3, sq_send, sq_recv,
):
    shards, planes, tok, chans, modes, taps, segs = dims
    blocks = tok // SUB
    pairs = blocks // 2
    tiles = chans // LANES
    groups = tiles // SUB
    wide = SUB * LANES
    part = tiles * modes // PLANE
    me = lax.axis_index("seq")
    core = lax.axis_index("chan")
    zed = me // PLANE
    spot = lax.rem(me, PLANE)
    after = lax.rem(me + 1, shards)
    before = lax.rem(me + shards - 1, shards)

    def at(ref, start, size):
        return ref.at[pl.ds(pl.multiple_of(start, SUB), size)]

    params = [
        pltpu.make_async_copy(rate_hbm, rate_in, param_sem.at[0]),
        pltpu.make_async_copy(sf_hbm, sf_in, param_sem.at[1]),
        pltpu.make_async_copy(residue_hbm, residue_in, param_sem.at[2]),
        pltpu.make_async_copy(gain_hbm, gain_in, param_sem.at[3]),
        pltpu.make_async_copy(seg_hbm, seg_ref, param_sem.at[4]),
    ]

    def load(index, src, dst, g):
        cols = pl.ds(g * wide, wide)
        return pltpu.make_async_copy(src.at[:, cols], dst.at[:, cols], in_sem.at[index, g])

    for index in (4, 0, 1):
        params[index].start()
    for g in range(groups):
        load(1, k_hbm, k_in, g).start()
        load(2, v_hbm, v_in, g).start()
    for index in (2, 3):
        params[index].start()
    for g in range(groups):
        load(0, q_hbm, q_in, g).start()
    for g in range(groups):
        load(3, r_hbm, r_in, g).start()

    barrier = pltpu.get_barrier_semaphore()

    @pl.loop(1, PLANE)
    def _(step):
        other = zed * PLANE + lax.rem(spot + step, PLANE)
        pl.semaphore_signal(barrier, inc=1, device_id=(other, core), device_id_type=MESH)

    @pl.loop(1, planes)
    def _(step):
        other = lax.rem(zed + step, planes) * PLANE + spot
        pl.semaphore_signal(barrier, inc=1, device_id=(other, core), device_id_type=MESH)

    @pl.when(zed > 0)
    def _():
        last = (zed - 1) * PLANE + PLANE - 1
        pl.semaphore_signal(barrier, inc=1, device_id=(last, core), device_id_type=MESH)

    @pl.when(me > 0)
    def _():
        pl.semaphore_signal(barrier, inc=1, device_id=(before, core), device_id_type=MESH)

    pl.semaphore_signal(barrier, inc=1, device_id=(me, 1 - core), device_id_type=MESH)

    params[4].wait()
    first = me * tok
    ends = []
    running = seg_ref[0]
    ends.append(running)
    for j in range(1, segs):
        running = running + seg_ref[j]
        ends.append(running)
    big = jnp.int32(1 << 30)
    low = big
    low8 = big
    high = jnp.int32(-1)
    for end in ends:
        low = jnp.minimum(low, jnp.where(end >= first, end, big))
        low8 = jnp.minimum(low8, jnp.where(end >= first + SUB, end, big))
        high = jnp.maximum(high, jnp.where(end <= first + tok - 1, end, -1))
    rows = lax.broadcasted_iota(jnp.int32, (tok, LANES), 0) + first
    last_m[...] = jnp.where(rows >= high, 1.0, 0.0)
    carry_m[...] = jnp.where(rows < low8, 1.0, 0.0)
    carry_m[:SUB, :] = jnp.where(rows[:SUB] < low, 1.0, 0.0)

    params[0].wait()
    for t in range(tiles):
        rate = rate_in[:, t * LANES : (t + 1) * LANES]
        rate_n[t * modes : (t + 1) * modes, :] = rate
        dec_n[t * modes : (t + 1) * modes, :] = jnp.exp(-rate)
    params[1].wait()
    for a in (1, 2):
        for t in range(tiles):
            taps_t[a, t * SUB : t * SUB + taps, :] = sf_in[a, :, t * LANES : (t + 1) * LANES]

    def row_of(block, tile):
        return (block * tiles + tile) * SUB

    def relayout_tile(src, dst, g, pair, j):
        x = src[pl.ds(pl.multiple_of(pair * 2 * SUB, 2 * SUB), 2 * SUB),
                pl.ds(pl.multiple_of(g * wide + j * LANES, LANES), LANES)].astype(F32)
        lower = pl.multiple_of(row_of(2 * pair + 1, g * SUB + j), SUB)
        dst[pl.ds(lower, SUB), :] = x[:SUB]
        upper = pl.multiple_of(row_of(2 * pair + 2, g * SUB + j), SUB)
        dst[pl.ds(upper, SUB), :] = x[SUB:]

    def relayout(src, dst, g):
        @pl.loop(0, pairs)
        def _(pair):
            for j in range(SUB):
                relayout_tile(src, dst, g, pair, j)

    def relayout_rim(src, dst):
        for t in range(tiles):
            x = src[:, t * LANES : (t + 1) * LANES].astype(F32)
            dst[t * SUB : (t + 1) * SUB, :] = jnp.where(me > 0, x, 0.0)

    def token(ref, block, g, s):
        return ref[pl.ds(row_of(block, g * SUB) + s, SUB, stride=SUB), :]

    def per_mode(ref, g, m):
        return ref[pl.ds(g * SUB * modes + m, SUB, stride=modes), :]

    def taps_of(a, g):
        return [taps_t[a, pl.ds(g * SUB * SUB + j, SUB, stride=SUB), :] for j in range(taps)]

    def fir(window, weight):
        out = weight[0] * window[-1]
        for j in range(1, taps):
            out = out + weight[j] * window[-1 - j]
        return out

    def z_rows(t, g):
        return pl.ds(pl.multiple_of((t * groups + g) * SUB, SUB), SUB)

    def block_of_z(block, g, k_win, v_win, state, k_taps, v_taps, decay, beside=None):
        k_win, v_win, state = list(k_win), list(v_win), list(state)
        for s in range(SUB):
            if beside is not None:
                beside(s)
            k_win.append(token(xk, block, g, s))
            v_win.append(token(xv, block, g, s))
            z = fir(k_win[-taps:], k_taps) * fir(v_win[-taps:], v_taps)
            t = (block - 1) * SUB + s
            zs[z_rows(t, g), :] = z
            z = z * last_m[pl.ds(t, 1), :]
            state = [d * old + z for d, old in zip(decay, state)]
        return k_win[1 - taps :], v_win[1 - taps :], state

    zero = jnp.zeros((SUB, LANES), F32)

    load(1, k_hbm, k_in, 0).wait()
    load(2, v_hbm, v_in, 0).wait()
    for j in range(SUB):
        relayout_tile(k_in, xk, 0, 0, j)
        relayout_tile(v_in, xv, 0, 0, j)

    for g in range(groups - 1):
        load(1, k_hbm, k_in, g + 1).wait()
        load(2, v_hbm, v_in, g + 1).wait()

    def end_states(g):
        k_taps, v_taps = taps_of(1, g), taps_of(2, g)
        decay = [per_mode(dec_n, g, m) for m in range(modes)]
        behind = range(SUB - taps + 1, SUB)

        def ahead(pair, half):
            after_it = jnp.minimum(g * pairs + pair + 1, groups * pairs - 1)
            g_next, pair_next = after_it // pairs, lax.rem(after_it, pairs)

            def one(s):
                src, dst = ((k_in, xk), (v_in, xv))[s % 2]
                if half is None:
                    relayout_tile(k_in, xk, g_next, pair_next, s)
                    relayout_tile(v_in, xv, g_next, pair_next, s)
                else:
                    relayout_tile(src, dst, g_next, pair_next, half * SUB // 2 + s // 2)

            return one

        start = block_of_z(
            2, g, [token(xk, 1, g, s) for s in behind], [token(xv, 1, g, s) for s in behind],
            [zero] * modes, k_taps, v_taps, decay, ahead(0, None),
        )

        def step(pair, carried):
            for half in range(2):
                carried = block_of_z(
                    2 * pair + 1 + half, g, *carried, k_taps, v_taps, decay, ahead(pair, half)
                )
            return carried

        _, _, state = lax.fori_loop(1, pairs, step, start)
        for m in range(modes):
            e_loc[pl.ds(g * SUB * modes + m, SUB, stride=modes), :] = state[m]

    side = 4

    def nth(i, j):
        near = lambda n: (n * (n + 1) // 2) % side
        y = lax.rem(spot // side + near(i), side)
        x = lax.rem(spot + near(j), side)
        return y * side + x

    def nth_of(n):
        return nth(n // side, lax.rem(n, side))

    @pl.loop(0, groups // 2)
    def _(g):
        end_states(g)

    owned = chans // PLANE
    for owner in range(PLANE):
        cols = slice(owner * owned, (owner + 1) * owned)
        edge[owner, 0] = k_in[tok - SUB : tok, cols]
        edge[owner, 1] = v_in[tok - SUB : tok, cols]
        edge[owner, 2] = k_in[0:SUB, cols]
        edge[owner, 3] = v_in[0:SUB, cols]

    crossing = ((spot + 1) // PLANE) * ((2 * planes - 3 - zed) // (planes - 1))
    crosses = crossing > 0
    pl.semaphore_wait(barrier, PLANE - 1 + planes - 1 + 1 + (2 * shards - 3 - me) // (shards - 1) + PLANE * crossing)

    def edge_copy(owner, slot, plane, kind):
        return pltpu.make_async_remote_copy(
            src_ref=edge.at[owner], dst_ref=edges.at[slot],
            send_sem=edge_send.at[kind, owner], recv_sem=edge_recv.at[slot],
            device_id=(plane * PLANE + owner, core), device_id_type=MESH,
        )

    @pl.loop(1, PLANE)
    def _(step):
        edge_copy(nth_of(PLANE - step), spot, zed, 0).start()

    @pl.when(crosses)
    def _():
        @pl.loop(0, PLANE)
        def _(owner):
            edge_copy(owner, PLANE, zed + 1, 1).start()

    edges[spot] = edge[spot]

    @pl.when(zed == 0)
    def _():
        edges[PLANE] = jnp.zeros_like(edges[PLANE])

    @pl.loop(groups // 2, groups)
    def _(g):
        end_states(g)

    def round_1(other):
        return pltpu.make_async_remote_copy(
            src_ref=e_out.at[other], dst_ref=e_buf.at[spot],
            send_sem=s1.at[other], recv_sem=r1.at[spot],
            device_id=(zed * PLANE + other, core), device_id_type=MESH,
        )

    def arrival_1(other):
        return pltpu.make_async_remote_copy(
            src_ref=e_out.at[other], dst_ref=e_buf.at[other],
            send_sem=s1.at[other], recv_sem=r1.at[other],
            device_id=(zed * PLANE + other, core), device_id_type=MESH,
        )

    for other in range(PLANE):
        e_out[other] = e_loc[other * part : (other + 1) * part, :].astype(jnp.bfloat16)

    @pl.loop(1, PLANE)
    def _(step):
        round_1(nth_of(PLANE - step)).start()

    def rim_copy(index, src, dst):
        return pltpu.make_async_remote_copy(
            src_ref=src.at[pl.ds(tok - SUB, SUB)], dst_ref=dst,
            send_sem=rim_send.at[index], recv_sem=rim_recv.at[index],
            device_id=(after, core), device_id_type=MESH,
        )

    rims = [rim_copy(0, k_hbm, rim_k), rim_copy(1, v_hbm, rim_v), rim_copy(2, q_hbm, rim_q)]
    @pl.when(me < shards - 1)
    def _():
        for copy in rims:
            copy.start()

    @pl.when(me == 0)
    def _():
        for rim in (rim_k, rim_v, rim_q):
            rim[...] = jnp.zeros_like(rim)

    e_buf[spot] = e_out[spot]

    begins = rows == 0
    for end in ends:
        begins = begins | (rows == end)
    keep_m[...] = jnp.where(begins, 0.0, 1.0)
    for t in range(tiles):
        taps_t[0, t * SUB : t * SUB + taps, :] = sf_in[0, :, t * LANES : (t + 1) * LANES]
    params[2].wait()
    params[3].wait()
    for t in range(tiles):
        x = -2.0 * rate_n[t * modes : (t + 1) * modes, :]
        series = 1.0 + x * (1.0 / 6.0)
        for n in (5.0, 4.0, 3.0, 2.0):
            series = 1.0 + x * (1.0 / n) * series
        coef_n[t * modes : (t + 1) * modes, :] = residue_in[:, t * LANES : (t + 1) * LANES] * jnp.sqrt(-x * series)

    @pl.loop(0, groups)
    def _(g):
        load(0, q_hbm, q_in, g).wait()
        relayout(q_in, xq, g)

    rising = (lax.broadcasted_iota(jnp.int32, (SUB, LANES), 0) + 1).astype(F32)

    @pl.loop(0, tiles)
    def _(t):
        for m in range(modes):
            rate = rate_n[pl.ds(t * modes + m, 1), :]
            coef = coef_n[pl.ds(t * modes + m, 1), :]
            here = pl.ds(pl.multiple_of((t * modes + m) * SUB, SUB), SUB)
            weights[here, :] = coef * jnp.exp(-rate * rising)
        whole = pl.ds(pl.multiple_of(t * modes, SUB), modes)
        dec8_n[whole, :] = jnp.exp(rate_n[whole, :] * float(-SUB))

    def tree(terms):
        while len(terms) > 1:
            terms = [a + b for a, b in zip(terms[::2], terms[1::2])]
        return terms[0]

    def conv_block(block, g, q_win, state, q_taps, decay, coef, z_of):
        q_win, state = list(q_win), list(state)
        for s in range(SUB):
            q_win.append(token(xq, block, g, s))
            qs = fir(q_win[-taps:], q_taps)
            t = (block - 1) * SUB + s
            z = z_of(t, s)
            keep = keep_m[pl.ds(t, 1), :]
            state = [(d * keep) * old + z for d, old in zip(decay, state)]
            out = tree([c * part for c, part in zip(coef, state)])
            there = pl.ds(row_of(block - 1, g * SUB) + s, SUB, stride=SUB)
            conv_std[there, :] = out * qs
            qs_std[there, :] = qs * carry_m[pl.ds(t, 1), :]
        return q_win[1 - taps :], state

    behind = range(SUB - taps + 1, SUB)

    def inner(g):
        q_taps = taps_of(0, g)
        decay = [per_mode(dec_n, g, m) for m in range(modes)]
        coef = [per_mode(coef_n, g, m) for m in range(modes)]

        def step(block, carried):
            return conv_block(block, g, *carried, q_taps, decay, coef, lambda t, s: zs[z_rows(t, g), :])

        lax.fori_loop(2, blocks + 1, step, ([token(xq, 1, g, s) for s in behind], [zero] * modes))

    def head(g):
        windows = [[token(x, 0, g, s) for s in behind] for x in (xk, xv)]
        weight = [taps_of(1, g), taps_of(2, g)]

        def z_of(t, s):
            for window, x in zip(windows, (xk, xv)):
                window.append(token(x, 1, g, s))
            return fir(windows[0][-taps:], weight[0]) * fir(windows[1][-taps:], weight[1])

        decay = [per_mode(dec_n, g, m) for m in range(modes)]
        coef = [per_mode(coef_n, g, m) for m in range(modes)]
        _, state = conv_block(
            1, g, [token(xq, 0, g, s) for s in behind], [zero] * modes, taps_of(0, g), decay, coef, z_of
        )
        for m in range(modes):
            head_n[pl.ds(g * SUB * modes + m, SUB, stride=modes), :] = state[m]

    inner(0)

    per = tiles // PLANE
    my_rate = at(rate_n, spot * part, part)[...]
    for i in range(SUB):
        source = pl.multiple_of((spot * per + i % per) * SUB, SUB)
        dec_own[i * SUB : (i + 1) * SUB, :] = dec_n[pl.ds(source, SUB), :]
        for a in (1, 2):
            taps_own[a - 1, i * SUB : (i + 1) * SUB, :] = taps_t[a, pl.ds(source, SUB), :]
    own_decay = [dec_own[pl.ds(m, SUB, stride=modes), :] for m in range(modes)]
    own_taps = [[taps_own[a, pl.ds(j, SUB, stride=SUB), :] for j in range(taps)] for a in range(2)]

    @pl.loop(1, PLANE)
    def _(step):
        source = lax.rem(spot + step, PLANE)
        edge_copy(source, source, zed, 0).wait_recv()

    @pl.when(zed > 0)
    def _():
        edge_copy(spot, PLANE, zed, 1).wait_recv()

    for j in range(PLANE):
        for a, dst in ((0, ek), (1, ev)):
            past = edges[(j + PLANE) % (PLANE + 1), a].astype(F32)
            here = edges[j, a + 2].astype(F32)
            for i in range(per):
                tile = j * per + i
                dst[row_of(0, tile) : row_of(0, tile) + SUB, :] = past[:, i * LANES : (i + 1) * LANES]
                dst[row_of(1, tile) : row_of(1, tile) + SUB, :] = here[:, i * LANES : (i + 1) * LANES]

    for g in range(groups):
        shard = zed * PLANE + (lax.broadcasted_iota(jnp.int32, (SUB, LANES), 0) + g * SUB) // per
        begin = shard * tok
        latest = jnp.full((SUB, LANES), -1, jnp.int32)
        for end in ends:
            latest = jnp.maximum(latest, jnp.where(end <= begin + (tok - 1), end, -1))
        window = [[token(x, 0, g, s) for s in range(SUB - taps + 1, SUB)] for x in (ek, ev)]
        state = [zero] * modes
        for s in range(SUB):
            window[0].append(token(ek, 1, g, s))
            window[1].append(token(ev, 1, g, s))
            z = fir(window[0][-taps:], own_taps[0]) * fir(window[1][-taps:], own_taps[1])
            z = jnp.where(begin + s >= latest, z, 0.0)
            state = [d * old + z for d, old in zip(own_decay, state)]
        for m in range(modes):
            e_first[pl.ds(g * SUB * modes + m, SUB, stride=modes), :] = state[m]

    @pl.loop(1, PLANE)
    def _(step):
        arrival_1(lax.rem(spot + step, PLANE)).wait_recv()

    span = jnp.exp(my_rate * float(-tok))
    spot_rows = lax.broadcasted_iota(jnp.int32, (PLANE, LANES), 0) + zed * PLANE
    plane_rows = lax.broadcasted_iota(jnp.int32, (SUB, LANES), 0)
    open_here = jnp.ones((PLANE, LANES), F32)
    open_plane = jnp.ones((SUB, LANES), F32)
    for end in ends:
        open_here = jnp.where(spot_rows == end // tok, 0.0, open_here)
        open_plane = jnp.where(plane_rows == end // (tok * PLANE), 0.0, open_plane)

    rest = jnp.exp(my_rate * float(SUB - tok))
    state = jnp.zeros_like(span)
    reach = jnp.ones_like(span)
    for other in range(PLANE):
        pre_buf[other] = state
        reach_buf[other] = reach
        factor = span * open_here[other : other + 1]
        state = factor * state + e_buf[other].astype(F32) + rest * e_first[other * part : (other + 1) * part, :]
        reach = factor * reach
    total_buf[...] = state

    def round_2(there, slot):
        return pltpu.make_async_remote_copy(
            src_ref=total_buf, dst_ref=plane_buf.at[slot],
            send_sem=s2.at[there], recv_sem=r2.at[slot],
            device_id=(there * PLANE + spot, core), device_id_type=MESH,
        )

    @pl.loop(zed + 1, planes)
    def _(there):
        round_2(there, zed).start()

    @pl.loop(1, groups - 1)
    def _(g):
        inner(g)

    plane_span = jnp.exp(my_rate * float(-tok * PLANE))

    def plane_step(there, state):
        round_2(there, there).wait_recv()
        row = jnp.sum(jnp.where(plane_rows == there, open_plane, 0.0), axis=0, keepdims=True)
        return plane_span * row * state + plane_buf[there]

    state = lax.fori_loop(0, zed, plane_step, jnp.zeros_like(span))
    def round_3(other, slot):
        return pltpu.make_async_remote_copy(
            src_ref=inc_out.at[other], dst_ref=inc_buf.at[slot],
            send_sem=s3.at[other], recv_sem=r3.at[slot],
            device_id=(zed * PLANE + other, core), device_id_type=MESH,
        )

    @pl.loop(1, PLANE)
    def _(step):
        other = nth_of(PLANE - step)
        inc_out[other] = (pre_buf[other] + reach_buf[other] * state).astype(jnp.bfloat16)
        round_3(other, spot).start()

    inc_buf[spot] = (pre_buf[spot] + reach_buf[spot] * state).astype(jnp.bfloat16)

    inner(groups - 1)

    for g in range(groups):
        load(3, r_hbm, r_in, g).wait()

    def add_residual(begin, end):
        @pl.loop(0, tiles)
        def _(t):
            cols = pl.ds(pl.multiple_of(t * LANES, LANES), LANES)
            for pair in range(begin, end):
                x = r_in[pair * 2 * SUB : (pair + 1) * 2 * SUB, cols].astype(F32)
                for half in range(2):
                    here = pl.ds(pl.multiple_of(row_of(2 * pair + half, t), SUB), SUB)
                    conv_std[here, :] = conv_std[here, :] + x[half * SUB : (half + 1) * SUB]

    add_residual(1, pairs)
    sq_loc[...] = jnp.zeros_like(sq_loc)

    @pl.when(me > 0)
    def _():
        for copy in rims:
            copy.wait_recv()

    relayout_rim(rim_k, xk)
    relayout_rim(rim_v, xv)
    relayout_rim(rim_q, xq)

    @pl.loop(0, groups)
    def _(g):
        head(g)

    add_residual(0, 1)


    def tile_of(slot, local):
        t = slot * per + local
        whole = pl.ds(pl.multiple_of(t * modes, SUB), modes)
        incoming = inc_buf[slot].astype(F32)[local * modes : (local + 1) * modes]
        at_8 = dec8_n[whole, :] * carry_m[SUB - 1 : SUB, :] * incoming + head_n[whole, :]
        value, later, decay = [], [], []
        for m in range(modes):
            here = pl.ds(pl.multiple_of((t * modes + m) * SUB, SUB), SUB)
            weight = weights[here, :]
            value.append(weight * incoming[m : m + 1])
            later.append(weight * at_8[m : m + 1])
            decay.append(jnp.broadcast_to(dec8_n[pl.ds(t * modes + m, 1), :], (SUB, LANES)))
        cols = pl.ds(pl.multiple_of(t * LANES, LANES), LANES)
        for pair in range(pairs):
            halves = []
            for block in (2 * pair, 2 * pair + 1):
                carried = tree(value)
                if block == 0:
                    value = later
                elif block < blocks - 1:
                    value = [v * d for v, d in zip(value, decay)]
                here = pl.ds(pl.multiple_of(row_of(block, t), SUB), SUB)
                halves.append(conv_std[here, :] + qs_std[here, :] * carried)
            both = pl.ds(pair * 2 * SUB, 2 * SUB)
            stream = jnp.concatenate(halves, axis=0).astype(jnp.bfloat16)
            stream_ref[both, cols] = stream
            back = stream.astype(F32)
            sq_loc[both, :] = sq_loc[both, :] + back * back

    @pl.loop(0, PLANE)
    def _(n):
        slot = nth_of(n)

        @pl.when(n > 0)
        def _():
            round_3(slot, slot).wait_recv()

        for local in range(per):
            tile_of(slot, local)

    swap = pltpu.make_async_remote_copy(
        src_ref=sq_loc, dst_ref=sq_far, send_sem=sq_send, recv_sem=sq_recv,
        device_id=(me, 1 - core), device_id_type=MESH,
    )
    swap.start()

    @pl.when(me < shards - 1)
    def _():
        for copy in rims:
            copy.wait_send()

    @pl.loop(1, PLANE)
    def _(step):
        other = lax.rem(spot + step, PLANE)
        round_1(other).wait_send()
        round_3(other, spot).wait_send()
        edge_copy(other, spot, zed, 0).wait_send()

    @pl.when(crosses)
    def _():
        @pl.loop(0, PLANE)
        def _(owner):
            edge_copy(owner, PLANE, zed + 1, 1).wait_send()

    @pl.loop(zed + 1, planes)
    def _(there):
        round_2(there, zed).wait_send()

    swap.wait()
    total = jnp.sum(sq_loc[...] + sq_far[...], axis=1, keepdims=True)
    scale = lax.rsqrt(total * (1.0 / (2 * chans)) + 1e-6)
    scale_ref[...] = jnp.broadcast_to(scale, (tok, LANES))


def finish(tok, chans, stream_ref, scale_ref, gain_ref, stream_hbm, normed_hbm, normed, sem):
    each = SUB // 2
    wide = each * LANES
    groups = chans // wide
    copies = [pltpu.make_async_copy(stream_ref, stream_hbm, sem.at[groups])]
    copies[0].start()
    scales = [scale_ref[pair * 2 * SUB : (pair + 1) * 2 * SUB, :] for pair in range(tok // (2 * SUB))]
    for g in range(groups):
        @pl.loop(g * each, (g + 1) * each)
        def _(t):
            cols = pl.ds(pl.multiple_of(t * LANES, LANES), LANES)
            gain = gain_ref[pl.ds(t, 1), :]
            for pair, scale in enumerate(scales):
                both = slice(pair * 2 * SUB, (pair + 1) * 2 * SUB)
                x = stream_ref[both, cols].astype(F32)
                normed[both, cols] = (x * scale * gain).astype(jnp.bfloat16)

        part = slice(g * wide, (g + 1) * wide)
        copy = pltpu.make_async_copy(normed.at[:, part], normed_hbm.at[:, part], sem.at[g])
        copy.start()
        copies.append(copy)
    for copy in copies:
        copy.wait()


def body(q_proj, k_proj, v_proj, resid, short_filter, residue, rate, gain, seg_lengths):
    tok, chans = q_proj.shape
    taps = short_filter.shape[1]
    modes = rate.shape[0]
    segs = seg_lengths.shape[0]
    shards = lax.axis_size("seq")
    planes = shards // PLANE
    tiles = chans // LANES
    groups = tiles // SUB
    blocks = tok // SUB
    part = tiles * modes // PLANE
    bf16 = jnp.bfloat16
    dims = (shards, planes, tok, chans, modes, taps, segs)
    vmem = pltpu.VMEM
    sem = pltpu.SemaphoreType.DMA
    hbm_spec = pl.BlockSpec(memory_space=pltpu.HBM)
    stream, scale, gain = pl.pallas_call(
        functools.partial(kernel, dims),
        out_shape=(
            jax.ShapeDtypeStruct((tok, chans), bf16),
            jax.ShapeDtypeStruct((tok, LANES), F32),
            jax.ShapeDtypeStruct((tiles, LANES), F32),
        ),
        in_specs=[hbm_spec] * 9,
        out_specs=(pl.BlockSpec(memory_space=vmem),) * 3,
        scratch_shapes=[
            vmem((tok, chans), bf16), vmem((tok, chans), bf16), vmem((tok, chans), bf16), vmem((tok, chans), bf16),
            vmem((3, taps, chans), F32), vmem((modes, chans), F32), vmem((modes, chans), F32),
            pltpu.SMEM((segs,), jnp.int32),
            vmem((SUB, chans), bf16), vmem((SUB, chans), bf16), vmem((SUB, chans), bf16),
            vmem((PLANE, 4, SUB, chans // PLANE), bf16), vmem((PLANE + 1, 4, SUB, chans // PLANE), bf16),
            vmem((2 * tiles * SUB, LANES), F32), vmem((2 * tiles * SUB, LANES), F32),
            vmem((tiles * modes, LANES), F32), vmem((tiles * modes, LANES), F32),
            vmem((SUB * modes, LANES), F32), vmem((2, SUB * SUB, LANES), F32),
            vmem(((blocks + 1) * tiles * SUB, LANES), F32),
            vmem(((blocks + 1) * tiles * SUB, LANES), F32),
            vmem(((blocks + 1) * tiles * SUB, LANES), F32),
            vmem((blocks * tiles * SUB, LANES), F32),
            vmem((blocks * tiles * SUB, LANES), F32),
            vmem((blocks * tiles * SUB, LANES), F32),
            vmem((3, tiles * SUB, LANES), F32),
            vmem((tiles * modes, LANES), F32), vmem((tiles * modes, LANES), F32), vmem((tiles * modes, LANES), F32),
            vmem((tiles * modes * SUB, LANES), F32), vmem((tiles * modes, LANES), F32),
            vmem((tok, LANES), F32), vmem((tok, LANES), F32), vmem((tok, LANES), F32),
            vmem((tiles * modes, LANES), F32),
            vmem((PLANE, part, LANES), bf16), vmem((PLANE, part, LANES), bf16),
            vmem((PLANE, part, LANES), F32), vmem((PLANE, part, LANES), F32),
            vmem((part, LANES), F32), vmem((planes, part, LANES), F32),
            vmem((PLANE, part, LANES), bf16), vmem((PLANE, part, LANES), bf16),
            vmem((tok, LANES), F32), vmem((tok, LANES), F32),
            sem((4, groups)), sem((5,)), sem((3,)), sem((3,)), sem((2, PLANE)), sem((PLANE + 1,)),
            sem((PLANE,)), sem((PLANE,)), sem((planes,)), sem((planes,)), sem((PLANE,)), sem((PLANE,)),
            sem, sem,
        ],
        compiler_params=pltpu.CompilerParams(
            collective_id=0, has_side_effects=True, vmem_limit_bytes=40 * 1024 * 1024
        ),
        name="hyena",
    )(*(pltpu.with_memory_space_constraint(x, pltpu.HBM) for x in (
        q_proj, k_proj, v_proj, resid, short_filter, residue, rate, gain.reshape(tiles, LANES), seg_lengths
    )))
    return pl.pallas_call(
        functools.partial(finish, tok, chans),
        out_shape=(jax.ShapeDtypeStruct((tok, chans), bf16),) * 2,
        in_specs=[pl.BlockSpec(memory_space=vmem)] * 3,
        out_specs=(hbm_spec,) * 2,
        scratch_shapes=[vmem((tok, chans), bf16), sem((2 * chans // (SUB * LANES) + 1,))],
        compiler_params=pltpu.CompilerParams(vmem_limit_bytes=16 * 1024 * 1024),
        name="finish",
    )(stream, scale, gain)


def solution(mesh):
    placed = (
        P("seq", "chan"),
        P("seq", "chan"),
        P("seq", "chan"),
        P("seq", "chan"),
        P(None, None, "chan"),
        P(None, "chan"),
        P(None, "chan"),
        P("chan"),
        P(),
    )
    return jax.shard_map(
        body,
        mesh=mesh,
        in_specs=placed,
        out_specs=(P("seq", "chan"), P("seq", "chan")),
        check_vma=False,
    )
```
